256 devices in a mesh: gx: 8 (over z_lo, x), gy: 4 (over z_hi), gz: 8 (over y, core).
Axes of the slice: x: 4, y: 4, z: 8 (z_hi: 4, z_lo: 2; z = z_hi * 2 + z_lo), core: 2. Of those that a mesh axis runs over, the one named last changes fastest.
Arguments:
- fields: bfloat16 [7, 64, 32, 128], P(None, 'gx', 'gy', 'gz'), may hold values from -6 to 6
- grain_ids: int32 [64, 32, 128], P('gx', 'gy', 'gz'), may hold values from 0 to 127
- material_table: bfloat16 [128, 64], replicated, may hold values from -6 to 6
- input_weight: bfloat16 [64, 7], replicated, may hold values from -2 to 2
- kernel_fine: bfloat16 [64, 1728], replicated, may hold values from -0.15625 to 0.15625
- kernel_down: bfloat16 [128, 1728], replicated, may hold values from -0.15625 to 0.15625
- kernel_bottle: bfloat16 [256, 3456], P('gx'), may hold values from -0.109375 to 0.109375
- cotangent: bfloat16 [256, 32, 16, 64], P('gx', None, 'gy', 'gz'), may hold values from -6 to 6
Outputs:
- bottle: bfloat16 [256, 32, 16, 64], P('gx', None, 'gy', 'gz')
- grad_down: float32 [128, 1728], P('gx', ('gy', 'gz'))
- grad_bottle: float32 [256, 3456], P('gx', ('gy', 'gz'))
The draws below stay inside these ranges and needn't reach their ends.
Inputs may be any that keep to these rules, and one draw needn't show every extreme that they name: `grain_ids`: each voxel's grain, a row of material_table.
All inputs are finite; a program needn't handle non-finite values.
Results may differ from the reference program's by a relative error of at most 0.028.
Values may be sent and summed in bfloat16 or wider, within the bound.
A program may use at most 64 MiB of HBM per device.

```python
import math
import jax
import jax.numpy as jnp
from jax import lax

C1 = 64
C2 = 128
C3 = 256
CF = 7
GRAINS = 128
TAPS = 27
NX = 64
NY = 32
NZ = 128
X1 = 32
Y1 = 16
Z1 = 64


def plant(drawn, rng, least, largest):
    longest = drawn.shape.index(max(drawn.shape))
    spots = []
    for shift in (0, 1):
        where = [jax.random.randint(jax.random.fold_in(rng, axis), (), 0, length) for axis, length in enumerate(drawn.shape)]
        where[longest] = (where[longest] + shift) % drawn.shape[longest]
        spots.append(tuple(where))
    return drawn.at[spots[0]].set(least).at[spots[1]].set(largest)


def block_levels(rng, extent, cuts, least, largest):
    level = 1.0
    for position, shards_of in cuts:
        draws = jax.random.uniform(jax.random.fold_in(jax.random.fold_in(rng, 6), position), (shards_of,), jnp.float32, least / len(cuts), largest / len(cuts))
        level = level * jnp.repeat(jnp.exp(draws), extent[position] // shards_of).reshape((-1,) + (1,) * (len(extent) - 1 - position))
    return level


def scatter_about(stream_key, dims, deviation, limit, split=(), held_as=jnp.bfloat16):
    drawn = deviation * jax.random.normal(stream_key, dims, jnp.float32)
    if split:
        drawn = drawn * block_levels(stream_key, dims, split, -0.22, 0.18)
    return jnp.clip(drawn, -limit, limit).astype(held_as)


def setup_inputs(seed: int = 0) -> dict:
    streams_of = jax.random.split(jax.random.key(seed), 9)
    return {
        "fields": scatter_about(streams_of[0], (CF, NX, NY, NZ), 1.0, 6.0, ((1, 8), (2, 4), (3, 8))),
        "grain_ids": plant(jax.random.randint(streams_of[1], (NX, NY, NZ), 0, GRAINS), jax.random.fold_in(streams_of[1], 1), 0, GRAINS - 1).astype(jnp.int32),
        "material_table": scatter_about(streams_of[2], (GRAINS, C1), 1.0, 6.0),
        "input_weight": scatter_about(streams_of[3], (C1, CF), CF ** -0.5, 2.0),
        "kernel_fine": scatter_about(streams_of[4], (C1, TAPS * C1), (TAPS * C1) ** -0.5, 0.15625),
        "kernel_down": scatter_about(streams_of[5], (C2, TAPS * C1), (TAPS * C1) ** -0.5, 0.15625),
        "kernel_bottle": scatter_about(streams_of[6], (C3, TAPS * C2), (TAPS * C2) ** -0.5, 0.109375, ((0, 8),)),
        "cotangent": scatter_about(streams_of[7], (C3, X1, Y1, Z1), 1.0, 6.0, ((0, 8), (2, 4), (3, 8))),
    }


def convolve(volume, kernel, stride):
    out_chans = kernel.shape[0]
    in_chans = kernel.shape[1] // 27
    weights = kernel.astype(jnp.float32).reshape(out_chans, 3, 3, 3, in_chans).transpose(0, 4, 1, 2, 3)
    result = lax.conv_general_dilated(volume.astype(jnp.float32)[None], weights, (stride, stride, stride), [(1, 1), (1, 1), (1, 1)], dimension_numbers=('NCDHW', 'OIDHW', 'NCDHW'), precision=lax.Precision.HIGHEST)
    return result[0]

def silu_grad(values):
    sigmoid = jax.nn.sigmoid(values)
    return sigmoid * (1.0 + values * (1.0 - sigmoid))

def reference(fields, grain_ids, material_table, input_weight, kernel_fine, kernel_down, kernel_bottle, cotangent):
    material = jnp.moveaxis(jnp.take(material_table, grain_ids, axis=0), 3, 0)
    mixture = jnp.dot(input_weight, fields.reshape(CF, -1), preferred_element_type=jnp.float32).reshape(material.shape) + material.astype(jnp.float32)
    embedded = jax.nn.silu(mixture).astype(jnp.bfloat16)
    fine = jax.nn.silu(convolve(embedded, kernel_fine, 1)).astype(jnp.bfloat16)
    pre_down = convolve(fine, kernel_down, 2)
    coarse = jax.nn.silu(pre_down).astype(jnp.bfloat16)

    def bottle_conv(volume, kernel):
        return convolve(volume, kernel, 1)
    pre_bottle, bottle_pull = jax.vjp(bottle_conv, coarse.astype(jnp.float32), kernel_bottle.astype(jnp.float32))
    bottle = jax.nn.silu(pre_bottle).astype(jnp.bfloat16)
    grad_pre_bottle = (cotangent.astype(jnp.float32) * silu_grad(pre_bottle)).astype(jnp.bfloat16)
    grad_down_act, grad_bottle = bottle_pull(grad_pre_bottle.astype(jnp.float32))
    grad_pre_down = (grad_down_act * silu_grad(pre_down)).astype(jnp.bfloat16)

    def down_conv(kernel):
        return convolve(fine, kernel, 2)
    ignored, down_pull = jax.vjp(down_conv, kernel_down.astype(jnp.float32))
    grad_down = down_pull(grad_pre_down.astype(jnp.float32))[0]
    grad_scale = 1.0 / math.sqrt(X1 * Y1 * Z1)
    return (bottle, grad_down * grad_scale, grad_bottle * grad_scale)
```

```python
import functools
import math

import jax
import jax.numpy as jnp
from jax import lax
from jax.experimental import pallas as pl
from jax.experimental.pallas import tpu as pltpu
from jax.sharding import PartitionSpec as P

MESH = pl.DeviceIdType.MESH
F32 = jnp.float32
BF16 = jnp.bfloat16
NT = (((1,), (1,)), ((), ()))


def silu(v):
    return v * jax.nn.sigmoid(v)


def silu_grad(v):
    s = jax.nn.sigmoid(v)
    return s * (1.0 + v * (1.0 - s))


def dot(a, b):
    return jnp.dot(a, b, preferred_element_type=F32)


def dot_nt(a, b):
    return lax.dot_general(a, b, NT, preferred_element_type=F32)


def tap_of(t):
    t = min(t, 26)
    return t // 9, (t // 3) % 3, t % 3


def lane_iota(shape):
    return lax.broadcasted_iota(jnp.int32, shape, len(shape) - 1)


def piece(ref_tiles, start, width):
    tile, shift = start // 128, start % 128
    low = ref_tiles(tile)
    if shift == 0:
        return low
    low = pltpu.roll(low, 128 - shift, 1)
    if shift + width <= 128:
        return low
    high = pltpu.roll(ref_tiles(tile + 1), 128 - shift, 1)
    return jnp.where(lane_iota(low.shape) < 128 - shift, low, high)


def body(
    sizes,
    fields,
    ids,
    table,
    w_in,
    k_fine,
    k_down,
    k_bot,
    cot,
    bottle_o,
    gdown_o,
    gbot_o,
    raw,
    brick,
    ext,
    es,
    af,
    fs,
    fmask,
    kf,
    kd,
    kb4,
    wblk,
    ac,
    ad,
    pd,
    cb,
    cs,
    sb,
    slab,
    a3,
    pre,
    gp,
    gt,
    ysend,
    zsend,
    csend,
    yrecv,
    zrecv,
    crecv,
    gpad,
    ag,
    acts,
    actr,
    downs,
    downr,
    dsum,
    gball,
    gbs,
    gbr,
    gds,
    gdr,
    sem_l,
    s1,
    r1,
    s2,
    r2,
    s3,
    r3,
    s4,
    r4,
    s5,
    r5,
    s6,
    r6,
    s7,
    r7,
):
    nx, ny, nz = sizes
    gx, gy, gz = lax.axis_index("gx"), lax.axis_index("gy"), lax.axis_index("gz")
    scale = 1.0 / math.sqrt(nx * 4 * ny * 4 * nz * 8)

    def device(dx, dy, dz):
        return (lax.rem(gx + dx + nx, nx), lax.rem(gy + dy + ny, ny), lax.rem(gz + dz + nz, nz))

    near = [(dx, dy, dz) for dx in (-1, 0, 1) for dy in (-1, 0, 1) for dz in (-1, 0, 1)]
    near = [n for n in near if n != (0, 0, 0)]
    columns = [(dx, 0, 0) for dx in range(1, nx)]
    planes = [(0, dy, dz) for dy in range(ny) for dz in range(nz) if (dy, dz) != (0, 0)]
    partners = sorted({(a % nx, b % ny, c % nz) for a, b, c in near + columns + planes})
    barrier = pltpu.get_barrier_semaphore()
    for p in partners:
        pl.semaphore_signal(barrier, inc=1, device_id=device(*p), device_id_type=MESH)

    sel_row = lax.broadcasted_iota(jnp.int32, (16, 128), 0)
    sel_lane = lax.broadcasted_iota(jnp.int32, (16, 128), 1)
    packed = jnp.zeros((64, 128), F32)
    for ch in range(8):
        plane = (fields[ch] if ch < 7 else ids[...]).astype(F32).reshape(64, 16).astype(BF16)
        select = jnp.where(sel_lane == sel_row * 8 + ch, 1.0, 0.0).astype(BF16)
        packed = packed + dot(plane, select)
    raw[...] = packed
    group = lane_iota((16, 128)) // 32
    for zb in range(4):
        block = None
        for y4 in range(4):
            rows = raw[pl.ds(y4, 16, stride=4), :]
            shift = ((y4 - zb) * 32) % 128
            rows = rows if shift == 0 else pltpu.roll(rows, shift, 1)
            block = rows if block is None else jnp.where(group == y4, rows, block)
        for r in range(16):
            brick[r // 2, r % 2, zb, :, :] = block[r : r + 1, :]
    ext[:, :, 6:8] = jnp.zeros((11, 4, 2, 1, 128), F32)

    kf[...] = jnp.zeros(kf.shape, BF16)
    kf[0:64, 0:1728] = k_fine[...]
    kf[64:128, 0:1728] = k_fine[...]
    kd[...] = jnp.zeros(kd.shape, BF16)
    kd[:, 0:1728] = k_down[...]
    for q in range(4):
        kb4[32 * q : 32 * q + 32, :] = k_bot[...]
    wblk[...] = jnp.zeros(wblk.shape, BF16)
    for t in range(27):
        for q in range(4):
            wblk[t * 128 + q * 32 : t * 128 + q * 32 + 32, q * 128 : q * 128 + 128] = k_bot[
                :, t * 128 : t * 128 + 128
            ]
    my = gy * 8 - 3 + lax.broadcasted_iota(jnp.int32, (13, 24, 128), 0)
    mz = gz * 16 - 3 + lax.broadcasted_iota(jnp.int32, (13, 24, 128), 1)
    inside = (my >= 0) & (my < ny * 8) & (mz >= 0) & (mz < nz * 16)
    fmask[...] = jnp.where(inside, 1.0, 0.0)
    fs[...] = jnp.zeros(fs.shape, F32)
    gpad[...] = jnp.zeros(gpad.shape, F32)
    slab[0] = jnp.zeros((64, 128), F32)
    slab[4 * nx + 1] = jnp.zeros((64, 128), F32)
    cb[...] = jnp.zeros(cb.shape, F32)

    pl.semaphore_wait(barrier, len(partners))

    x_src = {1: (6, 2, 0), 0: (0, 8, 2), -1: (0, 1, 10)}
    y_src = {1: (1, 1, 0), 0: (0, 2, 1), -1: (0, 1, 3)}
    z_src = {1: (3, 1, 0), 0: (0, 4, 1), -1: (0, 1, 5)}
    halo = []
    for number, (dx, dy, dz) in enumerate(near):
        (xs, xn, xd), (ys, yn, yd), (zs, zn, zd) = x_src[dx], y_src[dy], z_src[dz]
        halo.append(
            pltpu.make_async_remote_copy(
                src_ref=brick.at[xs : xs + xn, ys : ys + yn, zs : zs + zn],
                dst_ref=ext.at[xd : xd + xn, yd : yd + yn, zd : zd + zn],
                send_sem=s1.at[number],
                recv_sem=r1.at[number],
                device_id=device(dx, dy, dz),
                device_id_type=MESH,
            )
        )
    for c in halo:
        c.start()
    own = pltpu.make_async_copy(brick, ext.at[2:10, 1:3, 1:5], sem_l.at[0])
    own.start()

    row8 = lax.broadcasted_iota(jnp.int32, (128, 7), 0) % 8
    pick = jnp.where(row8 == lax.broadcasted_iota(jnp.int32, (128, 7), 1), 1.0, 0.0).astype(BF16)
    w_twice = jnp.concatenate([w_in[...].astype(F32)] * 2, axis=0).astype(BF16)
    w_rows = dot_nt(pick, w_twice)
    id_rows = jnp.where(lax.broadcasted_iota(jnp.int32, (128, 128), 0) % 8 == 7, 1.0, 0.0)
    w_emb = jnp.concatenate([id_rows, w_rows], axis=1)
    emb_row = lax.broadcasted_iota(jnp.int32, (128, 256), 0) // 8
    twice = jnp.where(
        lax.broadcasted_iota(jnp.int32, (64, 128), 1) % 64
        == lax.broadcasted_iota(jnp.int32, (64, 128), 0),
        1.0,
        0.0,
    ).astype(BF16)
    table2 = dot(table[...], twice).astype(BF16)

    own.wait()
    for c in halo:
        c.wait()

    blocks = ext[...].reshape(44, 8, 128)
    bx = lax.broadcasted_iota(jnp.int32, (44, 8, 128), 0)
    by = bx % 4
    bx = bx // 4
    bz = lax.broadcasted_iota(jnp.int32, (44, 8, 128), 1)
    outside = ((bx < 2) & (gx == 0)) | ((bx == 10) & (gx == nx - 1))
    outside = outside | ((by == 0) & (gy == 0)) | ((by == 3) & (gy == ny - 1))
    outside = outside | ((bz == 0) & (gz == 0)) | ((bz == 5) & (gz == nz - 1))
    fill = jnp.where(lane_iota((44, 8, 128)) % 8 == 7, -1.0, 0.0)
    blocks = jnp.where(outside, fill, blocks).reshape(352, 128).astype(BF16)
    lanes = lane_iota((352, 128)).astype(F32)
    for p in range(16):
        y4, z4 = p // 4, p % 4
        w_p = jnp.where(emb_row == p, w_emb, 0.0).astype(BF16)
        both = dot(blocks, w_p)
        onehot = jnp.where(both[:, 0:128] == lanes, 1.0, 0.0).astype(BF16)
        value = silu(both[:, 128:256] + dot(onehot, table2)).reshape(11, 4, 8, 128)
        for x in range(11):
            for yb in range(4):
                es[x, yb * 4 + y4, pl.ds(z4, 8, stride=4), :] = value[x, yb]

    half = lane_iota((13, 24, 128)) < 64

    def fine_plane(x, carry):
        for t in range(14):
            (ax, ay, az), (bx_, by_, bz_) = tap_of(2 * t), tap_of(2 * t + 1)
            low = es[x + ax, ay : ay + 13, az : az + 24, :]
            high = es[x + bx_, by_ : by_ + 13, bz_ : bz_ + 24, :]
            block = jnp.where(half, low, high)
            af[:, t * 128 : t * 128 + 128] = block.reshape(312, 128).astype(BF16)
        value = silu(dot_nt(af[...], kf[...])).reshape(13, 24, 128)
        keep = jnp.where((x > 0) | (gx > 0), 1.0, 0.0)
        value = value * fmask[...] * keep
        fs[x, :, 0:24, :] = value.astype(BF16).astype(F32)
        return carry

    lax.fori_loop(0, 9, fine_plane, 0)

    half16 = lane_iota((16, 128)) < 64
    for x in range(4):
        for y in range(6):
            row = (x * 6 + y) * 16
            for t in range(14):
                (ax, ay, az), (bx_, by_, bz_) = tap_of(2 * t), tap_of(2 * t + 1)
                low = fs[2 * x + ax, 2 * y + ay, pl.ds(az, 16, stride=2), :]
                high = fs[2 * x + bx_, 2 * y + by_, pl.ds(bz_, 16, stride=2), :]
                ac[row : row + 16, t * 128 : t * 128 + 128] = jnp.where(half16, low, high).astype(BF16)
    pd[...] = dot_nt(ac[...], kd[...]).reshape(4, 6, 16, 128)
    coarse = silu(pd[...])
    cy = gy * 4 - 1 + lax.broadcasted_iota(jnp.int32, (4, 6, 16, 128), 1)
    cz = gz * 8 - 1 + lax.broadcasted_iota(jnp.int32, (4, 6, 16, 128), 2)
    inside = (cy >= 0) & (cy < ny * 4) & (cz >= 0) & (cz < nz * 8)
    coarse = jnp.where(inside, coarse, 0.0)
    for x in range(4):
        for y in range(6):
            cb[x, y * 10 : y * 10 + 10, :] = coarse[x, y, 0:10, :]
    cs[...] = cb[...].astype(BF16)

    gather = []
    for k in range(1, nx):
        gather.append(
            pltpu.make_async_remote_copy(
                src_ref=cs,
                dst_ref=sb.at[gx],
                send_sem=s2.at[k],
                recv_sem=r2.at[k],
                device_id=device(k, 0, 0),
                device_id_type=MESH,
            )
        )
    for c in gather:
        c.start()

    half8 = lane_iota((8, 128)) < 64
    for y in range(4):
        for t in range(14):
            (ax, ay, az), (bx_, by_, bz_) = tap_of(2 * t), tap_of(2 * t + 1)
            parts = []
            for x in range(4):
                low = fs[2 * x + ax, 2 * y + 2 + ay, pl.ds(2 + az, 8, stride=2), :]
                high = fs[2 * x + bx_, 2 * y + 2 + by_, pl.ds(2 + bz_, 8, stride=2), :]
                parts.append(jnp.where(half8, low, high))
            ad[y * 32 : y * 32 + 32, t * 128 : t * 128 + 128] = jnp.concatenate(parts, axis=0).astype(BF16)

    slab[pl.ds(1 + gx * 4, 4)] = cs[...].astype(F32)
    for k, c in enumerate(gather, 1):
        c.wait()
        source = lax.rem(gx - k + nx, nx)
        slab[pl.ds(1 + source * 4, 4)] = sb[source].astype(F32)

    for y in range(4):
        for t in range(27):
            ax, ay, az = tap_of(t)
            start = (y + ay) * 10 + az
            window = slab[ax : ax + 32, start : start + 8, :].reshape(4, 64, 128).astype(BF16)
            a3[:, y * 64 : y * 64 + 64, t * 128 : t * 128 + 128] = window

    def bottle_group(q, carry):
        pre[q] = dot_nt(a3[q], kb4[...])
        return carry

    lax.fori_loop(0, 4, bottle_group, 0)
    group = lane_iota((256, 128)) // 32
    z = pre[0]
    for q in range(1, 4):
        z = jnp.where(group == q, pre[q], z)
    bottle_o[...] = silu(z).reshape(4, 64, 128).astype(BF16)
    grad = cot[...].astype(F32).reshape(256, 128) * silu_grad(z)
    grad = grad.astype(BF16).astype(F32)
    gp[...] = grad.reshape(4, 64, 128)

    for side in range(2):
        ysend[side] = gp[3 - 3 * side].astype(BF16)
        zsend[side] = jnp.concatenate(
            [gp[y, pl.ds(7 - 7 * side, 8, stride=8), :] for y in range(4)], axis=0
        ).astype(BF16)
        for other in range(2):
            corner = gp[3 - 3 * side, pl.ds(7 - 7 * other, 8, stride=8), :]
            csend[side * 2 + other] = jnp.concatenate([corner, corner], axis=0).astype(BF16)
    rim = []

    def rim_copy(src, dst, number, dy, dz):
        c = pltpu.make_async_remote_copy(
            src_ref=src,
            dst_ref=dst,
            send_sem=s3.at[number],
            recv_sem=r3.at[number],
            device_id=device(0, dy, dz),
            device_id_type=MESH,
        )
        c.start()
        rim.append(c)

    for side in range(2):
        rim_copy(ysend.at[side], yrecv.at[side], side, 1 - 2 * side, 0)
    for side in range(2):
        rim_copy(zsend.at[side], zrecv.at[side], 2 + side, 0, 1 - 2 * side)
    for corner in range(4):
        rim_copy(
            csend.at[corner],
            crecv.at[corner],
            4 + corner,
            1 - 2 * (corner // 2),
            1 - 2 * (corner % 2),
        )

    gt[...] = jnp.transpose(grad).astype(BF16)
    for n in range(9):
        total = None
        for q in range(4):
            part = dot(gt[32 * q : 32 * q + 32, :], a3[q, :, n * 384 : n * 384 + 384])
            total = part if total is None else total + part
        gball[:, n * 384 : n * 384 + 384] = total * scale
    for k in range(ny * nz):
        cut = piece(lambda tile: gball[:, tile * 128 : tile * 128 + 128], 108 * k, 108)
        gbs[k] = cut.astype(BF16)
    me = gy * nz + gz
    gb_copies = []
    for k, (_, dy, dz) in enumerate(planes):
        ty, tz = lax.rem(gy + dy, ny), lax.rem(gz + dz, nz)
        gb_copies.append(
            pltpu.make_async_remote_copy(
                src_ref=gbs.at[ty * nz + tz],
                dst_ref=gbr.at[me],
                send_sem=s6.at[k],
                recv_sem=r6.at[k],
                device_id=(gx, ty, tz),
                device_id_type=MESH,
            )
        )

    gpad[1:5, 1:9, 1:9, :] = gp[...].reshape(4, 8, 8, 128)
    for c in rim:
        c.wait()
    for c in gb_copies:
        c.start()

    def kept(flag, value):
        return jnp.where(flag, value.astype(F32), 0.0)

    y_ok = (gy > 0, gy < ny - 1)
    z_ok = (gz > 0, gz < nz - 1)
    for side in range(2):
        gpad[5 * side, 1:9, 1:9, :] = kept(y_ok[side], yrecv[side]).reshape(8, 8, 128)
        value = kept(z_ok[side], zrecv[side])
        for y in range(4):
            gpad[1 + y, 1:9, 9 * side : 9 * side + 1, :] = value[8 * y : 8 * y + 8].reshape(8, 1, 128)
        for other in range(2):
            value = kept(y_ok[side] & z_ok[other], crecv[side * 2 + other])
            gpad[5 * side, 1:9, 9 * other : 9 * other + 1, :] = value[0:8].reshape(8, 1, 128)
    edge = lane_iota((96, 128))
    low = pltpu.roll(gpad[:, 8, :, :].reshape(96, 128), 32, 1)
    gpad[:, 0, :, :] = jnp.where(edge < 32, 0.0, low).reshape(6, 16, 128)
    high = pltpu.roll(gpad[:, 1, :, :].reshape(96, 128), 96, 1)
    gpad[:, 9, :, :] = jnp.where(edge >= 96, 0.0, high).reshape(6, 16, 128)

    for t in range(27):
        ax, ay, az = tap_of(t)
        window = gpad[2 - ay : 6 - ay, 2 - ax : 10 - ax, 2 - az : 10 - az, :]
        ag[:, t * 128 : t * 128 + 128] = window.reshape(256, 128).astype(BF16)
    for q in range(4):
        act = dot(ag[...], wblk[:, q * 128 : q * 128 + 128]).reshape(4, 64, 128).astype(BF16)
        for part in range(2):
            acts[2 * q + part] = act[:, part * 32 : part * 32 + 32, :]
    act_copies = []
    for k in range(1, nx):
        target = lax.rem(gx + k, nx)
        act_copies.append(
            pltpu.make_async_remote_copy(
                src_ref=acts.at[target],
                dst_ref=actr.at[gx],
                send_sem=s4.at[k],
                recv_sem=r4.at[k],
                device_id=(target, gy, gz),
                device_id_type=MESH,
            )
        )
    for c in act_copies:
        c.start()
    slope = []
    for y in range(4):
        for x in range(4):
            slope.append(silu_grad(pd[x, y + 1, 1:9, :]))
    slope = jnp.concatenate(slope, axis=0)
    total = acts[gx].astype(F32)
    for k, c in enumerate(act_copies, 1):
        c.wait()
        total = total + actr[lax.rem(gx - k + nx, nx)].astype(F32)
    grad_down = (total.reshape(128, 128) * slope).astype(BF16).astype(F32)
    grad_down_t = jnp.transpose(grad_down).astype(BF16)

    part = dot(grad_down_t, ad[...]) * scale
    downs[...] = part.reshape(nx, 16, 1792).astype(BF16)
    down_copies = []
    for k in range(1, nx):
        target = lax.rem(gx + k, nx)
        down_copies.append(
            pltpu.make_async_remote_copy(
                src_ref=downs.at[target],
                dst_ref=downr.at[gx],
                send_sem=s5.at[k],
                recv_sem=r5.at[k],
                device_id=(target, gy, gz),
                device_id_type=MESH,
            )
        )
    for c in down_copies:
        c.start()

    total = gbs[me].astype(F32)
    for k, c in enumerate(gb_copies):
        c.wait()
    for k, (_, dy, dz) in enumerate(planes):
        source = lax.rem(gy - dy + ny, ny) * nz + lax.rem(gz - dz + nz, nz)
        total = total + gbr[source].astype(F32)
    gbot_o[...] = total[:, 0:108]

    dsum[...] = downs[gx].astype(F32)
    for k, c in enumerate(down_copies, 1):
        c.wait()
        dsum[...] += downr[lax.rem(gx - k + nx, nx)].astype(F32)
    for k in range(ny * nz):
        cut = piece(lambda tile: dsum[:, tile * 128 : tile * 128 + 128], 54 * k, 54)
        gds[k] = cut.astype(BF16)
    gd_copies = []
    for k, (_, dy, dz) in enumerate(planes):
        ty, tz = lax.rem(gy + dy, ny), lax.rem(gz + dz, nz)
        c = pltpu.make_async_remote_copy(
            src_ref=gds.at[ty * nz + tz],
            dst_ref=gdr.at[me],
            send_sem=s7.at[k],
            recv_sem=r7.at[k],
            device_id=(gx, ty, tz),
            device_id_type=MESH,
        )
        c.start()
        gd_copies.append(c)
    total = gds[me].astype(F32)
    for c in gd_copies:
        c.wait()
    for k, (_, dy, dz) in enumerate(planes):
        source = lax.rem(gy - dy + ny, ny) * nz + lax.rem(gz - dz + nz, nz)
        total = total + gdr[source].astype(F32)
    gdown_o[...] = total[:, 0:54]


def per_device(sizes, fields, grain_ids, table, w_in, k_fine, k_down, k_bot, cotangent):
    nx, ny, nz = sizes
    n = ny * nz
    cot = cotangent.reshape(32, 4, 8, 4, 8).transpose(3, 2, 4, 1, 0).reshape(4, 64, 128)
    vmem = pl.BlockSpec(memory_space=pltpu.VMEM)
    V = pltpu.VMEM
    D = pltpu.SemaphoreType.DMA
    scratch = [
        V((64, 128), F32),
        V((8, 2, 4, 1, 128), F32),
        V((11, 4, 8, 1, 128), F32),
        V((11, 16, 32, 128), F32),
        V((312, 1792), BF16),
        V((9, 13, 40, 128), F32),
        V((13, 24, 128), F32),
        V((128, 1792), BF16),
        V((128, 1792), BF16),
        V((128, 3456), BF16),
        V((3456, 512), BF16),
        V((384, 1792), BF16),
        V((128, 1792), BF16),
        V((4, 6, 16, 128), F32),
        V((4, 64, 128), F32),
        V((4, 64, 128), BF16),
        V((nx, 4, 64, 128), BF16),
        V((4 * nx + 2, 64, 128), F32),
        V((4, 256, 3456), BF16),
        V((4, 256, 128), F32),
        V((4, 64, 128), F32),
        V((128, 256), BF16),
        V((2, 64, 128), BF16),
        V((2, 32, 128), BF16),
        V((4, 16, 128), BF16),
        V((2, 64, 128), BF16),
        V((2, 32, 128), BF16),
        V((4, 16, 128), BF16),
        V((6, 10, 16, 128), F32),
        V((256, 3456), BF16),
        V((nx, 4, 32, 128), BF16),
        V((nx, 4, 32, 128), BF16),
        V((nx, 16, 1792), BF16),
        V((nx, 16, 1792), BF16),
        V((16, 1792), F32),
        V((32, 3456), F32),
        V((n, 32, 128), BF16),
        V((n, 32, 128), BF16),
        V((n, 16, 128), BF16),
        V((n, 16, 128), BF16),
        D((1,)),
        D((26,)),
        D((26,)),
        D((nx,)),
        D((nx,)),
        D((8,)),
        D((8,)),
        D((nx,)),
        D((nx,)),
        D((nx,)),
        D((nx,)),
        D((n,)),
        D((n,)),
        D((n,)),
        D((n,)),
    ]
    bottle, grad_down, grad_bottle = pl.pallas_call(
        functools.partial(body, sizes),
        out_shape=(
            jax.ShapeDtypeStruct((4, 64, 128), BF16),
            jax.ShapeDtypeStruct((16, 54), F32),
            jax.ShapeDtypeStruct((32, 108), F32),
        ),
        in_specs=[vmem] * 8,
        out_specs=(vmem, vmem, vmem),
        scratch_shapes=scratch,
        compiler_params=pltpu.CompilerParams(
            collective_id=0, has_side_effects=True, vmem_limit_bytes=60 * 1024 * 1024
        ),
    )(fields, grain_ids, table, w_in, k_fine, k_down, k_bot, cot)
    bottle = bottle.reshape(4, 8, 8, 4, 32).transpose(4, 3, 1, 0, 2).reshape(32, 32, 4, 8)
    return bottle, grad_down, grad_bottle


def solution(mesh):
    sizes = (mesh.shape["gx"], mesh.shape["gy"], mesh.shape["gz"])
    placed = (
        P(None, "gx", "gy", "gz"),
        P("gx", "gy", "gz"),
        P(),
        P(),
        P(),
        P(),
        P("gx", None),
        P("gx", None, "gy", "gz"),
    )
    return jax.shard_map(
        functools.partial(per_device, sizes),
        mesh=mesh,
        in_specs=placed,
        out_specs=(P("gx", None, "gy", "gz"), P("gx", ("gy", "gz")), P("gx", ("gy", "gz"))),
        check_vma=False,
    )
```

```python
import functools
import math

import jax
import jax.numpy as jnp
from jax import lax
from jax.experimental import pallas as pl
from jax.experimental.pallas import tpu as pltpu
from jax.sharding import PartitionSpec as P

MESH = pl.DeviceIdType.MESH
F32 = jnp.float32
BF16 = jnp.bfloat16
NT = (((1,), (1,)), ((), ()))


def silu(v):
    return v * jax.nn.sigmoid(v)


def silu_grad(v):
    s = jax.nn.sigmoid(v)
    return s * (1.0 + v * (1.0 - s))


def dot(a, b):
    return jnp.dot(a, b, preferred_element_type=F32)


def dot_nt(a, b):
    return lax.dot_general(a, b, NT, preferred_element_type=F32)


def tap_of(t):
    t = min(t, 26)
    return t // 9, (t // 3) % 3, t % 3


def lane_iota(shape):
    return lax.broadcasted_iota(jnp.int32, shape, len(shape) - 1)


def piece(ref_tiles, start, width):
    tile, shift = start // 128, start % 128
    low = ref_tiles(tile)
    if shift == 0:
        return low
    low = pltpu.roll(low, 128 - shift, 1)
    if shift + width <= 128:
        return low
    high = pltpu.roll(ref_tiles(tile + 1), 128 - shift, 1)
    return jnp.where(lane_iota(low.shape) < 128 - shift, low, high)


def body(
    sizes,
    fields_h,
    ids_h,
    table_h,
    w_in_h,
    k_fine_h,
    k_down_h,
    k_bot_h,
    cot_h,
    bottle_o,
    gdown_o,
    gbot_o,
    fields,
    ids,
    table,
    w_in,
    k_fine,
    cot,
    cotf,
    cotp,
    tt,
    bo,
    raw,
    brick,
    ext,
    es,
    af,
    fs,
    fmask,
    kf,
    kd,
    kb4,
    wblk,
    ac,
    ad,
    pd,
    cb,
    cs,
    sb,
    slab,
    a3,
    pre,
    gp,
    gt,
    ysend,
    zsend,
    csend,
    yrecv,
    zrecv,
    crecv,
    gpad,
    ag,
    acts,
    actr,
    downs,
    downr,
    dsum,
    gball,
    gbs,
    gbr,
    gb2s,
    gb2r,
    gds,
    gdr,
    sem_l,
    s1,
    r1,
    s2,
    r2,
    s3,
    r3,
    s4,
    r4,
    s5,
    r5,
    s6,
    r6,
    s7,
    r7,
    s8,
    r8,
):
    nx, ny, nz = sizes
    gx, gy, gz = lax.axis_index("gx"), lax.axis_index("gy"), lax.axis_index("gz")
    scale = 1.0 / math.sqrt(nx * 4 * ny * 4 * nz * 8)

    def device(dx, dy, dz):
        return (lax.rem(gx + dx + nx, nx), lax.rem(gy + dy + ny, ny), lax.rem(gz + dz + nz, nz))

    near = [(dx, dy, dz) for dx in (-1, 0, 1) for dy in (-1, 0, 1) for dz in (-1, 0, 1)]
    near = [n for n in near if n != (0, 0, 0)]
    columns = [(dx, 0, 0) for dx in range(1, nx)]
    planes = [(0, dy, dz) for dy in range(ny) for dz in range(nz) if (dy, dz) != (0, 0)]
    partners = sorted({(a % nx, b % ny, c % nz) for a, b, c in near + columns + planes})
    barrier = pltpu.get_barrier_semaphore()
    for p in partners:
        pl.semaphore_signal(barrier, inc=1, device_id=device(*p), device_id_type=MESH)

    loads = [
        pltpu.make_async_copy(src, dst, sem_l.at[1 + i])
        for i, (src, dst) in enumerate(
            [(fields_h, fields), (ids_h, ids), (table_h, table), (w_in_h, w_in), (k_fine_h, k_fine)]
            + [(k_down_h, kd.at[0:1728]), (cot_h, cot)]
            + [(k_bot_h, kb4.at[32 * q : 32 * q + 32]) for q in range(4)]
        )
    ]
    for c in loads:
        c.start()
    kd[1728:1792, :] = jnp.zeros((64, 128), BF16)
    kf[...] = jnp.zeros(kf.shape, BF16)
    wblk[...] = jnp.zeros(wblk.shape, BF16)
    fs[...] = jnp.zeros(fs.shape, F32)
    gpad[...] = jnp.zeros(gpad.shape, F32)
    slab[0] = jnp.zeros((64, 128), F32)
    slab[4 * nx + 1] = jnp.zeros((64, 128), F32)
    cb[...] = jnp.zeros(cb.shape, F32)
    cotf[...] = jnp.zeros(cotf.shape, F32)
    ext[:, :, 6:8] = jnp.zeros((11, 4, 2, 1, 128), F32)
    for c in loads[0:2]:
        c.wait()

    sel_row = lax.broadcasted_iota(jnp.int32, (16, 128), 0)
    sel_lane = lax.broadcasted_iota(jnp.int32, (16, 128), 1)
    packed = jnp.zeros((64, 128), F32)
    for ch in range(8):
        plane = (fields[ch] if ch < 7 else ids[...]).astype(F32).reshape(64, 16).astype(BF16)
        select = jnp.where(sel_lane == sel_row * 8 + ch, 1.0, 0.0).astype(BF16)
        packed = packed + dot(plane, select)
    raw[...] = packed
    group = lane_iota((16, 128)) // 32
    for zb in range(4):
        block = None
        for y4 in range(4):
            rows = raw[pl.ds(y4, 16, stride=4), :]
            shift = ((y4 - zb) * 32) % 128
            rows = rows if shift == 0 else pltpu.roll(rows, shift, 1)
            block = rows if block is None else jnp.where(group == y4, rows, block)
        for r in range(16):
            brick[r // 2, r % 2, zb, :, :] = block[r : r + 1, :]

    for c in loads[2:]:
        c.wait()
    kf[0:64, 0:1728] = k_fine[...]
    kf[64:128, 0:1728] = k_fine[...]
    for t in range(27):
        for q in range(4):
            wblk[t * 128 + q * 32 : t * 128 + q * 32 + 32, q * 128 : q * 128 + 128] = kb4[
                0:32, t * 128 : t * 128 + 128
            ]
    my = gy * 8 - 3 + lax.broadcasted_iota(jnp.int32, (13, 24, 128), 0)
    mz = gz * 16 - 3 + lax.broadcasted_iota(jnp.int32, (13, 24, 128), 1)
    inside = (my >= 0) & (my < ny * 8) & (mz >= 0) & (mz < nz * 16)
    fmask[...] = jnp.where(inside, 1.0, 0.0)

    pl.semaphore_wait(barrier, len(partners))

    x_src = {1: (6, 2, 0), 0: (0, 8, 2), -1: (0, 1, 10)}
    y_src = {1: (1, 1, 0), 0: (0, 2, 1), -1: (0, 1, 3)}
    z_src = {1: (3, 1, 0), 0: (0, 4, 1), -1: (0, 1, 5)}
    halo = []
    for number, (dx, dy, dz) in enumerate(near):
        (xs, xn, xd), (ys, yn, yd), (zs, zn, zd) = x_src[dx], y_src[dy], z_src[dz]
        halo.append(
            pltpu.make_async_remote_copy(
                src_ref=brick.at[xs : xs + xn, ys : ys + yn, zs : zs + zn],
                dst_ref=ext.at[xd : xd + xn, yd : yd + yn, zd : zd + zn],
                send_sem=s1.at[number],
                recv_sem=r1.at[number],
                device_id=device(dx, dy, dz),
                device_id_type=MESH,
            )
        )
    for c in halo:
        c.start()
    own = pltpu.make_async_copy(brick, ext.at[2:10, 1:3, 1:5], sem_l.at[0])
    own.start()

    row8 = lax.broadcasted_iota(jnp.int32, (128, 7), 0) % 8
    pick = jnp.where(row8 == lax.broadcasted_iota(jnp.int32, (128, 7), 1), 1.0, 0.0).astype(BF16)
    emb_row = lax.broadcasted_iota(jnp.int32, (128, 256), 0) // 8
    twice = jnp.where(
        lax.broadcasted_iota(jnp.int32, (64, 128), 1) % 64
        == lax.broadcasted_iota(jnp.int32, (64, 128), 0),
        1.0,
        0.0,
    ).astype(BF16)
    w_rows = dot(pick, dot(w_in[...], twice).astype(BF16))
    table2 = jnp.concatenate([table[...]] * 2, axis=0)
    id_rows = jnp.where(lax.broadcasted_iota(jnp.int32, (128, 128), 0) % 8 == 7, 1.0, 0.0)
    w_emb = jnp.concatenate([id_rows, w_rows], axis=1)

    own.wait()
    for c in halo:
        c.wait()

    blocks = ext[...].reshape(44, 8, 128)
    bx = lax.broadcasted_iota(jnp.int32, (44, 8, 128), 0)
    by = bx % 4
    bx = bx // 4
    bz = lax.broadcasted_iota(jnp.int32, (44, 8, 128), 1)
    outside = ((bx < 2) & (gx == 0)) | ((bx == 10) & (gx == nx - 1))
    outside = outside | ((by == 0) & (gy == 0)) | ((by == 3) & (gy == ny - 1))
    outside = outside | ((bz == 0) & (gz == 0)) | ((bz == 5) & (gz == nz - 1))
    fill = jnp.where(lane_iota((44, 8, 128)) % 8 == 7, -1.0, 0.0)
    blocks = jnp.where(outside, fill, blocks).reshape(352, 128).astype(BF16)
    lanes = lane_iota((352, 128)).astype(F32)
    for p in range(16):
        y4, z4 = p // 4, p % 4
        w_p = jnp.where(emb_row == p, w_emb, 0.0).astype(BF16)
        both = dot(blocks, w_p)
        onehot = jnp.where(both[:, 0:128] == lanes, 1.0, 0.0).astype(BF16)
        value = silu(both[:, 128:256] + dot_nt(onehot, table2)).reshape(11, 4, 8, 128)
        for x in range(11):
            for yb in range(4):
                es[x, yb * 4 + y4, pl.ds(z4, 8, stride=4), :] = value[x, yb]

    half = lane_iota((13, 24, 128)) < 64

    def fine_plane(x, carry):
        for t in range(14):
            (ax, ay, az), (bx_, by_, bz_) = tap_of(2 * t), tap_of(2 * t + 1)
            low = es[x + ax, ay : ay + 13, az : az + 24, :]
            high = es[x + bx_, by_ : by_ + 13, bz_ : bz_ + 24, :]
            block = jnp.where(half, low, high)
            af[:, t * 128 : t * 128 + 128] = block.reshape(312, 128).astype(BF16)
        value = silu(dot_nt(af[...], kf[...])).reshape(13, 24, 128)
        keep = jnp.where((x > 0) | (gx > 0), 1.0, 0.0)
        value = value * fmask[...] * keep
        fs[x, :, 0:24, :] = value.astype(BF16).astype(F32)
        return carry

    def coarse_copy(x, k):
        return pltpu.make_async_remote_copy(
            src_ref=cs.at[x],
            dst_ref=sb.at[gx, x],
            send_sem=s2.at[x, k],
            recv_sem=r2.at[x, k],
            device_id=device(k, 0, 0),
            device_id_type=MESH,
        )

    half16 = lane_iota((16, 128)) < 64
    cy = gy * 4 - 1 + lax.broadcasted_iota(jnp.int32, (6, 16, 128), 0)
    cz = gz * 8 - 1 + lax.broadcasted_iota(jnp.int32, (6, 16, 128), 1)
    inside = (cy >= 0) & (cy < ny * 4) & (cz >= 0) & (cz < nz * 8)

    def coarse_plane(x, carry):
        lax.fori_loop(2 * x + 1, 2 * x + 3, fine_plane, 0)
        for y in range(6):
            row = y * 16
            for t in range(14):
                (ax, ay, az), (bx_, by_, bz_) = tap_of(2 * t), tap_of(2 * t + 1)
                low = fs[2 * x + ax, 2 * y + ay, pl.ds(az, 16, stride=2), :]
                high = fs[2 * x + bx_, 2 * y + by_, pl.ds(bz_, 16, stride=2), :]
                ac[row : row + 16, t * 128 : t * 128 + 128] = jnp.where(half16, low, high).astype(BF16)
        before = dot(ac[...], kd[...]).reshape(6, 16, 128)
        pd[x] = before
        coarse = jnp.where(inside, silu(before), 0.0)
        for y in range(6):
            cb[x, y * 10 : y * 10 + 10, :] = coarse[y, 0:10, :]
        cs[x] = cb[x].astype(BF16)
        for k in range(1, nx):
            coarse_copy(x, k).start()
        return carry

    fine_plane(0, 0)
    lax.fori_loop(0, 4, coarse_plane, 0)

    half8 = lane_iota((8, 128)) < 64
    for y in range(4):
        for t in range(14):
            (ax, ay, az), (bx_, by_, bz_) = tap_of(2 * t), tap_of(2 * t + 1)
            parts = []
            for x in range(4):
                low = fs[2 * x + ax, 2 * y + 2 + ay, pl.ds(2 + az, 8, stride=2), :]
                high = fs[2 * x + bx_, 2 * y + 2 + by_, pl.ds(2 + bz_, 8, stride=2), :]
                parts.append(jnp.where(half8, low, high))
            ad[y * 32 : y * 32 + 32, t * 128 : t * 128 + 128] = jnp.concatenate(parts, axis=0).astype(BF16)

    slab[pl.ds(1 + gx * 4, 4)] = cs[...].astype(F32)

    cotf[:, 0:32] = cot[...].astype(F32).reshape(1024, 32)
    group = lane_iota((32, 128)) // 8
    spread = lax.broadcasted_iota(jnp.int32, (8, 128), 0)
    spread = jnp.where(lane_iota((8, 128)) % 8 == spread, 1.0, 0.0).astype(BF16)
    for y in range(4):
        for z in range(8):
            rows = cotf[pl.ds(y * 8 + z, 32, stride=32), :]
            rows = jnp.concatenate([jnp.where(group == q, rows, 0.0) for q in range(4)], axis=0)
            cotp[y, pl.ds(z, 8, stride=8), :] = dot_nt(spread, rows.astype(BF16))

    for k in range(1, nx):
        for x in range(4):
            coarse_copy(x, k).wait()
        source = lax.rem(gx - k + nx, nx)
        slab[pl.ds(1 + source * 4, 4)] = sb[source].astype(F32)

    for y in range(4):
        for t in range(27):
            ax, ay, az = tap_of(t)
            start = (y + ay) * 10 + az
            window = slab[ax : ax + 32, start : start + 8, :].reshape(4, 64, 128).astype(BF16)
            a3[:, y * 64 : y * 64 + 64, t * 128 : t * 128 + 128] = window

    def bottle_group(q, carry):
        pre[q] = dot_nt(a3[q], kb4[...])
        return carry

    lax.fori_loop(0, 4, bottle_group, 0)
    group = lane_iota((256, 128)) // 32
    z = pre[0]
    for q in range(1, 4):
        z = jnp.where(group == q, pre[q], z)
    grad = cotp[...].reshape(256, 128) * silu_grad(z)
    grad = grad.astype(BF16).astype(F32)
    gp[...] = grad.reshape(4, 64, 128)

    for side in range(2):
        ysend[side] = gp[3 - 3 * side].astype(BF16)
        zsend[side] = jnp.concatenate(
            [gp[y, pl.ds(7 - 7 * side, 8, stride=8), :] for y in range(4)], axis=0
        ).astype(BF16)
        for other in range(2):
            corner = gp[3 - 3 * side, pl.ds(7 - 7 * other, 8, stride=8), :]
            csend[side * 2 + other] = jnp.concatenate([corner, corner], axis=0).astype(BF16)
    rim = []

    def rim_copy(src, dst, number, dy, dz):
        c = pltpu.make_async_remote_copy(
            src_ref=src,
            dst_ref=dst,
            send_sem=s3.at[number],
            recv_sem=r3.at[number],
            device_id=device(0, dy, dz),
            device_id_type=MESH,
        )
        c.start()
        rim.append(c)

    for side in range(2):
        rim_copy(ysend.at[side], yrecv.at[side], side, 1 - 2 * side, 0)
    for side in range(2):
        rim_copy(zsend.at[side], zrecv.at[side], 2 + side, 0, 1 - 2 * side)
    for corner in range(4):
        rim_copy(
            csend.at[corner],
            crecv.at[corner],
            4 + corner,
            1 - 2 * (corner // 2),
            1 - 2 * (corner % 2),
        )

    gt[...] = jnp.transpose(grad).astype(BF16)
    for n in range(9):
        total = None
        for q in range(4):
            part = dot(gt[32 * q : 32 * q + 32, :], a3[q, :, n * 384 : n * 384 + 384])
            total = part if total is None else total + part
        gball[:, n * 384 : n * 384 + 384] = total * scale
    for k in range(ny * nz):
        cut = piece(lambda tile: gball[:, tile * 128 : tile * 128 + 128], 108 * k, 108)
        gbs[k % nz, k // nz] = cut.astype(BF16)
    me = gy * nz + gz
    gb_copies = []
    for k in range(1, nz):
        target = lax.rem(gz + k, nz)
        gb_copies.append(
            pltpu.make_async_remote_copy(
                src_ref=gbs.at[target],
                dst_ref=gbr.at[gz],
                send_sem=s6.at[k],
                recv_sem=r6.at[k],
                device_id=(gx, gy, target),
                device_id_type=MESH,
            )
        )

    gpad[1:5, 1:9, 1:9, :] = gp[...].reshape(4, 8, 8, 128)
    for c in rim:
        c.wait()
    for c in gb_copies:
        c.start()

    def kept(flag, value):
        return jnp.where(flag, value.astype(F32), 0.0)

    y_ok = (gy > 0, gy < ny - 1)
    z_ok = (gz > 0, gz < nz - 1)
    for side in range(2):
        gpad[5 * side, 1:9, 1:9, :] = kept(y_ok[side], yrecv[side]).reshape(8, 8, 128)
        value = kept(z_ok[side], zrecv[side])
        for y in range(4):
            gpad[1 + y, 1:9, 9 * side : 9 * side + 1, :] = value[8 * y : 8 * y + 8].reshape(8, 1, 128)
        for other in range(2):
            value = kept(y_ok[side] & z_ok[other], crecv[side * 2 + other])
            gpad[5 * side, 1:9, 9 * other : 9 * other + 1, :] = value[0:8].reshape(8, 1, 128)
    edge = lane_iota((96, 128))
    low = pltpu.roll(gpad[:, 8, :, :].reshape(96, 128), 32, 1)
    gpad[:, 0, :, :] = jnp.where(edge < 32, 0.0, low).reshape(6, 16, 128)
    high = pltpu.roll(gpad[:, 1, :, :].reshape(96, 128), 96, 1)
    gpad[:, 9, :, :] = jnp.where(edge >= 96, 0.0, high).reshape(6, 16, 128)

    for t in range(27):
        ax, ay, az = tap_of(t)
        window = gpad[2 - ay : 6 - ay, 2 - ax : 10 - ax, 2 - az : 10 - az, :]
        ag[:, t * 128 : t * 128 + 128] = window.reshape(256, 128).astype(BF16)
    def act_copy(slot, target, source):
        return pltpu.make_async_remote_copy(
            src_ref=acts.at[target],
            dst_ref=actr.at[slot],
            send_sem=s4.at[target],
            recv_sem=r4.at[source],
            device_id=(target, gy, gz),
            device_id_type=MESH,
        )

    for q in range(4):
        act = dot(ag[...], wblk[:, q * 128 : q * 128 + 128]).reshape(4, 64, 128).astype(BF16)
        for part in range(2):
            target = 2 * q + part
            acts[target] = act[:, part * 32 : part * 32 + 32, :]

            @pl.when(gx != target)
            def _(target=target):
                act_copy(gx, target, gx).start()

    z = pre[0]
    group = lane_iota((256, 128)) // 32
    for q in range(1, 4):
        z = jnp.where(group == q, pre[q], z)
    out = silu(z).astype(BF16).astype(F32).reshape(4, 64, 128)
    for y in range(4):
        turned = jnp.transpose(jnp.concatenate([out[y], jnp.zeros((64, 128), F32)], axis=0))
        for q in range(4):
            tt[y * 32 : y * 32 + 32, q * 128 : q * 128 + 128] = turned[q * 32 : q * 32 + 32].astype(BF16)
    row = lax.broadcasted_iota(jnp.int32, (512, 128), 0)
    x_of = (row // 128) * 8 + (row % 128) // 8
    x_of = jnp.where(row % 128 < 64, x_of, -1)
    for k in range(8):
        select = jnp.where((x_of == lane_iota((512, 128))) & (row % 8 == k), 1.0, 0.0).astype(BF16)
        turned = dot(tt[...], select)
        for y in range(4):
            bo[pl.ds(y * 8 + k, 32, stride=32), :] = turned[y * 32 : y * 32 + 32]
    bottle_o[...] = bo[...].reshape(32, 4, 8, 128)[:, :, :, 0:32].astype(BF16)

    slope = []
    for y in range(4):
        for x in range(4):
            slope.append(silu_grad(pd[x, y + 1, 1:9, :]))
    slope = jnp.concatenate(slope, axis=0)
    total = acts[gx].astype(F32)
    for k in range(1, nx):
        source = lax.rem(gx - k + nx, nx)
        act_copy(source, lax.rem(gx + k, nx), source).wait()
        total = total + actr[source].astype(F32)
    grad_down = (total.reshape(128, 128) * slope).astype(BF16).astype(F32)
    grad_down_t = jnp.transpose(grad_down).astype(BF16)

    part = dot(grad_down_t, ad[...]) * scale
    downs[...] = part.reshape(nx, 16, 1792).astype(BF16)
    down_copies = []
    for k in range(1, nx):
        target = lax.rem(gx + k, nx)
        down_copies.append(
            pltpu.make_async_remote_copy(
                src_ref=downs.at[target],
                dst_ref=downr.at[gx],
                send_sem=s5.at[k],
                recv_sem=r5.at[k],
                device_id=(target, gy, gz),
                device_id_type=MESH,
            )
        )
    for c in down_copies:
        c.start()

    total = gbs[gz].astype(F32)
    for k, c in enumerate(gb_copies, 1):
        c.wait()
        total = total + gbr[lax.rem(gz - k + nz, nz)].astype(F32)
    gb2s[...] = total.astype(BF16)
    gb2_copies = []
    for k in range(1, ny):
        target = lax.rem(gy + k, ny)
        c = pltpu.make_async_remote_copy(
            src_ref=gb2s.at[target],
            dst_ref=gb2r.at[gy],
            send_sem=s8.at[k],
            recv_sem=r8.at[k],
            device_id=(gx, target, gz),
            device_id_type=MESH,
        )
        c.start()
        gb2_copies.append(c)

    dsum[...] = downs[gx].astype(F32)
    for k, c in enumerate(down_copies, 1):
        c.wait()
        dsum[...] += downr[lax.rem(gx - k + nx, nx)].astype(F32)
    low_half = lane_iota((8, 128)) < 64
    for k in range(ny * nz):
        cut = piece(lambda tile: dsum[:, tile * 128 : tile * 128 + 128], 54 * k, 54)
        cut = jnp.where(low_half, cut[0:8], pltpu.roll(cut[8:16], 64, 1))
        gds[k] = cut.astype(BF16)
    gd_copies = []
    planes.sort(key=lambda p: -2 * min(p[1], ny - p[1]) - min(p[2], nz - p[2]))
    for k, (_, dy, dz) in enumerate(planes):
        ty, tz = lax.rem(gy + dy, ny), lax.rem(gz + dz, nz)
        c = pltpu.make_async_remote_copy(
            src_ref=gds.at[ty * nz + tz],
            dst_ref=gdr.at[me],
            send_sem=s7.at[k],
            recv_sem=r7.at[k],
            device_id=(gx, ty, tz),
            device_id_type=MESH,
        )
        c.start()
        gd_copies.append(c)
    total = gb2s[gy].astype(F32)
    for k, c in enumerate(gb2_copies, 1):
        c.wait()
        total = total + gb2r[lax.rem(gy - k + ny, ny)].astype(F32)
    gbot_o[...] = total[:, 0:108]
    total = gds[me].astype(F32)
    for c in gd_copies:
        c.wait()
    for k, (_, dy, dz) in enumerate(planes):
        source = lax.rem(gy - dy + ny, ny) * nz + lax.rem(gz - dz + nz, nz)
        total = total + gdr[source].astype(F32)
    gdown_o[0:8, :] = total[:, 0:54]
    gdown_o[8:16, :] = pltpu.roll(total, 64, 1)[:, 0:54]


def per_device(sizes, fields, grain_ids, table, w_in, k_fine, k_down, k_bot, cotangent):
    nx, ny, nz = sizes
    n = ny * nz
    cot = cotangent.transpose(0, 2, 3, 1)
    vmem = pl.BlockSpec(memory_space=pltpu.VMEM)
    V = pltpu.VMEM
    D = pltpu.SemaphoreType.DMA
    scratch = [
        V((7, 8, 8, 16), BF16),
        V((8, 8, 16), jnp.int32),
        V((64, 128), BF16),
        V((7, 64), BF16),
        V((64, 1728), BF16),
        V((32, 4, 8, 32), BF16),
        V((1024, 128), F32),
        V((4, 64, 128), F32),
        V((128, 512), BF16),
        V((1024, 128), F32),
        V((64, 128), F32),
        V((8, 2, 4, 1, 128), F32),
        V((11, 4, 8, 1, 128), F32),
        V((11, 16, 32, 128), F32),
        V((312, 1792), BF16),
        V((9, 13, 40, 128), F32),
        V((13, 24, 128), F32),
        V((128, 1792), BF16),
        V((1792, 128), BF16),
        V((128, 3456), BF16),
        V((3456, 512), BF16),
        V((96, 1792), BF16),
        V((128, 1792), BF16),
        V((4, 6, 16, 128), F32),
        V((4, 64, 128), F32),
        V((4, 64, 128), BF16),
        V((nx, 4, 64, 128), BF16),
        V((4 * nx + 2, 64, 128), F32),
        V((4, 256, 3456), BF16),
        V((4, 256, 128), F32),
        V((4, 64, 128), F32),
        V((128, 256), BF16),
        V((2, 64, 128), BF16),
        V((2, 32, 128), BF16),
        V((4, 16, 128), BF16),
        V((2, 64, 128), BF16),
        V((2, 32, 128), BF16),
        V((4, 16, 128), BF16),
        V((6, 10, 16, 128), F32),
        V((256, 3456), BF16),
        V((nx, 4, 32, 128), BF16),
        V((nx, 4, 32, 128), BF16),
        V((nx, 16, 1792), BF16),
        V((nx, 16, 1792), BF16),
        V((16, 1792), F32),
        V((32, 3456), F32),
        V((nz, ny, 32, 128), BF16),
        V((nz, ny, 32, 128), BF16),
        V((ny, 32, 128), BF16),
        V((ny, 32, 128), BF16),
        V((n, 8, 128), BF16),
        V((n, 8, 128), BF16),
        D((12,)),
        D((26,)),
        D((26,)),
        D((4, nx)),
        D((4, nx)),
        D((8,)),
        D((8,)),
        D((nx,)),
        D((nx,)),
        D((nx,)),
        D((nx,)),
        D((nz,)),
        D((nz,)),
        D((n,)),
        D((n,)),
        D((ny,)),
        D((ny,)),
    ]
    bottle, grad_down, grad_bottle = pl.pallas_call(
        functools.partial(body, sizes),
        out_shape=(
            jax.ShapeDtypeStruct((32, 4, 8, 32), BF16),
            jax.ShapeDtypeStruct((16, 54), F32),
            jax.ShapeDtypeStruct((32, 108), F32),
        ),
        in_specs=[pl.BlockSpec(memory_space=pl.ANY)] * 8,
        out_specs=(vmem, vmem, vmem),
        scratch_shapes=scratch,
        compiler_params=pltpu.CompilerParams(
            collective_id=0, has_side_effects=True, vmem_limit_bytes=60 * 1024 * 1024
        ),
    )(fields, grain_ids, table.T, w_in.T, k_fine, k_down.T, k_bot, cot)
    return bottle.transpose(0, 3, 1, 2), grad_down, grad_bottle


def solution(mesh):
    sizes = (mesh.shape["gx"], mesh.shape["gy"], mesh.shape["gz"])
    placed = (
        P(None, "gx", "gy", "gz"),
        P("gx", "gy", "gz"),
        P(),
        P(),
        P(),
        P(),
        P("gx", None),
        P("gx", None, "gy", "gz"),
    )
    return jax.shard_map(
        functools.partial(per_device, sizes),
        mesh=mesh,
        in_specs=placed,
        out_specs=(P("gx", None, "gy", "gz"), P("gx", ("gy", "gz")), P("gx", ("gy", "gz"))),
        check_vma=False,
    )
```

```python
import functools
import math

import jax
import jax.numpy as jnp
from jax import lax
from jax.experimental import pallas as pl
from jax.experimental.pallas import tpu as pltpu
from jax.sharding import PartitionSpec as P

MESH = pl.DeviceIdType.MESH
F32 = jnp.float32
BF16 = jnp.bfloat16
NT = (((1,), (1,)), ((), ()))


def silu(v):
    return v * jax.nn.sigmoid(v)


def silu_grad(v):
    s = jax.nn.sigmoid(v)
    return s * (1.0 + v * (1.0 - s))


def dot(a, b):
    return jnp.dot(a, b, preferred_element_type=F32)


def dot_nt(a, b):
    return lax.dot_general(a, b, NT, preferred_element_type=F32)


def tap_of(t):
    t = min(t, 26)
    return t // 9, (t // 3) % 3, t % 3


def lane_iota(shape):
    return lax.broadcasted_iota(jnp.int32, shape, len(shape) - 1)


def piece(ref_tiles, start, width):
    tile, shift = start // 128, start % 128
    low = ref_tiles(tile)
    if shift == 0:
        return low
    low = pltpu.roll(low, 128 - shift, 1)
    if shift + width <= 128:
        return low
    high = pltpu.roll(ref_tiles(tile + 1), 128 - shift, 1)
    return jnp.where(lane_iota(low.shape) < 128 - shift, low, high)


def body(
    sizes,
    fields_h,
    ids_h,
    table_h,
    w_in_h,
    k_fine_h,
    k_down_h,
    k_bot_h,
    cot_h,
    bottle_o,
    gdown_o,
    gbot_o,
    fields,
    ids,
    table,
    w_in,
    k_fine,
    cot,
    cotf,
    cotp,
    tt,
    bo,
    raw,
    brick,
    ext,
    es,
    af,
    yf,
    fs,
    fmask,
    kf,
    kd,
    kb,
    wblk,
    ac,
    ad,
    pd,
    cb,
    cs,
    sb,
    slab,
    a3,
    ysum,
    pre,
    gp,
    gt,
    ysend,
    zsend,
    csend,
    yrecv,
    zrecv,
    crecv,
    gpad,
    gpadr,
    ag,
    acts,
    actr,
    downs,
    downr,
    dsum,
    gball,
    gbs,
    gbr,
    gb2s,
    gb2r,
    gds,
    gdr,
    sem_l,
    s1,
    r1,
    s2,
    r2,
    s3,
    r3,
    s4,
    r4,
    s5,
    r5,
    s6,
    r6,
    s7,
    r7,
    s8,
    r8,
):
    nx, ny, nz = sizes
    gx, gy, gz = lax.axis_index("gx"), lax.axis_index("gy"), lax.axis_index("gz")
    scale = 1.0 / math.sqrt(nx * 4 * ny * 4 * nz * 8)

    def device(dx, dy, dz):
        return (lax.rem(gx + dx + nx, nx), lax.rem(gy + dy + ny, ny), lax.rem(gz + dz + nz, nz))

    near = [(dx, dy, dz) for dx in (-1, 0, 1) for dy in (-1, 0, 1) for dz in (-1, 0, 1)]
    near = [n for n in near if n != (0, 0, 0)]
    columns = [(dx, 0, 0) for dx in range(1, nx)]
    planes = [(0, dy, dz) for dy in range(ny) for dz in range(nz) if (dy, dz) != (0, 0)]
    partners = sorted({(a % nx, b % ny, c % nz) for a, b, c in near + columns + planes})
    barrier = pltpu.get_barrier_semaphore()
    for p in partners:
        pl.semaphore_signal(barrier, inc=1, device_id=device(*p), device_id_type=MESH)

    loads = [
        pltpu.make_async_copy(src, dst, sem_l.at[1 + i])
        for i, (src, dst) in enumerate(
            [(fields_h, fields), (ids_h, ids), (table_h, table), (w_in_h, w_in), (k_fine_h, k_fine)]
            + [(k_down_h, kd.at[0:1728]), (cot_h, cot)]
            + [
                (k_bot_h.at[:, x * 1152 : x * 1152 + 1152], kb.at[32 * x : 32 * x + 32])
                for x in range(3)
            ]
        )
    ]
    for c in loads:
        c.start()
    kd[1728:1792, :] = jnp.zeros((64, 128), BF16)
    kb[96:128, :] = jnp.zeros((32, 1152), BF16)
    kf[...] = jnp.zeros(kf.shape, BF16)
    wblk[...] = jnp.zeros(wblk.shape, BF16)
    fs[...] = jnp.zeros(fs.shape, F32)
    gpad[...] = jnp.zeros(gpad.shape, F32)
    slab[0] = jnp.zeros((64, 128), F32)
    slab[4 * nx + 1 : 4 * nx + 4] = jnp.zeros((3, 64, 128), F32)
    cb[...] = jnp.zeros(cb.shape, F32)
    cotf[...] = jnp.zeros(cotf.shape, F32)
    ext[:, :, 6:8] = jnp.zeros((11, 4, 2, 1, 128), F32)
    for c in loads[0:2]:
        c.wait()

    sel_row = lax.broadcasted_iota(jnp.int32, (16, 128), 0)
    sel_lane = lax.broadcasted_iota(jnp.int32, (16, 128), 1)
    packed = jnp.zeros((64, 128), F32)
    for ch in range(8):
        plane = (fields[ch] if ch < 7 else ids[...]).astype(F32).reshape(64, 16).astype(BF16)
        select = jnp.where(sel_lane == sel_row * 8 + ch, 1.0, 0.0).astype(BF16)
        packed = packed + dot(plane, select)
    raw[...] = packed
    group = lane_iota((16, 128)) // 32
    for zb in range(4):
        block = None
        for y4 in range(4):
            rows = raw[pl.ds(y4, 16, stride=4), :]
            shift = ((y4 - zb) * 32) % 128
            rows = rows if shift == 0 else pltpu.roll(rows, shift, 1)
            block = rows if block is None else jnp.where(group == y4, rows, block)
        for r in range(16):
            brick[r // 2, r % 2, zb, :, :] = block[r : r + 1, :]

    for c in loads[2:]:
        c.wait()
    lane = lane_iota((64, 640))
    first = jnp.where(lane < 576, k_fine[:, 0:640].astype(F32), 0.0)
    second = pltpu.roll(k_fine[:, 512:1152].astype(F32), 576, 1)
    kf[0:64, :] = first.astype(BF16)
    kf[64:128, :] = jnp.where(lane < 576, second, 0.0).astype(BF16)
    for n in (128, 192):
        kf[n : n + 64, 0:576] = k_fine[:, 1152:1728]
    for t in range(27):
        for q in range(2):
            row = t * 64 + q * 32
            wblk[row : row + 32, q * 128 : q * 128 + 128] = kb[
                (t // 9) * 32 : (t // 9) * 32 + 32, (t % 9) * 128 : (t % 9) * 128 + 128
            ]
    my = gy * 8 - 3 + lax.broadcasted_iota(jnp.int32, (13, 24, 128), 0)
    mz = gz * 16 - 3 + lax.broadcasted_iota(jnp.int32, (13, 24, 128), 1)
    inside = (my >= 0) & (my < ny * 8) & (mz >= 0) & (mz < nz * 16)
    fmask[...] = jnp.where(inside, 1.0, 0.0)

    pl.semaphore_wait(barrier, len(partners))

    x_src = {1: (6, 2, 0), 0: (0, 8, 2), -1: (0, 1, 10)}
    y_src = {1: (1, 1, 0), 0: (0, 2, 1), -1: (0, 1, 3)}
    z_src = {1: (3, 1, 0), 0: (0, 4, 1), -1: (0, 1, 5)}
    halo = []
    for number, (dx, dy, dz) in enumerate(near):
        (xs, xn, xd), (ys, yn, yd), (zs, zn, zd) = x_src[dx], y_src[dy], z_src[dz]
        halo.append(
            pltpu.make_async_remote_copy(
                src_ref=brick.at[xs : xs + xn, ys : ys + yn, zs : zs + zn],
                dst_ref=ext.at[xd : xd + xn, yd : yd + yn, zd : zd + zn],
                send_sem=s1.at[number],
                recv_sem=r1.at[number],
                device_id=device(dx, dy, dz),
                device_id_type=MESH,
            )
        )
    for c in halo:
        c.start()
    own = pltpu.make_async_copy(brick, ext.at[2:10, 1:3, 1:5], sem_l.at[0])
    own.start()

    row8 = lax.broadcasted_iota(jnp.int32, (128, 7), 0) % 8
    pick = jnp.where(row8 == lax.broadcasted_iota(jnp.int32, (128, 7), 1), 1.0, 0.0).astype(BF16)
    emb_lane = lane_iota((128, 128)) // 8
    twice = jnp.where(
        lax.broadcasted_iota(jnp.int32, (64, 128), 1) % 64
        == lax.broadcasted_iota(jnp.int32, (64, 128), 0),
        1.0,
        0.0,
    ).astype(BF16)
    w_rows = dot(pick, dot(w_in[...], twice).astype(BF16))
    table2 = jnp.concatenate([table[...]] * 2, axis=0)
    w_cols = jnp.transpose(w_rows)

    own.wait()
    for c in halo:
        c.wait()

    blocks = ext[...].reshape(44, 8, 128)
    bx = lax.broadcasted_iota(jnp.int32, (44, 8, 128), 0)
    by = bx % 4
    bx = bx // 4
    bz = lax.broadcasted_iota(jnp.int32, (44, 8, 128), 1)
    outside = ((bx < 2) & (gx == 0)) | ((bx == 10) & (gx == nx - 1))
    outside = outside | ((by == 0) & (gy == 0)) | ((by == 3) & (gy == ny - 1))
    outside = outside | ((bz == 0) & (gz == 0)) | ((bz == 5) & (gz == nz - 1))
    fill = jnp.where(lane_iota((44, 8, 128)) % 8 == 7, -1.0, 0.0)
    blocks = jnp.where(outside, fill, blocks).reshape(352, 128)
    components = blocks.astype(BF16)
    lanes = lane_iota((352, 128)).astype(F32)
    for p in range(16):
        y4, z4 = p // 4, p % 4
        w_p = jnp.where(emb_lane == p, w_cols, 0.0).astype(BF16)
        grain = jnp.broadcast_to(blocks[:, p * 8 + 7 : p * 8 + 8], (352, 128))
        onehot = jnp.where(grain == lanes, 1.0, 0.0).astype(BF16)
        both = jnp.concatenate([onehot, components], axis=1)
        value = silu(dot_nt(both, jnp.concatenate([table2, w_p], axis=1)))
        value = value.reshape(11, 4, 8, 128)
        for x in range(11):
            for yb in range(4):
                es[x, yb * 4 + y4, pl.ds(z4, 8, stride=4), :] = value[x, yb]

    half = lane_iota((13, 24, 128)) < 64

    def spread_plane(e):
        for t in range(5):
            ay, az = (2 * t) // 3, (2 * t) % 3
            by_, bz_ = min(2 * t + 1, 8) // 3, min(2 * t + 1, 8) % 3
            low = es[e, ay : ay + 13, az : az + 24, :]
            high = es[e, by_ : by_ + 13, bz_ : bz_ + 24, :]
            block = jnp.where(half, low, high)
            af[:, t * 128 : t * 128 + 128] = block.reshape(312, 128).astype(BF16)
        yf[e] = dot_nt(af[...], kf[...])

    half_rows = lane_iota((312, 128)) < 64

    def fine_plane(x, carry):
        spread_plane(x + 2)
        two = jnp.where(half_rows, yf[x, :, 0:128], yf[x + 1, :, 0:128])
        value = two + pltpu.roll(two, 64, 1) + yf[x + 2, :, 128:256]
        value = silu(value).reshape(13, 24, 128)
        keep = jnp.where((x > 0) | (gx > 0), 1.0, 0.0)
        value = value * fmask[...] * keep
        fs[x, :, 0:24, :] = value.astype(BF16).astype(F32)
        return carry

    def coarse_copy(x, k):
        return pltpu.make_async_remote_copy(
            src_ref=cs.at[x],
            dst_ref=sb.at[gx, x],
            send_sem=s2.at[x, k],
            recv_sem=r2.at[x, k],
            device_id=device(k, 0, 0),
            device_id_type=MESH,
        )

    half16 = lane_iota((16, 128)) < 64
    cy = gy * 4 - 1 + lax.broadcasted_iota(jnp.int32, (6, 16, 128), 0)
    cz = gz * 8 - 1 + lax.broadcasted_iota(jnp.int32, (6, 16, 128), 1)
    inside = (cy >= 0) & (cy < ny * 4) & (cz >= 0) & (cz < nz * 8)

    def coarse_plane(x, carry):
        lax.fori_loop(2 * x + 1, 2 * x + 3, fine_plane, 0)
        for y in range(6):
            row = y * 16
            for t in range(14):
                (ax, ay, az), (bx_, by_, bz_) = tap_of(2 * t), tap_of(2 * t + 1)
                low = fs[2 * x + ax, 2 * y + ay, pl.ds(az, 16, stride=2), :]
                high = fs[2 * x + bx_, 2 * y + by_, pl.ds(bz_, 16, stride=2), :]
                ac[row : row + 16, t * 128 : t * 128 + 128] = jnp.where(half16, low, high).astype(BF16)
        before = dot(ac[...], kd[...]).reshape(6, 16, 128)
        pd[x] = before
        coarse = jnp.where(inside, silu(before), 0.0)
        for y in range(6):
            cb[x, y * 10 : y * 10 + 10, :] = coarse[y, 0:10, :]
        cs[x] = cb[x].astype(BF16)
        for k in range(1, nx):
            coarse_copy(x, k).start()
        return carry

    def first_planes(e, carry):
        spread_plane(e)
        return carry

    lax.fori_loop(0, 2, first_planes, 0)
    fine_plane(0, 0)
    lax.fori_loop(0, 4, coarse_plane, 0)

    half8 = lane_iota((8, 128)) < 64
    for x in range(4):
        for t in range(14):
            (ax, ay, az), (bx_, by_, bz_) = tap_of(2 * t), tap_of(2 * t + 1)
            parts = []
            for y in range(4):
                low = fs[2 * x + ax, 2 * y + 2 + ay, pl.ds(2 + az, 8, stride=2), :]
                high = fs[2 * x + bx_, 2 * y + 2 + by_, pl.ds(2 + bz_, 8, stride=2), :]
                parts.append(jnp.where(half8, low, high))
            ad[x * 32 : x * 32 + 32, t * 128 : t * 128 + 128] = jnp.concatenate(parts, axis=0).astype(BF16)

    slab[pl.ds(1 + gx * 4, 4)] = cs[...].astype(F32)

    cotf[:, 0:32] = cot[...].astype(F32).reshape(1024, 32)
    group = lane_iota((32, 128)) // 8
    spread = lax.broadcasted_iota(jnp.int32, (8, 128), 0)
    spread = jnp.where(lane_iota((8, 128)) % 8 == spread, 1.0, 0.0).astype(BF16)
    for y in range(4):
        for z in range(8):
            rows = cotf[pl.ds(y * 8 + z, 32, stride=32), :]
            rows = jnp.concatenate([jnp.where(group == q, rows, 0.0) for q in range(4)], axis=0)
            cotp[pl.ds(y * 8 + z, 8, stride=32), :] = dot_nt(spread, rows.astype(BF16))

    for k in range(1, nx):
        for x in range(4):
            coarse_copy(x, k).wait()
        source = lax.rem(gx - k + nx, nx)
        slab[pl.ds(1 + source * 4, 4)] = sb[source].astype(F32)

    for pair in range(2):
        for t in range(9):
            start = (2 * pair + t // 3) * 10 + t % 3
            window = [slab[:, start : start + 8, :], slab[:, start + 10 : start + 18, :]]
            window = jnp.concatenate(window, axis=1).astype(BF16)
            a3[:, pair * 16 : pair * 16 + 16, t * 128 : t * 128 + 128] = window

    def bottle_planes(c, carry):
        part = a3[pl.ds(c * 9, 9)].reshape(288, 1152)
        ysum[pl.ds(c * 9, 9)] = dot_nt(part, kb[...]).reshape(9, 32, 128)
        return carry

    lax.fori_loop(0, 4, bottle_planes, 0)
    group = lane_iota((256, 128)) // 32
    z = None
    for ax in range(3):
        term = None
        for q in range(4):
            rows = ysum[8 * q + ax : 8 * q + ax + 8].reshape(256, 128)
            shift = ((q - ax) * 32) % 128
            rows = rows if shift == 0 else pltpu.roll(rows, shift, 1)
            term = rows if term is None else jnp.where(group == q, rows, term)
        z = term if z is None else z + term
    pre[...] = z
    grad = cotp[...] * silu_grad(z)
    grad = grad.astype(BF16).astype(F32)
    gp[...] = grad

    for side in range(2):
        row = 3 - 3 * side
        ysend[side] = grad.reshape(8, 32, 128)[:, row * 8 : row * 8 + 8].reshape(64, 128).astype(BF16)
        zsend[side] = gp[pl.ds(7 - 7 * side, 32, stride=8), :].astype(BF16)
        for other in range(2):
            corner = gp[pl.ds(row * 8 + 7 - 7 * other, 8, stride=32), :]
            csend[side * 2 + other] = jnp.concatenate([corner, corner], axis=0).astype(BF16)
    rim = []

    def rim_copy(src, dst, number, dy, dz):
        c = pltpu.make_async_remote_copy(
            src_ref=src,
            dst_ref=dst,
            send_sem=s3.at[number],
            recv_sem=r3.at[number],
            device_id=device(0, dy, dz),
            device_id_type=MESH,
        )
        c.start()
        rim.append(c)

    for side in range(2):
        rim_copy(ysend.at[side], yrecv.at[side], side, 1 - 2 * side, 0)
    for side in range(2):
        rim_copy(zsend.at[side], zrecv.at[side], 2 + side, 0, 1 - 2 * side)
    for corner in range(4):
        rim_copy(
            csend.at[corner],
            crecv.at[corner],
            4 + corner,
            1 - 2 * (corner // 2),
            1 - 2 * (corner % 2),
        )

    turned = jnp.transpose(grad)
    turned = [turned[32 * q : 32 * q + 32] for q in range(4)] + [jnp.zeros((32, 128), F32)]
    turned = jnp.concatenate(turned, axis=1)
    turned = [turned, pltpu.roll(turned, 32, 1), pltpu.roll(turned, 64, 1)]
    gt[...] = jnp.concatenate(turned, axis=0).astype(BF16)
    for n in range(3):
        columns_n = a3[:, :, n * 384 : n * 384 + 384].reshape(1152, 384)
        gball[:, n * 384 : n * 384 + 384] = dot(gt[...], columns_n) * scale

    def gball_tile(tile):
        row, lane = (tile // 9) * 32, (tile % 9) * 128
        return gball[row : row + 32, lane : lane + 128]

    for k in range(ny * nz):
        cut = piece(gball_tile, 108 * k, 108)
        gbs[k % nz, k // nz] = cut.astype(BF16)
    me = gy * nz + gz
    gb_copies = []
    for k in range(1, nz):
        target = lax.rem(gz + k, nz)
        gb_copies.append(
            pltpu.make_async_remote_copy(
                src_ref=gbs.at[target],
                dst_ref=gbr.at[gz],
                send_sem=s6.at[k],
                recv_sem=r6.at[k],
                device_id=(gx, gy, target),
                device_id_type=MESH,
            )
        )

    gpad[1:9, 1:5, 1:9, :] = gp[...].reshape(8, 4, 8, 128)
    for c in rim:
        c.wait()
    for c in gb_copies:
        c.start()

    def kept(flag, value):
        return jnp.where(flag, value.astype(F32), 0.0)

    y_ok = (gy > 0, gy < ny - 1)
    z_ok = (gz > 0, gz < nz - 1)
    for side in range(2):
        gpad[1:9, 5 * side, 1:9, :] = kept(y_ok[side], yrecv[side]).reshape(8, 8, 128)
        value = kept(z_ok[side], zrecv[side])
        gpad[1:9, 1:5, 9 * side : 9 * side + 1, :] = value.reshape(8, 4, 1, 128)
        for other in range(2):
            value = kept(y_ok[side] & z_ok[other], crecv[side * 2 + other])
            gpad[1:9, 5 * side, 9 * other : 9 * other + 1, :] = value[0:8].reshape(8, 1, 128)
    edge = lane_iota((96, 128))
    low = pltpu.roll(gpad[8].reshape(96, 128), 32, 1)
    gpad[0] = jnp.where(edge < 32, 0.0, low).reshape(6, 16, 128)
    high = pltpu.roll(gpad[1].reshape(96, 128), 96, 1)
    gpad[9] = jnp.where(edge >= 96, 0.0, high).reshape(6, 16, 128)
    gpadr[...] = pltpu.roll(gpad[...].reshape(960, 128), 64, 1).reshape(10, 6, 16, 128)

    def grad_window(ref, t):
        ax, ay, az = tap_of(t)
        window = ref[2 - ax : 10 - ax, 2 - ay : 6 - ay, 2 - az : 10 - az, :]
        return window.reshape(256, 128)

    half_rows = lane_iota((256, 128)) < 64
    for t in range(14):
        for pair, (one, two) in enumerate([(gpad, gpadr), (gpadr, gpad)]):
            window = jnp.where(half_rows, grad_window(one, 2 * t), grad_window(two, 2 * t + 1))
            ag[pair, :, t * 128 : t * 128 + 128] = window.astype(BF16)
    def act_copy(slot, target, source):
        return pltpu.make_async_remote_copy(
            src_ref=acts.at[target],
            dst_ref=actr.at[slot],
            send_sem=s4.at[target],
            recv_sem=r4.at[source],
            device_id=(target, gy, gz),
            device_id_type=MESH,
        )

    for pair in range(2):
        act = dot(ag[pair], wblk[...]).astype(BF16)
        for part in range(4):
            target = 4 * pair + part
            row, lane = (part % 2) * 128, (part // 2) * 128
            acts[target] = act[row : row + 128, lane : lane + 128]

            @pl.when(gx != target)
            def _(target=target):
                act_copy(gx, target, gx).start()

    out = silu(pre[...]).astype(BF16).astype(F32).reshape(8, 4, 8, 128)
    for y in range(4):
        turned = jnp.transpose(jnp.concatenate([out[:, y].reshape(64, 128), jnp.zeros((64, 128), F32)], axis=0))
        for q in range(4):
            tt[y * 32 : y * 32 + 32, q * 128 : q * 128 + 128] = turned[q * 32 : q * 32 + 32].astype(BF16)
    row = lax.broadcasted_iota(jnp.int32, (512, 128), 0)
    x_of = (row // 128) * 8 + (row % 128) // 8
    x_of = jnp.where(row % 128 < 64, x_of, -1)
    for k in range(8):
        select = jnp.where((x_of == lane_iota((512, 128))) & (row % 8 == k), 1.0, 0.0).astype(BF16)
        turned = dot(tt[...], select)
        for y in range(4):
            bo[pl.ds(y * 8 + k, 32, stride=32), :] = turned[y * 32 : y * 32 + 32]
    bottle_o[...] = bo[...].reshape(32, 4, 8, 128)[:, :, :, 0:32].astype(BF16)

    slope = [silu_grad(pd[x, y + 1, 1:9, :]) for x in range(4) for y in range(4)]
    slope = jnp.concatenate(slope, axis=0)
    total = acts[gx].astype(F32)
    for k in range(1, nx):
        source = lax.rem(gx - k + nx, nx)
        act_copy(source, lax.rem(gx + k, nx), source).wait()
        total = total + actr[source].astype(F32)
    grad_down = (total * slope).astype(BF16).astype(F32)
    grad_down_t = jnp.transpose(grad_down).astype(BF16)

    part = dot(grad_down_t, ad[...]) * scale
    downs[...] = part.reshape(nx, 16, 1792).astype(BF16)
    down_copies = []
    for k in range(1, nx):
        target = lax.rem(gx + k, nx)
        down_copies.append(
            pltpu.make_async_remote_copy(
                src_ref=downs.at[target],
                dst_ref=downr.at[gx],
                send_sem=s5.at[k],
                recv_sem=r5.at[k],
                device_id=(target, gy, gz),
                device_id_type=MESH,
            )
        )
    for c in down_copies:
        c.start()

    total = gbs[gz].astype(F32)
    for k, c in enumerate(gb_copies, 1):
        c.wait()
        total = total + gbr[lax.rem(gz - k + nz, nz)].astype(F32)
    gb2s[...] = total.astype(BF16)
    gb2_copies = []
    for k in range(1, ny):
        target = lax.rem(gy + k, ny)
        c = pltpu.make_async_remote_copy(
            src_ref=gb2s.at[target],
            dst_ref=gb2r.at[gy],
            send_sem=s8.at[k],
            recv_sem=r8.at[k],
            device_id=(gx, target, gz),
            device_id_type=MESH,
        )
        c.start()
        gb2_copies.append(c)

    dsum[...] = downs[gx].astype(F32)
    for k, c in enumerate(down_copies, 1):
        c.wait()
        dsum[...] += downr[lax.rem(gx - k + nx, nx)].astype(F32)
    low_half = lane_iota((8, 128)) < 64
    for k in range(ny * nz):
        cut = piece(lambda tile: dsum[:, tile * 128 : tile * 128 + 128], 54 * k, 54)
        cut = jnp.where(low_half, cut[0:8], pltpu.roll(cut[8:16], 64, 1))
        gds[k] = cut.astype(BF16)
    gd_copies = []
    planes.sort(key=lambda p: -2 * min(p[1], ny - p[1]) - min(p[2], nz - p[2]))
    for k, (_, dy, dz) in enumerate(planes):
        ty, tz = lax.rem(gy + dy, ny), lax.rem(gz + dz, nz)
        c = pltpu.make_async_remote_copy(
            src_ref=gds.at[ty * nz + tz],
            dst_ref=gdr.at[me],
            send_sem=s7.at[k],
            recv_sem=r7.at[k],
            device_id=(gx, ty, tz),
            device_id_type=MESH,
        )
        c.start()
        gd_copies.append(c)
    total = gb2s[gy].astype(F32)
    for k, c in enumerate(gb2_copies, 1):
        c.wait()
        total = total + gb2r[lax.rem(gy - k + ny, ny)].astype(F32)
    gbot_o[...] = total[:, 0:108]
    total = gds[me].astype(F32)
    for c in gd_copies:
        c.wait()
    for k, (_, dy, dz) in enumerate(planes):
        source = lax.rem(gy - dy + ny, ny) * nz + lax.rem(gz - dz + nz, nz)
        total = total + gdr[source].astype(F32)
    gdown_o[0:8, :] = total[:, 0:54]
    gdown_o[8:16, :] = pltpu.roll(total, 64, 1)[:, 0:54]


def per_device(sizes, fields, grain_ids, table, w_in, k_fine, k_down, k_bot, cotangent):
    nx, ny, nz = sizes
    n = ny * nz
    cot = cotangent.transpose(0, 2, 3, 1)
    vmem = pl.BlockSpec(memory_space=pltpu.VMEM)
    V = pltpu.VMEM
    D = pltpu.SemaphoreType.DMA
    scratch = [
        V((7, 8, 8, 16), BF16),
        V((8, 8, 16), jnp.int32),
        V((64, 128), BF16),
        V((7, 64), BF16),
        V((64, 1728), BF16),
        V((32, 4, 8, 32), BF16),
        V((1024, 128), F32),
        V((256, 128), F32),
        V((128, 512), BF16),
        V((1024, 128), F32),
        V((64, 128), F32),
        V((8, 2, 4, 1, 128), F32),
        V((11, 4, 8, 1, 128), F32),
        V((11, 16, 32, 128), F32),
        V((312, 640), BF16),
        V((11, 312, 256), F32),
        V((9, 13, 40, 128), F32),
        V((13, 24, 128), F32),
        V((256, 640), BF16),
        V((1792, 128), BF16),
        V((128, 1152), BF16),
        V((1792, 256), BF16),
        V((96, 1792), BF16),
        V((128, 1792), BF16),
        V((4, 6, 16, 128), F32),
        V((4, 64, 128), F32),
        V((4, 64, 128), BF16),
        V((nx, 4, 64, 128), BF16),
        V((4 * nx + 4, 64, 128), F32),
        V((36, 32, 1152), BF16),
        V((36, 32, 128), F32),
        V((256, 128), F32),
        V((256, 128), F32),
        V((96, 1152), BF16),
        V((2, 64, 128), BF16),
        V((2, 32, 128), BF16),
        V((4, 16, 128), BF16),
        V((2, 64, 128), BF16),
        V((2, 32, 128), BF16),
        V((4, 16, 128), BF16),
        V((10, 6, 16, 128), F32),
        V((10, 6, 16, 128), F32),
        V((2, 256, 1792), BF16),
        V((nx, 128, 128), BF16),
        V((nx, 128, 128), BF16),
        V((nx, 16, 1792), BF16),
        V((nx, 16, 1792), BF16),
        V((16, 1792), F32),
        V((96, 1152), F32),
        V((nz, ny, 32, 128), BF16),
        V((nz, ny, 32, 128), BF16),
        V((ny, 32, 128), BF16),
        V((ny, 32, 128), BF16),
        V((n, 8, 128), BF16),
        V((n, 8, 128), BF16),
        D((12,)),
        D((26,)),
        D((26,)),
        D((4, nx)),
        D((4, nx)),
        D((8,)),
        D((8,)),
        D((nx,)),
        D((nx,)),
        D((nx,)),
        D((nx,)),
        D((nz,)),
        D((nz,)),
        D((n,)),
        D((n,)),
        D((ny,)),
        D((ny,)),
    ]
    bottle, grad_down, grad_bottle = pl.pallas_call(
        functools.partial(body, sizes),
        out_shape=(
            jax.ShapeDtypeStruct((32, 4, 8, 32), BF16),
            jax.ShapeDtypeStruct((16, 54), F32),
            jax.ShapeDtypeStruct((32, 108), F32),
        ),
        in_specs=[pl.BlockSpec(memory_space=pl.ANY)] * 8,
        out_specs=(vmem, vmem, vmem),
        scratch_shapes=scratch,
        compiler_params=pltpu.CompilerParams(
            collective_id=0, has_side_effects=True, vmem_limit_bytes=60 * 1024 * 1024
        ),
    )(fields, grain_ids, table.T, w_in.T, k_fine, k_down.T, k_bot, cot)
    return bottle.transpose(0, 3, 1, 2), grad_down, grad_bottle


def solution(mesh):
    sizes = (mesh.shape["gx"], mesh.shape["gy"], mesh.shape["gz"])
    placed = (
        P(None, "gx", "gy", "gz"),
        P("gx", "gy", "gz"),
        P(),
        P(),
        P(),
        P(),
        P("gx", None),
        P("gx", None, "gy", "gz"),
    )
    return jax.shard_map(
        functools.partial(per_device, sizes),
        mesh=mesh,
        in_specs=placed,
        out_specs=(P("gx", None, "gy", "gz"), P("gx", ("gy", "gz")), P("gx", ("gy", "gz"))),
        check_vma=False,
    )
```

```python
import functools
import math

import jax
import jax.numpy as jnp
from jax import lax
from jax.experimental import pallas as pl
from jax.experimental.pallas import tpu as pltpu
from jax.sharding import PartitionSpec as P

MESH = pl.DeviceIdType.MESH
F32 = jnp.float32
BF16 = jnp.bfloat16
NT = (((1,), (1,)), ((), ()))


def silu(v):
    return v * jax.nn.sigmoid(v)


def silu_grad(v):
    s = jax.nn.sigmoid(v)
    return s * (1.0 + v * (1.0 - s))


def dot(a, b):
    return jnp.dot(a, b, preferred_element_type=F32)


def dot_nt(a, b):
    return lax.dot_general(a, b, NT, preferred_element_type=F32)


def tap_of(t):
    t = min(t, 26)
    return t // 9, (t // 3) % 3, t % 3


def lane_iota(shape):
    return lax.broadcasted_iota(jnp.int32, shape, len(shape) - 1)


def piece(ref_tiles, start, width):
    tile, shift = start // 128, start % 128
    low = ref_tiles(tile)
    if shift == 0:
        return low
    low = pltpu.roll(low, 128 - shift, 1)
    if shift + width <= 128:
        return low
    high = pltpu.roll(ref_tiles(tile + 1), 128 - shift, 1)
    return jnp.where(lane_iota(low.shape) < 128 - shift, low, high)


def body(
    sizes,
    fields_h,
    ids_h,
    table_h,
    w_in_h,
    k_fine_h,
    k_down_h,
    k_bot_h,
    cot_h,
    bottle_o,
    gdown_o,
    gbot_o,
    fields,
    ids,
    table,
    w_in,
    k_fine,
    cot,
    cotf,
    cotp,
    tt,
    bo,
    raw,
    brick,
    ext,
    es,
    af,
    yf,
    fs,
    fmask,
    kf,
    kd,
    kb,
    wblk,
    ac,
    ad,
    pd,
    cb,
    cs,
    sb,
    slab,
    a3,
    ysum,
    pre,
    gp,
    gt,
    ysend,
    zsend,
    csend,
    yrecv,
    zrecv,
    crecv,
    gpad,
    gpadr,
    ag,
    acts,
    actr,
    downs,
    downr,
    dsum,
    gball,
    gbs,
    gbr,
    gb2s,
    gb2r,
    gds,
    gdr,
    sem_l,
    s1,
    r1,
    s2,
    r2,
    s3,
    r3,
    s4,
    r4,
    s5,
    r5,
    s6,
    r6,
    s7,
    r7,
    s8,
    r8,
):
    nx, ny, nz = sizes
    gx, gy, gz = lax.axis_index("gx"), lax.axis_index("gy"), lax.axis_index("gz")
    scale = 1.0 / math.sqrt(nx * 4 * ny * 4 * nz * 8)

    def device(dx, dy, dz):
        return (lax.rem(gx + dx + nx, nx), lax.rem(gy + dy + ny, ny), lax.rem(gz + dz + nz, nz))

    near = [(dx, dy, dz) for dx in (-1, 0, 1) for dy in (-1, 0, 1) for dz in (-1, 0, 1)]
    near = [n for n in near if n != (0, 0, 0)]
    columns = [(dx, 0, 0) for dx in range(1, nx)]
    planes = [(0, dy, dz) for dy in range(ny) for dz in range(nz) if (dy, dz) != (0, 0)]
    partners = sorted({(a % nx, b % ny, c % nz) for a, b, c in near + columns + planes})
    partners.sort(key=lambda p: -2 * min(p[1], ny - p[1]) - min(p[2], nz - p[2]) - min(p[0], nx - p[0]))
    barrier = pltpu.get_barrier_semaphore()
    for p in partners:
        pl.semaphore_signal(barrier, inc=1, device_id=device(*p), device_id_type=MESH)

    loads = [
        pltpu.make_async_copy(src, dst, sem_l.at[1 + i])
        for i, (src, dst) in enumerate(
            [(fields_h, fields), (ids_h, ids), (table_h, table), (w_in_h, w_in), (k_fine_h, k_fine)]
            + [(k_down_h, kd.at[0:1728]), (cot_h, cot)]
            + [
                (k_bot_h.at[:, x * 1152 : x * 1152 + 1152], kb.at[32 * x : 32 * x + 32])
                for x in range(3)
            ]
        )
    ]
    for c in loads:
        c.start()
    kd[1728:1792, :] = jnp.zeros((64, 128), BF16)
    kb[96:128, :] = jnp.zeros((32, 1152), BF16)
    kf[...] = jnp.zeros(kf.shape, BF16)
    wblk[...] = jnp.zeros(wblk.shape, BF16)
    fs[...] = jnp.zeros(fs.shape, F32)
    gpad[...] = jnp.zeros(gpad.shape, F32)
    a3[0] = jnp.zeros((32, 1152), BF16)
    a3[4 * nx + 1 : 4 * nx + 4] = jnp.zeros((3, 32, 1152), BF16)
    ysum[0] = jnp.zeros((32, 128), F32)
    ysum[4 * nx + 1] = jnp.zeros((32, 128), F32)
    cb[...] = jnp.zeros(cb.shape, F32)
    cotf[...] = jnp.zeros(cotf.shape, F32)
    ext[:, :, 6:8] = jnp.zeros((11, 4, 2, 1, 128), F32)
    for c in loads[0:2]:
        c.wait()

    sel_row = lax.broadcasted_iota(jnp.int32, (16, 128), 0)
    sel_lane = lax.broadcasted_iota(jnp.int32, (16, 128), 1)
    packed = jnp.zeros((64, 128), F32)
    for ch in range(8):
        plane = (fields[ch] if ch < 7 else ids[...]).astype(F32).reshape(64, 16).astype(BF16)
        select = jnp.where(sel_lane == sel_row * 8 + ch, 1.0, 0.0).astype(BF16)
        packed = packed + dot(plane, select)
    raw[...] = packed
    group = lane_iota((16, 128)) // 32
    for zb in range(4):
        block = None
        for y4 in range(4):
            rows = raw[pl.ds(y4, 16, stride=4), :]
            shift = ((y4 - zb) * 32) % 128
            rows = rows if shift == 0 else pltpu.roll(rows, shift, 1)
            block = rows if block is None else jnp.where(group == y4, rows, block)
        for r in range(16):
            brick[r // 2, r % 2, zb, :, :] = block[r : r + 1, :]

    for c in loads[2:]:
        c.wait()
    lane = lane_iota((64, 640))
    first = jnp.where(lane < 576, k_fine[:, 0:640].astype(F32), 0.0)
    second = pltpu.roll(k_fine[:, 512:1152].astype(F32), 576, 1)
    kf[0:64, :] = first.astype(BF16)
    kf[64:128, :] = jnp.where(lane < 576, second, 0.0).astype(BF16)
    for n in (128, 192):
        kf[n : n + 64, 0:576] = k_fine[:, 1152:1728]
    for t in range(27):
        for q in range(2):
            row = t * 64 + q * 32
            wblk[row : row + 32, q * 128 : q * 128 + 128] = kb[
                (t // 9) * 32 : (t // 9) * 32 + 32, (t % 9) * 128 : (t % 9) * 128 + 128
            ]
    my = gy * 8 - 3 + lax.broadcasted_iota(jnp.int32, (13, 24, 128), 0)
    mz = gz * 16 - 3 + lax.broadcasted_iota(jnp.int32, (13, 24, 128), 1)
    inside = (my >= 0) & (my < ny * 8) & (mz >= 0) & (mz < nz * 16)
    fmask[...] = jnp.where(inside, 1.0, 0.0)

    pl.semaphore_wait(barrier, len(partners))

    x_src = {1: (6, 2, 0), 0: (0, 8, 2), -1: (0, 1, 10)}
    y_src = {1: (1, 1, 0), 0: (0, 2, 1), -1: (0, 1, 3)}
    z_src = {1: (3, 1, 0), 0: (0, 4, 1), -1: (0, 1, 5)}
    halo = []
    for number, (dx, dy, dz) in enumerate(near):
        (xs, xn, xd), (ys, yn, yd), (zs, zn, zd) = x_src[dx], y_src[dy], z_src[dz]
        halo.append(
            pltpu.make_async_remote_copy(
                src_ref=brick.at[xs : xs + xn, ys : ys + yn, zs : zs + zn],
                dst_ref=ext.at[xd : xd + xn, yd : yd + yn, zd : zd + zn],
                send_sem=s1.at[number],
                recv_sem=r1.at[number],
                device_id=device(dx, dy, dz),
                device_id_type=MESH,
            )
        )
    for c in halo:
        c.start()
    own = pltpu.make_async_copy(brick, ext.at[2:10, 1:3, 1:5], sem_l.at[0])
    own.start()

    row8 = lax.broadcasted_iota(jnp.int32, (128, 7), 0) % 8
    pick = jnp.where(row8 == lax.broadcasted_iota(jnp.int32, (128, 7), 1), 1.0, 0.0).astype(BF16)
    emb_lane = lane_iota((128, 128)) // 8
    twice = jnp.where(
        lax.broadcasted_iota(jnp.int32, (64, 128), 1) % 64
        == lax.broadcasted_iota(jnp.int32, (64, 128), 0),
        1.0,
        0.0,
    ).astype(BF16)
    w_rows = dot(pick, dot(w_in[...], twice).astype(BF16))
    table2 = jnp.concatenate([table[...]] * 2, axis=0)
    w_cols = jnp.transpose(w_rows)

    own.wait()
    for c, n in zip(halo, near):
        if n[0] == 0:
            c.wait()

    by = lax.broadcasted_iota(jnp.int32, (4, 8, 128), 0)
    bz = lax.broadcasted_iota(jnp.int32, (4, 8, 128), 1)
    outside = ((by == 0) & (gy == 0)) | ((by == 3) & (gy == ny - 1))
    outside = outside | ((bz == 0) & (gz == 0)) | ((bz == 5) & (gz == nz - 1))
    fill = jnp.where(lane_iota((4, 8, 128)) % 8 == 7, -1.0, 0.0)

    def embed(planes_x):
        rows = len(planes_x) * 32
        blocks = []
        for x in planes_x:
            block = jnp.where(outside, fill, ext[x].reshape(4, 8, 128))
            if x < 2:
                block = jnp.where(gx == 0, fill, block)
            if x == 10:
                block = jnp.where(gx == nx - 1, fill, block)
            blocks.append(block)
        blocks = jnp.concatenate(blocks, axis=0).reshape(rows, 128)
        components = blocks.astype(BF16)
        lanes = lane_iota((rows, 128)).astype(F32)
        for p in range(16):
            y4, z4 = p // 4, p % 4
            w_p = jnp.where(emb_lane == p, w_cols, 0.0).astype(BF16)
            grain = jnp.broadcast_to(blocks[:, p * 8 + 7 : p * 8 + 8], (rows, 128))
            onehot = jnp.where(grain == lanes, 1.0, 0.0).astype(BF16)
            both = jnp.concatenate([onehot, components], axis=1)
            value = silu(dot_nt(both, jnp.concatenate([table2, w_p], axis=1)))
            value = value.reshape(len(planes_x), 4, 8, 128)
            for i, x in enumerate(planes_x):
                for yb in range(4):
                    es[x, yb * 4 + y4, pl.ds(z4, 8, stride=4), :] = value[i, yb]

    half = lane_iota((13, 24, 128)) < 64

    def spread_plane(e):
        for t in range(5):
            ay, az = (2 * t) // 3, (2 * t) % 3
            by_, bz_ = min(2 * t + 1, 8) // 3, min(2 * t + 1, 8) % 3
            low = es[e, ay : ay + 13, az : az + 24, :]
            high = es[e, by_ : by_ + 13, bz_ : bz_ + 24, :]
            block = jnp.where(half, low, high)
            af[:, t * 128 : t * 128 + 128] = block.reshape(312, 128).astype(BF16)
        yf[e] = dot_nt(af[...], kf[...])

    half_rows = lane_iota((312, 128)) < 64

    def next_plane(x, carry):
        spread_plane(x + 2)
        fine_plane(x)
        return carry

    def fine_plane(x):
        two = jnp.where(half_rows, yf[x, :, 0:128], yf[x + 1, :, 0:128])
        value = two + pltpu.roll(two, 64, 1) + yf[x + 2, :, 128:256]
        value = silu(value).reshape(13, 24, 128)
        keep = jnp.where((x > 0) | (gx > 0), 1.0, 0.0)
        value = value * fmask[...] * keep
        fs[x, :, 0:24, :] = value.astype(BF16).astype(F32)

    def coarse_copy(x, k):
        return pltpu.make_async_remote_copy(
            src_ref=cs.at[x],
            dst_ref=sb.at[gx, x],
            send_sem=s2.at[x, k],
            recv_sem=r2.at[x, k],
            device_id=device(k, 0, 0),
            device_id_type=MESH,
        )

    half16 = lane_iota((16, 128)) < 64
    cy = gy * 4 - 1 + lax.broadcasted_iota(jnp.int32, (6, 16, 128), 0)
    cz = gz * 8 - 1 + lax.broadcasted_iota(jnp.int32, (6, 16, 128), 1)
    inside = (cy >= 0) & (cy < ny * 4) & (cz >= 0) & (cz < nz * 8)

    def coarse_plane(x, carry):
        lax.fori_loop(2 * x + 1, 2 * x + 3, next_plane, 0)
        for y in range(6):
            row = y * 16
            for t in range(14):
                (ax, ay, az), (bx_, by_, bz_) = tap_of(2 * t), tap_of(2 * t + 1)
                low = fs[2 * x + ax, 2 * y + ay, pl.ds(az, 16, stride=2), :]
                high = fs[2 * x + bx_, 2 * y + by_, pl.ds(bz_, 16, stride=2), :]
                ac[row : row + 16, t * 128 : t * 128 + 128] = jnp.where(half16, low, high).astype(BF16)
        before = dot(ac[...], kd[...]).reshape(6, 16, 128)
        pd[x] = before
        coarse = jnp.where(inside, silu(before), 0.0)
        for y in range(6):
            cb[x, y * 10 : y * 10 + 10, :] = coarse[y, 0:10, :]
        cs[x] = cb[x].astype(BF16)
        sb[gx, x] = cb[x].astype(BF16)
        for k in range(1, nx):
            coarse_copy(x, k).start()
        return carry

    embed(range(2, 10))
    spread_plane(2)
    for c, n in zip(halo, near):
        if n[0] != 0:
            c.wait()
    embed((0, 1, 10))

    def first_planes(e, carry):
        spread_plane(e)
        return carry

    lax.fori_loop(0, 2, first_planes, 0)
    fine_plane(0)
    lax.fori_loop(0, 4, coarse_plane, 0)

    half8 = lane_iota((8, 128)) < 64
    for x in range(4):
        for t in range(14):
            (ax, ay, az), (bx_, by_, bz_) = tap_of(2 * t), tap_of(2 * t + 1)
            parts = []
            for y in range(4):
                low = fs[2 * x + ax, 2 * y + 2 + ay, pl.ds(2 + az, 8, stride=2), :]
                high = fs[2 * x + bx_, 2 * y + 2 + by_, pl.ds(2 + bz_, 8, stride=2), :]
                parts.append(jnp.where(half8, low, high))
            ad[x * 32 : x * 32 + 32, t * 128 : t * 128 + 128] = jnp.concatenate(parts, axis=0).astype(BF16)


    cotf[:, 0:32] = cot[...].astype(F32).reshape(1024, 32)
    group = lane_iota((32, 128)) // 8
    spread = lax.broadcasted_iota(jnp.int32, (8, 128), 0)
    spread = jnp.where(lane_iota((8, 128)) % 8 == spread, 1.0, 0.0).astype(BF16)
    for y in range(4):
        for z in range(8):
            rows = cotf[pl.ds(y * 8 + z, 32, stride=32), :]
            rows = jnp.concatenate([jnp.where(group == q, rows, 0.0) for q in range(4)], axis=0)
            cotp[pl.ds(y * 8 + z, 8, stride=32), :] = dot_nt(spread, rows.astype(BF16))

    def bottle_plane(x, carry):
        for k in range(1, nx):
            coarse_copy(x, k).wait()
        slab[...] = sb[:, x].astype(F32)
        for pair in range(2):
            for t in range(9):
                start = (2 * pair + t // 3) * 10 + t % 3
                window = [slab[:, start : start + 8, :], slab[:, start + 10 : start + 18, :]]
                window = jnp.concatenate(window, axis=1).astype(BF16)
                for n in range(nx):
                    a3[1 + 4 * n + x, pair * 16 : pair * 16 + 16, t * 128 : t * 128 + 128] = window[n]
        part = jnp.concatenate([a3[1 + 4 * n + x] for n in range(nx)], axis=0)
        part = dot_nt(part, kb[...]).reshape(nx, 32, 128)
        for n in range(nx):
            ysum[1 + 4 * n + x] = part[n]
        return carry

    lax.fori_loop(0, 4, bottle_plane, 0)
    group = lane_iota((256, 128)) // 32
    z = None
    for ax in range(3):
        term = None
        for q in range(4):
            rows = ysum[8 * q + ax : 8 * q + ax + 8].reshape(256, 128)
            shift = ((q - ax) * 32) % 128
            rows = rows if shift == 0 else pltpu.roll(rows, shift, 1)
            term = rows if term is None else jnp.where(group == q, rows, term)
        z = term if z is None else z + term
    pre[...] = z
    grad = cotp[...] * silu_grad(z)
    grad = grad.astype(BF16).astype(F32)
    gp[...] = grad

    for side in range(2):
        row = 3 - 3 * side
        ysend[side] = grad.reshape(8, 32, 128)[:, row * 8 : row * 8 + 8].reshape(64, 128).astype(BF16)
        zsend[side] = gp[pl.ds(7 - 7 * side, 32, stride=8), :].astype(BF16)
        for other in range(2):
            corner = gp[pl.ds(row * 8 + 7 - 7 * other, 8, stride=32), :]
            csend[side * 2 + other] = jnp.concatenate([corner, corner], axis=0).astype(BF16)
    rim = []

    def rim_copy(src, dst, number, dy, dz):
        c = pltpu.make_async_remote_copy(
            src_ref=src,
            dst_ref=dst,
            send_sem=s3.at[number],
            recv_sem=r3.at[number],
            device_id=device(0, dy, dz),
            device_id_type=MESH,
        )
        c.start()
        rim.append(c)

    for side in range(2):
        rim_copy(ysend.at[side], yrecv.at[side], side, 1 - 2 * side, 0)
    for side in range(2):
        rim_copy(zsend.at[side], zrecv.at[side], 2 + side, 0, 1 - 2 * side)
    for corner in range(4):
        rim_copy(
            csend.at[corner],
            crecv.at[corner],
            4 + corner,
            1 - 2 * (corner // 2),
            1 - 2 * (corner % 2),
        )

    turned = jnp.transpose(grad)
    turned = [turned[32 * q : 32 * q + 32] for q in range(4)] + [jnp.zeros((32, 128), F32)]
    turned = jnp.concatenate(turned, axis=1)
    turned = [turned, pltpu.roll(turned, 32, 1), pltpu.roll(turned, 64, 1)]
    gt[...] = jnp.concatenate(turned, axis=0).astype(BF16)
    for n in range(3):
        columns_n = a3[:, :, n * 384 : n * 384 + 384].reshape(1152, 384)
        gball[:, n * 384 : n * 384 + 384] = dot(gt[...], columns_n) * scale

    def gball_tile(tile):
        row, lane = (tile // 9) * 32, (tile % 9) * 128
        return gball[row : row + 32, lane : lane + 128]

    for k in range(ny * nz):
        cut = piece(gball_tile, 108 * k, 108)
        gbs[k % nz, k // nz] = cut.astype(BF16)
    me = gy * nz + gz
    gb_copies = []
    for k in range(1, nz):
        target = lax.rem(gz + k, nz)
        gb_copies.append(
            pltpu.make_async_remote_copy(
                src_ref=gbs.at[target],
                dst_ref=gbr.at[gz],
                send_sem=s6.at[k],
                recv_sem=r6.at[k],
                device_id=(gx, gy, target),
                device_id_type=MESH,
            )
        )

    gpad[1:9, 1:5, 1:9, :] = gp[...].reshape(8, 4, 8, 128)
    for c in rim:
        c.wait()
    for c in gb_copies:
        c.start()

    def kept(flag, value):
        return jnp.where(flag, value.astype(F32), 0.0)

    y_ok = (gy > 0, gy < ny - 1)
    z_ok = (gz > 0, gz < nz - 1)
    for side in range(2):
        gpad[1:9, 5 * side, 1:9, :] = kept(y_ok[side], yrecv[side]).reshape(8, 8, 128)
        value = kept(z_ok[side], zrecv[side])
        gpad[1:9, 1:5, 9 * side : 9 * side + 1, :] = value.reshape(8, 4, 1, 128)
        for other in range(2):
            value = kept(y_ok[side] & z_ok[other], crecv[side * 2 + other])
            gpad[1:9, 5 * side, 9 * other : 9 * other + 1, :] = value[0:8].reshape(8, 1, 128)
    edge = lane_iota((96, 128))
    low = pltpu.roll(gpad[8].reshape(96, 128), 32, 1)
    gpad[0] = jnp.where(edge < 32, 0.0, low).reshape(6, 16, 128)
    high = pltpu.roll(gpad[1].reshape(96, 128), 96, 1)
    gpad[9] = jnp.where(edge >= 96, 0.0, high).reshape(6, 16, 128)
    gpadr[...] = pltpu.roll(gpad[...].reshape(960, 128), 64, 1).reshape(10, 6, 16, 128)

    def grad_window(ref, t):
        ax, ay, az = tap_of(t)
        window = ref[2 - ax : 10 - ax, 2 - ay : 6 - ay, 2 - az : 10 - az, :]
        return window.reshape(256, 128)

    half_rows = lane_iota((256, 128)) < 64
    for t in range(14):
        for pair, (one, two) in enumerate([(gpad, gpadr), (gpadr, gpad)]):
            window = jnp.where(half_rows, grad_window(one, 2 * t), grad_window(two, 2 * t + 1))
            ag[pair, :, t * 128 : t * 128 + 128] = window.astype(BF16)
    def act_copy(slot, target, source):
        return pltpu.make_async_remote_copy(
            src_ref=acts.at[target],
            dst_ref=actr.at[slot],
            send_sem=s4.at[target],
            recv_sem=r4.at[source],
            device_id=(target, gy, gz),
            device_id_type=MESH,
        )

    for pair in range(2):
        act = dot(ag[pair], wblk[...]).astype(BF16)
        for part in range(4):
            target = 4 * pair + part
            row, lane = (part % 2) * 128, (part // 2) * 128
            acts[target] = act[row : row + 128, lane : lane + 128]

            @pl.when(gx != target)
            def _(target=target):
                act_copy(gx, target, gx).start()

    out = silu(pre[...]).astype(BF16).astype(F32).reshape(8, 4, 8, 128)
    for y in range(4):
        turned = jnp.transpose(jnp.concatenate([out[:, y].reshape(64, 128), jnp.zeros((64, 128), F32)], axis=0))
        for q in range(4):
            tt[y * 32 : y * 32 + 32, q * 128 : q * 128 + 128] = turned[q * 32 : q * 32 + 32].astype(BF16)
    row = lax.broadcasted_iota(jnp.int32, (512, 128), 0)
    x_of = (row // 128) * 8 + (row % 128) // 8
    x_of = jnp.where(row % 128 < 64, x_of, -1)
    for k in range(8):
        select = jnp.where((x_of == lane_iota((512, 128))) & (row % 8 == k), 1.0, 0.0).astype(BF16)
        turned = dot(tt[...], select)
        for y in range(4):
            bo[pl.ds(y * 8 + k, 32, stride=32), :] = turned[y * 32 : y * 32 + 32]
    bottle_o[...] = bo[...].reshape(32, 4, 8, 128)[:, :, :, 0:32].astype(BF16)

    slope = [silu_grad(pd[x, y + 1, 1:9, :]) for x in range(4) for y in range(4)]
    slope = jnp.concatenate(slope, axis=0)
    total = acts[gx].astype(F32)
    for k in range(1, nx):
        source = lax.rem(gx - k + nx, nx)
        act_copy(source, lax.rem(gx + k, nx), source).wait()
        total = total + actr[source].astype(F32)
    grad_down = (total * slope).astype(BF16).astype(F32)
    grad_down_t = jnp.transpose(grad_down).astype(BF16)

    part = dot(grad_down_t, ad[...]) * scale
    downs[...] = part.reshape(nx, 16, 1792).astype(BF16)
    down_copies = []
    for k in range(1, nx):
        target = lax.rem(gx + k, nx)
        down_copies.append(
            pltpu.make_async_remote_copy(
                src_ref=downs.at[target],
                dst_ref=downr.at[gx],
                send_sem=s5.at[k],
                recv_sem=r5.at[k],
                device_id=(target, gy, gz),
                device_id_type=MESH,
            )
        )
    for c in down_copies:
        c.start()

    total = gbs[gz].astype(F32)
    for k, c in enumerate(gb_copies, 1):
        c.wait()
        total = total + gbr[lax.rem(gz - k + nz, nz)].astype(F32)
    gb2s[...] = total.astype(BF16)
    gb2_copies = []
    for k in range(1, ny):
        target = lax.rem(gy + k, ny)
        c = pltpu.make_async_remote_copy(
            src_ref=gb2s.at[target],
            dst_ref=gb2r.at[gy],
            send_sem=s8.at[k],
            recv_sem=r8.at[k],
            device_id=(gx, target, gz),
            device_id_type=MESH,
        )
        c.start()
        gb2_copies.append(c)

    dsum[...] = downs[gx].astype(F32)
    for k, c in enumerate(down_copies, 1):
        c.wait()
        dsum[...] += downr[lax.rem(gx - k + nx, nx)].astype(F32)
    low_half = lane_iota((8, 128)) < 64
    for k in range(ny * nz):
        cut = piece(lambda tile: dsum[:, tile * 128 : tile * 128 + 128], 54 * k, 54)
        cut = jnp.where(low_half, cut[0:8], pltpu.roll(cut[8:16], 64, 1))
        gds[k] = cut.astype(BF16)
    gd_copies = []
    planes.sort(key=lambda p: -2 * min(p[1], ny - p[1]) - min(p[2], nz - p[2]))
    for k, (_, dy, dz) in enumerate(planes):
        ty, tz = lax.rem(gy + dy, ny), lax.rem(gz + dz, nz)
        c = pltpu.make_async_remote_copy(
            src_ref=gds.at[ty * nz + tz],
            dst_ref=gdr.at[me],
            send_sem=s7.at[k],
            recv_sem=r7.at[k],
            device_id=(gx, ty, tz),
            device_id_type=MESH,
        )
        c.start()
        gd_copies.append(c)
    total = gb2s[gy].astype(F32)
    for k, c in enumerate(gb2_copies, 1):
        c.wait()
        total = total + gb2r[lax.rem(gy - k + ny, ny)].astype(F32)
    gbot_o[...] = total[:, 0:108]
    total = gds[me].astype(F32)
    for c in gd_copies:
        c.wait()
    for k, (_, dy, dz) in enumerate(planes):
        source = lax.rem(gy - dy + ny, ny) * nz + lax.rem(gz - dz + nz, nz)
        total = total + gdr[source].astype(F32)
    gdown_o[0:8, :] = total[:, 0:54]
    gdown_o[8:16, :] = pltpu.roll(total, 64, 1)[:, 0:54]


def put_out(a, b, c, a_out, b_out, c_out, sems):
    copies = [
        pltpu.make_async_copy(source, out, sems.at[i])
        for i, (source, out) in enumerate([(a, a_out), (b, b_out), (c, c_out)])
    ]
    for copy in copies:
        copy.start()
    for copy in copies:
        copy.wait()


def per_device(sizes, fields, grain_ids, table, w_in, k_fine, k_down, k_bot, cotangent):
    nx, ny, nz = sizes
    n = ny * nz
    cot = cotangent.transpose(0, 2, 3, 1)
    vmem = pl.BlockSpec(memory_space=pltpu.VMEM)
    V = pltpu.VMEM
    D = pltpu.SemaphoreType.DMA
    scratch = [
        V((7, 8, 8, 16), BF16),
        V((8, 8, 16), jnp.int32),
        V((64, 128), BF16),
        V((7, 64), BF16),
        V((64, 1728), BF16),
        V((32, 4, 8, 32), BF16),
        V((1024, 128), F32),
        V((256, 128), F32),
        V((128, 512), BF16),
        V((1024, 128), F32),
        V((64, 128), F32),
        V((8, 2, 4, 1, 128), F32),
        V((11, 4, 8, 1, 128), F32),
        V((11, 16, 32, 128), F32),
        V((312, 640), BF16),
        V((11, 312, 256), F32),
        V((9, 13, 40, 128), F32),
        V((13, 24, 128), F32),
        V((256, 640), BF16),
        V((1792, 128), BF16),
        V((128, 1152), BF16),
        V((1792, 256), BF16),
        V((96, 1792), BF16),
        V((128, 1792), BF16),
        V((4, 6, 16, 128), F32),
        V((4, 64, 128), F32),
        V((4, 64, 128), BF16),
        V((nx, 4, 64, 128), BF16),
        V((nx, 64, 128), F32),
        V((36, 32, 1152), BF16),
        V((36, 32, 128), F32),
        V((256, 128), F32),
        V((256, 128), F32),
        V((96, 1152), BF16),
        V((2, 64, 128), BF16),
        V((2, 32, 128), BF16),
        V((4, 16, 128), BF16),
        V((2, 64, 128), BF16),
        V((2, 32, 128), BF16),
        V((4, 16, 128), BF16),
        V((10, 6, 16, 128), F32),
        V((10, 6, 16, 128), F32),
        V((2, 256, 1792), BF16),
        V((nx, 128, 128), BF16),
        V((nx, 128, 128), BF16),
        V((nx, 16, 1792), BF16),
        V((nx, 16, 1792), BF16),
        V((16, 1792), F32),
        V((96, 1152), F32),
        V((nz, ny, 32, 128), BF16),
        V((nz, ny, 32, 128), BF16),
        V((ny, 32, 128), BF16),
        V((ny, 32, 128), BF16),
        V((n, 8, 128), BF16),
        V((n, 8, 128), BF16),
        D((12,)),
        D((26,)),
        D((26,)),
        D((4, nx)),
        D((4, nx)),
        D((8,)),
        D((8,)),
        D((nx,)),
        D((nx,)),
        D((nx,)),
        D((nx,)),
        D((nz,)),
        D((nz,)),
        D((n,)),
        D((n,)),
        D((ny,)),
        D((ny,)),
    ]
    bottle, grad_down, grad_bottle = pl.pallas_call(
        functools.partial(body, sizes),
        out_shape=(
            V((32, 4, 8, 32), BF16),
            V((16, 54), F32),
            V((32, 108), F32),
        ),
        in_specs=[pl.BlockSpec(memory_space=pl.ANY)] * 8,
        out_specs=(vmem, vmem, vmem),
        scratch_shapes=scratch,
        compiler_params=pltpu.CompilerParams(
            collective_id=0, has_side_effects=True, vmem_limit_bytes=60 * 1024 * 1024
        ),
    )(fields, grain_ids, table.T, w_in.T, k_fine, k_down.T, k_bot, cot)
    bottle, grad_down, grad_bottle = pl.pallas_call(
        put_out,
        out_shape=(
            jax.ShapeDtypeStruct((32, 4, 8, 32), BF16),
            jax.ShapeDtypeStruct((16, 54), F32),
            jax.ShapeDtypeStruct((32, 108), F32),
        ),
        in_specs=[vmem] * 3,
        out_specs=[pl.BlockSpec(memory_space=pl.ANY)] * 3,
        scratch_shapes=[D((3,))],
        compiler_params=pltpu.CompilerParams(vmem_limit_bytes=1024 * 1024),
    )(bottle, grad_down, grad_bottle)
    return bottle.transpose(0, 3, 1, 2), grad_down, grad_bottle


def solution(mesh):
    sizes = (mesh.shape["gx"], mesh.shape["gy"], mesh.shape["gz"])
    placed = (
        P(None, "gx", "gy", "gz"),
        P("gx", "gy", "gz"),
        P(),
        P(),
        P(),
        P(),
        P("gx", None),
        P("gx", None, "gy", "gz"),
    )
    return jax.shard_map(
        functools.partial(per_device, sizes),
        mesh=mesh,
        in_specs=placed,
        out_specs=(P("gx", None, "gy", "gz"), P("gx", ("gy", "gz")), P("gx", ("gy", "gz"))),
        check_vma=False,
    )
```

```python
import functools
import math

import jax
import jax.numpy as jnp
from jax import lax
from jax.experimental import pallas as pl
from jax.experimental.pallas import tpu as pltpu
from jax.sharding import PartitionSpec as P

MESH = pl.DeviceIdType.MESH
F32 = jnp.float32
BF16 = jnp.bfloat16
NT = (((1,), (1,)), ((), ()))


def silu(v):
    return v * jax.nn.sigmoid(v)


def silu_grad(v):
    s = jax.nn.sigmoid(v)
    return s * (1.0 + v * (1.0 - s))


def dot(a, b):
    return jnp.dot(a, b, preferred_element_type=F32)


def dot_nt(a, b):
    return lax.dot_general(a, b, NT, preferred_element_type=F32)


def tap_of(t):
    t = min(t, 26)
    return t // 9, (t // 3) % 3, t % 3


def lane_iota(shape):
    return lax.broadcasted_iota(jnp.int32, shape, len(shape) - 1)


def piece(ref_tiles, start, width):
    tile, shift = start // 128, start % 128
    low = ref_tiles(tile)
    if shift == 0:
        return low
    low = pltpu.roll(low, 128 - shift, 1)
    if shift + width <= 128:
        return low
    high = pltpu.roll(ref_tiles(tile + 1), 128 - shift, 1)
    return jnp.where(lane_iota(low.shape) < 128 - shift, low, high)


def body(
    sizes,
    fields_h,
    ids_h,
    table_h,
    w_in_h,
    k_fine_h,
    k_down_h,
    k_bot_h,
    cot_h,
    bottle_o,
    gdown_o,
    gbot_o,
    fields,
    ids,
    table,
    w_in,
    k_fine,
    cot,
    cotf,
    cotp,
    tt,
    bo,
    raw,
    brick,
    ext,
    es,
    af,
    yf,
    fs,
    fmask,
    kf,
    kd,
    kb,
    wblk,
    ac,
    ad,
    pd,
    cb,
    cs,
    sb,
    slab,
    a3,
    ysum,
    pre,
    gp,
    gt,
    ysend,
    zsend,
    csend,
    yrecv,
    zrecv,
    crecv,
    gpad,
    gpadr,
    ag,
    acts,
    actr,
    downs,
    downr,
    dsum,
    dpart,
    bds,
    bdr,
    b2s,
    b2r,
    gball,
    gbs,
    gbr,
    gb2s,
    gb2r,
    gds,
    gdr,
    sem_l,
    s1,
    r1,
    s2,
    r2,
    s3,
    r3,
    s4,
    r4,
    s5,
    r5,
    s6,
    r6,
    s7,
    r7,
    s8,
    r8,
    s9,
    r9,
    s10,
    r10,
):
    nx, ny, nz = sizes
    gx, gy, gz = lax.axis_index("gx"), lax.axis_index("gy"), lax.axis_index("gz")
    scale = 1.0 / math.sqrt(nx * 4 * ny * 4 * nz * 8)

    def device(dx, dy, dz):
        return (lax.rem(gx + dx + nx, nx), lax.rem(gy + dy + ny, ny), lax.rem(gz + dz + nz, nz))

    near = [(dx, dy, dz) for dx in (-1, 0, 1) for dy in (-1, 0, 1) for dz in (-1, 0, 1)]
    near = [n for n in near if n != (0, 0, 0)]
    columns = [(dx, 0, 0) for dx in range(1, nx)]
    planes = [(0, dy, dz) for dy in range(ny) for dz in range(nz) if (dy, dz) != (0, 0)]
    sheets = [(dx, dy, 0) for dx in range(nx) for dy in range(ny) if (dx, dy) != (0, 0)]
    partners = sorted({(a % nx, b % ny, c % nz) for a, b, c in near + columns + planes + sheets})
    partners.sort(key=lambda p: -2 * min(p[1], ny - p[1]) - min(p[2], nz - p[2]) - min(p[0], nx - p[0]))
    barrier = pltpu.get_barrier_semaphore()
    for p in partners:
        pl.semaphore_signal(barrier, inc=1, device_id=device(*p), device_id_type=MESH)

    loads = [
        pltpu.make_async_copy(src, dst, sem_l.at[1 + i])
        for i, (src, dst) in enumerate(
            [(fields_h, fields), (ids_h, ids), (table_h, table), (w_in_h, w_in), (k_fine_h, k_fine)]
            + [(k_down_h, kd.at[0:1728]), (cot_h, cot)]
            + [
                (k_bot_h.at[:, x * 1152 : x * 1152 + 1152], kb.at[32 * x : 32 * x + 32])
                for x in range(3)
            ]
        )
    ]
    for c in loads:
        c.start()
    kd[1728:1792, :] = jnp.zeros((64, 128), BF16)
    kb[96:128, :] = jnp.zeros((32, 1152), BF16)
    kf[...] = jnp.zeros(kf.shape, BF16)
    wblk[...] = jnp.zeros(wblk.shape, BF16)
    fs[...] = jnp.zeros(fs.shape, F32)
    gpad[...] = jnp.zeros(gpad.shape, F32)
    a3[0] = jnp.zeros((32, 1152), BF16)
    a3[4 * nx + 1 : 4 * nx + 4] = jnp.zeros((3, 32, 1152), BF16)
    ysum[0] = jnp.zeros((32, 128), F32)
    ysum[4 * nx + 1] = jnp.zeros((32, 128), F32)
    cb[...] = jnp.zeros(cb.shape, F32)
    cotf[...] = jnp.zeros(cotf.shape, F32)
    ext[:, :, 6:8] = jnp.zeros((11, 4, 2, 1, 128), F32)
    for c in loads[0:2]:
        c.wait()

    sel_row = lax.broadcasted_iota(jnp.int32, (16, 128), 0)
    sel_lane = lax.broadcasted_iota(jnp.int32, (16, 128), 1)
    packed = jnp.zeros((64, 128), F32)
    for ch in range(8):
        plane = (fields[ch] if ch < 7 else ids[...]).astype(F32).reshape(64, 16).astype(BF16)
        select = jnp.where(sel_lane == sel_row * 8 + ch, 1.0, 0.0).astype(BF16)
        packed = packed + dot(plane, select)
    raw[...] = packed
    group = lane_iota((16, 128)) // 32
    for zb in range(4):
        block = None
        for y4 in range(4):
            rows = raw[pl.ds(y4, 16, stride=4), :]
            shift = ((y4 - zb) * 32) % 128
            rows = rows if shift == 0 else pltpu.roll(rows, shift, 1)
            block = rows if block is None else jnp.where(group == y4, rows, block)
        for r in range(16):
            brick[r // 2, r % 2, zb, :, :] = block[r : r + 1, :]

    for c in loads[2:]:
        c.wait()
    lane = lane_iota((64, 640))
    first = jnp.where(lane < 576, k_fine[:, 0:640].astype(F32), 0.0)
    second = pltpu.roll(k_fine[:, 512:1152].astype(F32), 576, 1)
    kf[0:64, :] = first.astype(BF16)
    kf[64:128, :] = jnp.where(lane < 576, second, 0.0).astype(BF16)
    for n in (128, 192):
        kf[n : n + 64, 0:576] = k_fine[:, 1152:1728]
    for t in range(27):
        for q in range(2):
            row = t * 64 + q * 32
            wblk[row : row + 32, q * 128 : q * 128 + 128] = kb[
                (t // 9) * 32 : (t // 9) * 32 + 32, (t % 9) * 128 : (t % 9) * 128 + 128
            ]
    my = gy * 8 - 3 + lax.broadcasted_iota(jnp.int32, (13, 24, 128), 0)
    mz = gz * 16 - 3 + lax.broadcasted_iota(jnp.int32, (13, 24, 128), 1)
    inside = (my >= 0) & (my < ny * 8) & (mz >= 0) & (mz < nz * 16)
    fmask[...] = jnp.where(inside, 1.0, 0.0)

    pl.semaphore_wait(barrier, len(partners))

    x_src = {1: (6, 2, 0), 0: (0, 8, 2), -1: (0, 1, 10)}
    y_src = {1: (1, 1, 0), 0: (0, 2, 1), -1: (0, 1, 3)}
    z_src = {1: (3, 1, 0), 0: (0, 4, 1), -1: (0, 1, 5)}
    halo = []
    for number, (dx, dy, dz) in enumerate(near):
        (xs, xn, xd), (ys, yn, yd), (zs, zn, zd) = x_src[dx], y_src[dy], z_src[dz]
        halo.append(
            pltpu.make_async_remote_copy(
                src_ref=brick.at[xs : xs + xn, ys : ys + yn, zs : zs + zn],
                dst_ref=ext.at[xd : xd + xn, yd : yd + yn, zd : zd + zn],
                send_sem=s1.at[number],
                recv_sem=r1.at[number],
                device_id=device(dx, dy, dz),
                device_id_type=MESH,
            )
        )
    for c in halo:
        c.start()
    own = pltpu.make_async_copy(brick, ext.at[2:10, 1:3, 1:5], sem_l.at[0])
    own.start()

    row8 = lax.broadcasted_iota(jnp.int32, (128, 7), 0) % 8
    pick = jnp.where(row8 == lax.broadcasted_iota(jnp.int32, (128, 7), 1), 1.0, 0.0).astype(BF16)
    emb_lane = lane_iota((128, 128)) // 8
    twice = jnp.where(
        lax.broadcasted_iota(jnp.int32, (64, 128), 1) % 64
        == lax.broadcasted_iota(jnp.int32, (64, 128), 0),
        1.0,
        0.0,
    ).astype(BF16)
    w_rows = dot(pick, dot(w_in[...], twice).astype(BF16))
    table2 = jnp.concatenate([table[...]] * 2, axis=0)
    w_cols = jnp.transpose(w_rows)

    own.wait()
    for c, n in zip(halo, near):
        if n[0] == 0:
            c.wait()

    by = lax.broadcasted_iota(jnp.int32, (4, 8, 128), 0)
    bz = lax.broadcasted_iota(jnp.int32, (4, 8, 128), 1)
    outside = ((by == 0) & (gy == 0)) | ((by == 3) & (gy == ny - 1))
    outside = outside | ((bz == 0) & (gz == 0)) | ((bz == 5) & (gz == nz - 1))
    fill = jnp.where(lane_iota((4, 8, 128)) % 8 == 7, -1.0, 0.0)

    def embed(planes_x):
        rows = len(planes_x) * 32
        blocks = []
        for x in planes_x:
            block = jnp.where(outside, fill, ext[x].reshape(4, 8, 128))
            if x < 2:
                block = jnp.where(gx == 0, fill, block)
            if x == 10:
                block = jnp.where(gx == nx - 1, fill, block)
            blocks.append(block)
        blocks = jnp.concatenate(blocks, axis=0).reshape(rows, 128)
        components = blocks.astype(BF16)
        lanes = lane_iota((rows, 128)).astype(F32)
        for p in range(16):
            y4, z4 = p // 4, p % 4
            w_p = jnp.where(emb_lane == p, w_cols, 0.0).astype(BF16)
            grain = jnp.broadcast_to(blocks[:, p * 8 + 7 : p * 8 + 8], (rows, 128))
            onehot = jnp.where(grain == lanes, 1.0, 0.0).astype(BF16)
            both = jnp.concatenate([onehot, components], axis=1)
            value = silu(dot_nt(both, jnp.concatenate([table2, w_p], axis=1)))
            value = value.reshape(len(planes_x), 4, 8, 128)
            for i, x in enumerate(planes_x):
                for yb in range(4):
                    es[x, yb * 4 + y4, pl.ds(z4, 8, stride=4), :] = value[i, yb]

    half = lane_iota((13, 24, 128)) < 64

    def spread_plane(e):
        for t in range(5):
            ay, az = (2 * t) // 3, (2 * t) % 3
            by_, bz_ = min(2 * t + 1, 8) // 3, min(2 * t + 1, 8) % 3
            low = es[e, ay : ay + 13, az : az + 24, :]
            high = es[e, by_ : by_ + 13, bz_ : bz_ + 24, :]
            block = jnp.where(half, low, high)
            af[:, t * 128 : t * 128 + 128] = block.reshape(312, 128).astype(BF16)
        yf[e] = dot_nt(af[...], kf[...])

    half_rows = lane_iota((312, 128)) < 64

    def next_plane(x, carry):
        spread_plane(x + 2)
        fine_plane(x)
        return carry

    def fine_plane(x):
        two = jnp.where(half_rows, yf[x, :, 0:128], yf[x + 1, :, 0:128])
        value = two + pltpu.roll(two, 64, 1) + yf[x + 2, :, 128:256]
        value = silu(value).reshape(13, 24, 128)
        keep = jnp.where((x > 0) | (gx > 0), 1.0, 0.0)
        value = value * fmask[...] * keep
        fs[x, :, 0:24, :] = value.astype(BF16).astype(F32)

    def coarse_copy(x, k):
        return pltpu.make_async_remote_copy(
            src_ref=cs.at[x],
            dst_ref=sb.at[gx, x],
            send_sem=s2.at[x, k],
            recv_sem=r2.at[x, k],
            device_id=device(k, 0, 0),
            device_id_type=MESH,
        )

    half16 = lane_iota((16, 128)) < 64
    cy = gy * 4 - 1 + lax.broadcasted_iota(jnp.int32, (6, 16, 128), 0)
    cz = gz * 8 - 1 + lax.broadcasted_iota(jnp.int32, (6, 16, 128), 1)
    inside = (cy >= 0) & (cy < ny * 4) & (cz >= 0) & (cz < nz * 8)

    def coarse_plane(x, carry):
        lax.fori_loop(2 * x + 1, 2 * x + 3, next_plane, 0)
        for y in range(6):
            row = y * 16
            for t in range(14):
                (ax, ay, az), (bx_, by_, bz_) = tap_of(2 * t), tap_of(2 * t + 1)
                low = fs[2 * x + ax, 2 * y + ay, pl.ds(az, 16, stride=2), :]
                high = fs[2 * x + bx_, 2 * y + by_, pl.ds(bz_, 16, stride=2), :]
                ac[row : row + 16, t * 128 : t * 128 + 128] = jnp.where(half16, low, high).astype(BF16)
        before = dot(ac[...], kd[...]).reshape(6, 16, 128)
        pd[x] = before
        coarse = jnp.where(inside, silu(before), 0.0)
        for y in range(6):
            cb[x, y * 10 : y * 10 + 10, :] = coarse[y, 0:10, :]
        cs[x] = cb[x].astype(BF16)
        sb[gx, x] = cb[x].astype(BF16)
        for k in range(1, nx):
            coarse_copy(x, k).start()
        return carry

    embed(range(2, 10))
    spread_plane(2)
    for c, n in zip(halo, near):
        if n[0] != 0:
            c.wait()
    embed((0, 1, 10))

    def first_planes(e, carry):
        spread_plane(e)
        return carry

    lax.fori_loop(0, 2, first_planes, 0)
    fine_plane(0)
    lax.fori_loop(0, 4, coarse_plane, 0)

    half8 = lane_iota((8, 128)) < 64
    for x in range(4):
        for t in range(14):
            (ax, ay, az), (bx_, by_, bz_) = tap_of(2 * t), tap_of(2 * t + 1)
            parts = []
            for y in range(4):
                low = fs[2 * x + ax, 2 * y + 2 + ay, pl.ds(2 + az, 8, stride=2), :]
                high = fs[2 * x + bx_, 2 * y + 2 + by_, pl.ds(2 + bz_, 8, stride=2), :]
                parts.append(jnp.where(half8, low, high))
            ad[x * 32 : x * 32 + 32, t * 128 : t * 128 + 128] = jnp.concatenate(parts, axis=0).astype(BF16)


    cotf[:, 0:32] = cot[...].astype(F32).reshape(1024, 32)
    group = lane_iota((32, 128)) // 8
    spread = lax.broadcasted_iota(jnp.int32, (8, 128), 0)
    spread = jnp.where(lane_iota((8, 128)) % 8 == spread, 1.0, 0.0).astype(BF16)
    for y in range(4):
        for z in range(8):
            rows = cotf[pl.ds(y * 8 + z, 32, stride=32), :]
            rows = jnp.concatenate([jnp.where(group == q, rows, 0.0) for q in range(4)], axis=0)
            cotp[pl.ds(y * 8 + z, 8, stride=32), :] = dot_nt(spread, rows.astype(BF16))

    def bottle_plane(x, carry):
        for k in range(1, nx):
            coarse_copy(x, k).wait()
        slab[...] = sb[:, x].astype(F32)
        for pair in range(2):
            for t in range(9):
                start = (2 * pair + t // 3) * 10 + t % 3
                window = [slab[:, start : start + 8, :], slab[:, start + 10 : start + 18, :]]
                window = jnp.concatenate(window, axis=1).astype(BF16)
                for n in range(nx):
                    a3[1 + 4 * n + x, pair * 16 : pair * 16 + 16, t * 128 : t * 128 + 128] = window[n]
        part = jnp.concatenate([a3[1 + 4 * n + x] for n in range(nx)], axis=0)
        part = dot_nt(part, kb[...]).reshape(nx, 32, 128)
        for n in range(nx):
            ysum[1 + 4 * n + x] = part[n]
        return carry

    lax.fori_loop(0, 4, bottle_plane, 0)
    group = lane_iota((256, 128)) // 32
    z = None
    for ax in range(3):
        term = None
        for q in range(4):
            rows = ysum[8 * q + ax : 8 * q + ax + 8].reshape(256, 128)
            shift = ((q - ax) * 32) % 128
            rows = rows if shift == 0 else pltpu.roll(rows, shift, 1)
            term = rows if term is None else jnp.where(group == q, rows, term)
        z = term if z is None else z + term
    pre[...] = z
    grad = cotp[...] * silu_grad(z)
    grad = grad.astype(BF16).astype(F32)
    gp[...] = grad

    for side in range(2):
        row = 3 - 3 * side
        ysend[side] = grad.reshape(8, 32, 128)[:, row * 8 : row * 8 + 8].reshape(64, 128).astype(BF16)
        zsend[side] = gp[pl.ds(7 - 7 * side, 32, stride=8), :].astype(BF16)
        for other in range(2):
            corner = gp[pl.ds(row * 8 + 7 - 7 * other, 8, stride=32), :]
            csend[side * 2 + other] = jnp.concatenate([corner, corner], axis=0).astype(BF16)
    rim = []

    def rim_copy(src, dst, number, dy, dz):
        c = pltpu.make_async_remote_copy(
            src_ref=src,
            dst_ref=dst,
            send_sem=s3.at[number],
            recv_sem=r3.at[number],
            device_id=device(0, dy, dz),
            device_id_type=MESH,
        )
        c.start()
        rim.append(c)

    for side in range(2):
        rim_copy(ysend.at[side], yrecv.at[side], side, 1 - 2 * side, 0)
    for side in range(2):
        rim_copy(zsend.at[side], zrecv.at[side], 2 + side, 0, 1 - 2 * side)
    for corner in range(4):
        rim_copy(
            csend.at[corner],
            crecv.at[corner],
            4 + corner,
            1 - 2 * (corner // 2),
            1 - 2 * (corner % 2),
        )

    turned = jnp.transpose(grad)
    turned = [turned[32 * q : 32 * q + 32] for q in range(4)] + [jnp.zeros((32, 128), F32)]
    turned = jnp.concatenate(turned, axis=1)
    turned = [turned, pltpu.roll(turned, 32, 1), pltpu.roll(turned, 64, 1)]
    gt[...] = jnp.concatenate(turned, axis=0).astype(BF16)
    for n in range(3):
        columns_n = a3[:, :, n * 384 : n * 384 + 384].reshape(1152, 384)
        gball[:, n * 384 : n * 384 + 384] = dot(gt[...], columns_n) * scale

    def gball_tile(tile):
        row, lane = (tile // 9) * 32, (tile % 9) * 128
        return gball[row : row + 32, lane : lane + 128]

    for k in range(ny * nz):
        cut = piece(gball_tile, 108 * k, 108)
        gbs[k % nz, k // nz] = cut.astype(BF16)
    me = gy * nz + gz
    gb_copies = []
    for k in range(1, nz):
        target = lax.rem(gz + k, nz)
        gb_copies.append(
            pltpu.make_async_remote_copy(
                src_ref=gbs.at[target],
                dst_ref=gbr.at[gz],
                send_sem=s6.at[k],
                recv_sem=r6.at[k],
                device_id=(gx, gy, target),
                device_id_type=MESH,
            )
        )

    gpad[1:9, 1:5, 1:9, :] = gp[...].reshape(8, 4, 8, 128)
    for c in rim:
        c.wait()
    for c in gb_copies:
        c.start()

    def kept(flag, value):
        return jnp.where(flag, value.astype(F32), 0.0)

    y_ok = (gy > 0, gy < ny - 1)
    z_ok = (gz > 0, gz < nz - 1)
    for side in range(2):
        gpad[1:9, 5 * side, 1:9, :] = kept(y_ok[side], yrecv[side]).reshape(8, 8, 128)
        value = kept(z_ok[side], zrecv[side])
        gpad[1:9, 1:5, 9 * side : 9 * side + 1, :] = value.reshape(8, 4, 1, 128)
        for other in range(2):
            value = kept(y_ok[side] & z_ok[other], crecv[side * 2 + other])
            gpad[1:9, 5 * side, 9 * other : 9 * other + 1, :] = value[0:8].reshape(8, 1, 128)
    edge = lane_iota((96, 128))
    low = pltpu.roll(gpad[8].reshape(96, 128), 32, 1)
    gpad[0] = jnp.where(edge < 32, 0.0, low).reshape(6, 16, 128)
    high = pltpu.roll(gpad[1].reshape(96, 128), 96, 1)
    gpad[9] = jnp.where(edge >= 96, 0.0, high).reshape(6, 16, 128)
    gpadr[...] = pltpu.roll(gpad[...].reshape(960, 128), 64, 1).reshape(10, 6, 16, 128)

    def grad_window(ref, t):
        ax, ay, az = tap_of(t)
        window = ref[2 - ax : 10 - ax, 2 - ay : 6 - ay, 2 - az : 10 - az, :]
        return window.reshape(256, 128)

    half_rows = lane_iota((256, 128)) < 64
    for t in range(14):
        for pair, (one, two) in enumerate([(gpad, gpadr), (gpadr, gpad)]):
            window = jnp.where(half_rows, grad_window(one, 2 * t), grad_window(two, 2 * t + 1))
            ag[pair, :, t * 128 : t * 128 + 128] = window.astype(BF16)
    def act_copy(slot, target, source):
        return pltpu.make_async_remote_copy(
            src_ref=acts.at[target],
            dst_ref=actr.at[slot],
            send_sem=s4.at[target],
            recv_sem=r4.at[source],
            device_id=(target, gy, gz),
            device_id_type=MESH,
        )

    for pair in range(2):
        act = dot(ag[pair], wblk[...]).astype(BF16)
        for part in range(4):
            target = 4 * pair + part
            row, lane = (part % 2) * 128, (part // 2) * 128
            acts[target] = act[row : row + 128, lane : lane + 128]

            @pl.when(gx != target)
            def _(target=target):
                act_copy(gx, target, gx).start()

    out = silu(pre[...]).astype(BF16).astype(F32).reshape(8, 4, 8, 128)
    for y in range(4):
        turned = jnp.transpose(jnp.concatenate([out[:, y].reshape(64, 128), jnp.zeros((64, 128), F32)], axis=0))
        for q in range(4):
            tt[y * 32 : y * 32 + 32, q * 128 : q * 128 + 128] = turned[q * 32 : q * 32 + 32].astype(BF16)
    row = lax.broadcasted_iota(jnp.int32, (512, 128), 0)
    x_of = (row // 128) * 8 + (row % 128) // 8
    x_of = jnp.where(row % 128 < 64, x_of, -1)
    for k in range(8):
        select = jnp.where((x_of == lane_iota((512, 128))) & (row % 8 == k), 1.0, 0.0).astype(BF16)
        turned = dot(tt[...], select)
        for y in range(4):
            bo[pl.ds(y * 8 + k, 32, stride=32), :] = turned[y * 32 : y * 32 + 32]
    bottle_o[...] = bo[...].reshape(32, 4, 8, 128)[:, :, :, 0:32].astype(BF16)

    slope = [silu_grad(pd[x, y + 1, 1:9, :]) for x in range(4) for y in range(4)]
    slope = jnp.concatenate(slope, axis=0)
    total = acts[gx].astype(F32)
    for k in range(1, nx):
        source = lax.rem(gx - k + nx, nx)
        act_copy(source, lax.rem(gx + k, nx), source).wait()
        total = total + actr[source].astype(F32)
    grad_down = (total * slope).astype(BF16).astype(F32)
    grad_down_t = jnp.transpose(grad_down).astype(BF16)

    part = dot(grad_down_t, ad[...]) * scale
    part = part.reshape(nx, 16, 1792)
    downs[...] = part[:, 0:8].astype(BF16)
    dpart[...] = part[:, 8:16].reshape(8 * nx, 1792)
    down_copies = []
    for k in range(1, nx):
        target = lax.rem(gx + k, nx)
        down_copies.append(
            pltpu.make_async_remote_copy(
                src_ref=downs.at[target],
                dst_ref=downr.at[gx],
                send_sem=s5.at[k],
                recv_sem=r5.at[k],
                device_id=(target, gy, gz),
                device_id_type=MESH,
            )
        )
    for c in down_copies:
        c.start()

    low_half = lane_iota((8 * nx, 128)) < 64
    for k in range(ny * nz // 2):
        tz, pair = k % nz, k // nz
        low = piece(lambda tile: dpart[:, tile * 128 : tile * 128 + 128], 54 * (2 * pair * nz + tz), 54)
        high = 54 * ((2 * pair + 1) * nz + tz) - 64
        high = piece(lambda tile: dpart[:, tile * 128 : tile * 128 + 128], high, 118)
        bds[tz, pair] = jnp.where(low_half, low, high).reshape(nx, 8, 128).astype(BF16)
    bd_copies = []
    for k in range(1, nz):
        target = lax.rem(gz + k, nz)
        c = pltpu.make_async_remote_copy(
            src_ref=bds.at[target],
            dst_ref=bdr.at[gz],
            send_sem=s9.at[k],
            recv_sem=r9.at[k],
            device_id=(gx, gy, target),
            device_id_type=MESH,
        )
        c.start()
        bd_copies.append(c)

    total = gbs[gz].astype(F32)
    for k, c in enumerate(gb_copies, 1):
        c.wait()
        total = total + gbr[lax.rem(gz - k + nz, nz)].astype(F32)
    gb2s[...] = total.astype(BF16)
    gb2_copies = []
    for k in range(1, ny):
        target = lax.rem(gy + k, ny)
        c = pltpu.make_async_remote_copy(
            src_ref=gb2s.at[target],
            dst_ref=gb2r.at[gy],
            send_sem=s8.at[k],
            recv_sem=r8.at[k],
            device_id=(gx, target, gz),
            device_id_type=MESH,
        )
        c.start()
        gb2_copies.append(c)

    dsum[...] = downs[gx].astype(F32)
    for k, c in enumerate(down_copies, 1):
        c.wait()
        dsum[...] += downr[lax.rem(gx - k + nx, nx)].astype(F32)
    for k in range(ny * nz):
        gds[k] = piece(lambda tile: dsum[:, tile * 128 : tile * 128 + 128], 54 * k, 54).astype(BF16)
    gd_copies = []
    planes.sort(key=lambda p: -2 * min(p[1], ny - p[1]) - min(p[2], nz - p[2]))
    for k, (_, dy, dz) in enumerate(planes):
        ty, tz = lax.rem(gy + dy, ny), lax.rem(gz + dz, nz)
        c = pltpu.make_async_remote_copy(
            src_ref=gds.at[ty * nz + tz],
            dst_ref=gdr.at[me],
            send_sem=s7.at[k],
            recv_sem=r7.at[k],
            device_id=(gx, ty, tz),
            device_id_type=MESH,
        )
        c.start()
        gd_copies.append(c)
    total = bds[gz].astype(F32)
    for k, c in enumerate(bd_copies, 1):
        c.wait()
        total = total + bdr[lax.rem(gz - k + nz, nz)].astype(F32)
    b2s[...] = total.astype(BF16)
    sheets.sort(key=lambda p: -2 * min(p[1], ny - p[1]) - min(p[0], nx - p[0]))
    b2_copies = []
    for k, (dx, dy, _) in enumerate(sheets):
        tx, ty = lax.rem(gx + dx, nx), lax.rem(gy + dy, ny)
        c = pltpu.make_async_remote_copy(
            src_ref=b2s.at[ty // 2, tx],
            dst_ref=b2r.at[gx * ny + gy],
            send_sem=s10.at[k],
            recv_sem=r10.at[k],
            device_id=(tx, ty, gz),
            device_id_type=MESH,
        )
        c.start()
        b2_copies.append(c)
    total = gb2s[gy].astype(F32)
    for k, c in enumerate(gb2_copies, 1):
        c.wait()
        total = total + gb2r[lax.rem(gy - k + ny, ny)].astype(F32)
    gbot_o[...] = total[:, 0:108]
    total = gds[me].astype(F32)
    for c in gd_copies:
        c.wait()
    for k, (_, dy, dz) in enumerate(planes):
        source = lax.rem(gy - dy + ny, ny) * nz + lax.rem(gz - dz + nz, nz)
        total = total + gdr[source].astype(F32)
    gdown_o[0:8, :] = total[:, 0:54]
    total = b2s[gy // 2, gx].astype(F32)
    for c in b2_copies:
        c.wait()
    for k, (dx, dy, _) in enumerate(sheets):
        source = lax.rem(gx - dx + nx, nx) * ny + lax.rem(gy - dy + ny, ny)
        total = total + b2r[source].astype(F32)
    total = jnp.where(lax.rem(gy, 2) == 1, pltpu.roll(total, 64, 1), total)
    gdown_o[8:16, :] = total[:, 0:54]


def put_out(a, b, c, a_out, b_out, c_out, sems):
    copies = [
        pltpu.make_async_copy(source, out, sems.at[i])
        for i, (source, out) in enumerate([(a, a_out), (b, b_out), (c, c_out)])
    ]
    for copy in copies:
        copy.start()
    for copy in copies:
        copy.wait()


def per_device(sizes, fields, grain_ids, table, w_in, k_fine, k_down, k_bot, cotangent):
    nx, ny, nz = sizes
    n = ny * nz
    cot = cotangent.transpose(0, 2, 3, 1)
    vmem = pl.BlockSpec(memory_space=pltpu.VMEM)
    V = pltpu.VMEM
    D = pltpu.SemaphoreType.DMA
    scratch = [
        V((7, 8, 8, 16), BF16),
        V((8, 8, 16), jnp.int32),
        V((64, 128), BF16),
        V((7, 64), BF16),
        V((64, 1728), BF16),
        V((32, 4, 8, 32), BF16),
        V((1024, 128), F32),
        V((256, 128), F32),
        V((128, 512), BF16),
        V((1024, 128), F32),
        V((64, 128), F32),
        V((8, 2, 4, 1, 128), F32),
        V((11, 4, 8, 1, 128), F32),
        V((11, 16, 32, 128), F32),
        V((312, 640), BF16),
        V((11, 312, 256), F32),
        V((9, 13, 40, 128), F32),
        V((13, 24, 128), F32),
        V((256, 640), BF16),
        V((1792, 128), BF16),
        V((128, 1152), BF16),
        V((1792, 256), BF16),
        V((96, 1792), BF16),
        V((128, 1792), BF16),
        V((4, 6, 16, 128), F32),
        V((4, 64, 128), F32),
        V((4, 64, 128), BF16),
        V((nx, 4, 64, 128), BF16),
        V((nx, 64, 128), F32),
        V((36, 32, 1152), BF16),
        V((36, 32, 128), F32),
        V((256, 128), F32),
        V((256, 128), F32),
        V((96, 1152), BF16),
        V((2, 64, 128), BF16),
        V((2, 32, 128), BF16),
        V((4, 16, 128), BF16),
        V((2, 64, 128), BF16),
        V((2, 32, 128), BF16),
        V((4, 16, 128), BF16),
        V((10, 6, 16, 128), F32),
        V((10, 6, 16, 128), F32),
        V((2, 256, 1792), BF16),
        V((nx, 128, 128), BF16),
        V((nx, 128, 128), BF16),
        V((nx, 8, 1792), BF16),
        V((nx, 8, 1792), BF16),
        V((8, 1792), F32),
        V((8 * nx, 1792), F32),
        V((nz, ny // 2, nx, 8, 128), BF16),
        V((nz, ny // 2, nx, 8, 128), BF16),
        V((ny // 2, nx, 8, 128), BF16),
        V((nx * ny, 8, 128), BF16),
        V((96, 1152), F32),
        V((nz, ny, 32, 128), BF16),
        V((nz, ny, 32, 128), BF16),
        V((ny, 32, 128), BF16),
        V((ny, 32, 128), BF16),
        V((n, 8, 128), BF16),
        V((n, 8, 128), BF16),
        D((12,)),
        D((26,)),
        D((26,)),
        D((4, nx)),
        D((4, nx)),
        D((8,)),
        D((8,)),
        D((nx,)),
        D((nx,)),
        D((nx,)),
        D((nx,)),
        D((nz,)),
        D((nz,)),
        D((n,)),
        D((n,)),
        D((ny,)),
        D((ny,)),
        D((nz,)),
        D((nz,)),
        D((nx * ny,)),
        D((nx * ny,)),
    ]
    bottle, grad_down, grad_bottle = pl.pallas_call(
        functools.partial(body, sizes),
        out_shape=(
            V((32, 4, 8, 32), BF16),
            V((16, 54), F32),
            V((32, 108), F32),
        ),
        in_specs=[pl.BlockSpec(memory_space=pl.ANY)] * 8,
        out_specs=(vmem, vmem, vmem),
        scratch_shapes=scratch,
        compiler_params=pltpu.CompilerParams(
            collective_id=0, has_side_effects=True, vmem_limit_bytes=60 * 1024 * 1024
        ),
    )(fields, grain_ids, table.T, w_in.T, k_fine, k_down.T, k_bot, cot)
    bottle, grad_down, grad_bottle = pl.pallas_call(
        put_out,
        out_shape=(
            jax.ShapeDtypeStruct((32, 4, 8, 32), BF16),
            jax.ShapeDtypeStruct((16, 54), F32),
            jax.ShapeDtypeStruct((32, 108), F32),
        ),
        in_specs=[vmem] * 3,
        out_specs=[pl.BlockSpec(memory_space=pl.ANY)] * 3,
        scratch_shapes=[D((3,))],
        compiler_params=pltpu.CompilerParams(vmem_limit_bytes=1024 * 1024),
    )(bottle, grad_down, grad_bottle)
    return bottle.transpose(0, 3, 1, 2), grad_down, grad_bottle


def solution(mesh):
    sizes = (mesh.shape["gx"], mesh.shape["gy"], mesh.shape["gz"])
    placed = (
        P(None, "gx", "gy", "gz"),
        P("gx", "gy", "gz"),
        P(),
        P(),
        P(),
        P(),
        P("gx", None),
        P("gx", None, "gy", "gz"),
    )
    return jax.shard_map(
        functools.partial(per_device, sizes),
        mesh=mesh,
        in_specs=placed,
        out_specs=(P("gx", None, "gy", "gz"), P("gx", ("gy", "gz")), P("gx", ("gy", "gz"))),
        check_vma=False,
    )
```

```python
import functools
import math

import jax
import jax.numpy as jnp
from jax import lax
from jax.experimental import pallas as pl
from jax.experimental.pallas import tpu as pltpu
from jax.sharding import PartitionSpec as P

MESH = pl.DeviceIdType.MESH
F32 = jnp.float32
BF16 = jnp.bfloat16
NT = (((1,), (1,)), ((), ()))


def silu(v):
    return v * jax.nn.sigmoid(v)


def silu_grad(v):
    s = jax.nn.sigmoid(v)
    return s * (1.0 + v * (1.0 - s))


def dot(a, b):
    return jnp.dot(a, b, preferred_element_type=F32)


def dot_nt(a, b):
    return lax.dot_general(a, b, NT, preferred_element_type=F32)


def tap_of(t):
    t = min(t, 26)
    return t // 9, (t // 3) % 3, t % 3


def lane_iota(shape):
    return lax.broadcasted_iota(jnp.int32, shape, len(shape) - 1)


def piece(ref_tiles, start, width):
    tile, shift = start // 128, start % 128
    low = ref_tiles(tile)
    if shift == 0:
        return low
    low = pltpu.roll(low, 128 - shift, 1)
    if shift + width <= 128:
        return low
    high = pltpu.roll(ref_tiles(tile + 1), 128 - shift, 1)
    return jnp.where(lane_iota(low.shape) < 128 - shift, low, high)


def body(
    sizes,
    fields_h,
    ids_h,
    table_h,
    w_in_h,
    k_fine_h,
    k_down_h,
    k_bot_h,
    cot_h,
    bottle_o,
    gdown_o,
    gbot_o,
    fields,
    ids,
    table,
    w_in,
    k_fine,
    cot,
    cotf,
    cotp,
    tt,
    bo,
    raw,
    brick,
    ext,
    es,
    af,
    yf,
    fs,
    fmask,
    kf,
    kd,
    kb,
    wblk,
    ac,
    ad,
    pd,
    cb,
    cs,
    sb,
    slab,
    a3,
    ysum,
    pre,
    gp,
    gt,
    ysend,
    zsend,
    csend,
    yrecv,
    zrecv,
    crecv,
    gpad,
    gpadr,
    ag,
    acts,
    actr,
    downs,
    downr,
    dsum,
    dpart,
    bds,
    bdr,
    b2s,
    b2r,
    gball,
    gbs,
    gbr,
    gb2s,
    gb2r,
    gds,
    gdr,
    sem_l,
    s1,
    r1,
    s2,
    r2,
    s3,
    r3,
    s4,
    r4,
    s5,
    r5,
    s6,
    r6,
    s7,
    r7,
    s8,
    r8,
    s9,
    r9,
    s10,
    r10,
):
    nx, ny, nz = sizes
    gx, gy, gz = lax.axis_index("gx"), lax.axis_index("gy"), lax.axis_index("gz")
    scale = 1.0 / math.sqrt(nx * 4 * ny * 4 * nz * 8)

    def device(dx, dy, dz):
        return (lax.rem(gx + dx + nx, nx), lax.rem(gy + dy + ny, ny), lax.rem(gz + dz + nz, nz))

    near = [(dx, dy, dz) for dx in (-1, 0, 1) for dy in (-1, 0, 1) for dz in (-1, 0, 1)]
    near = [n for n in near if n != (0, 0, 0)]
    columns = [(dx, 0, 0) for dx in range(1, nx)]
    planes = [(0, dy, dz) for dy in range(ny) for dz in range(nz) if (dy, dz) != (0, 0)]
    sheets = [(dx, dy, 0) for dx in range(nx) for dy in range(ny) if (dx, dy) != (0, 0)]
    partners = sorted({(a % nx, b % ny, c % nz) for a, b, c in near + columns + [(0, 0, nz // 2)]})
    partners.sort(key=lambda p: -2 * min(p[1], ny - p[1]) - min(p[2], nz - p[2]) - min(p[0], nx - p[0]))
    barrier = pltpu.get_barrier_semaphore()
    for p in partners:
        pl.semaphore_signal(barrier, inc=1, device_id=device(*p), device_id_type=MESH)

    loads = [
        pltpu.make_async_copy(src, dst, sem_l.at[1 + i])
        for i, (src, dst) in enumerate(
            [(fields_h, fields), (ids_h, ids), (table_h, table), (w_in_h, w_in), (k_fine_h, k_fine)]
            + [(k_down_h, kd.at[0:1728]), (cot_h, cot)]
            + [
                (k_bot_h.at[:, x * 1152 : x * 1152 + 1152], kb.at[32 * x : 32 * x + 32])
                for x in range(3)
            ]
        )
    ]
    for c in loads:
        c.start()
    kd[1728:1792, :] = jnp.zeros((64, 128), BF16)
    kb[96:128, :] = jnp.zeros((32, 1152), BF16)
    kf[...] = jnp.zeros(kf.shape, BF16)
    wblk[...] = jnp.zeros(wblk.shape, BF16)
    fs[...] = jnp.zeros(fs.shape, F32)
    gpad[...] = jnp.zeros(gpad.shape, F32)
    a3[0] = jnp.zeros((32, 1152), BF16)
    a3[4 * nx + 1 : 4 * nx + 4] = jnp.zeros((3, 32, 1152), BF16)
    ysum[0] = jnp.zeros((32, 128), F32)
    ysum[4 * nx + 1] = jnp.zeros((32, 128), F32)
    cb[...] = jnp.zeros(cb.shape, F32)
    cotf[...] = jnp.zeros(cotf.shape, F32)
    ext[:, :, 6:8] = jnp.zeros((11, 4, 2, 1, 128), F32)
    for c in loads[0:2]:
        c.wait()

    sel_row = lax.broadcasted_iota(jnp.int32, (16, 128), 0)
    sel_lane = lax.broadcasted_iota(jnp.int32, (16, 128), 1)
    packed = jnp.zeros((64, 128), F32)
    for ch in range(8):
        plane = (fields[ch] if ch < 7 else ids[...]).astype(F32).reshape(64, 16).astype(BF16)
        select = jnp.where(sel_lane == sel_row * 8 + ch, 1.0, 0.0).astype(BF16)
        packed = packed + dot(plane, select)
    raw[...] = packed
    group = lane_iota((16, 128)) // 32
    for zb in range(4):
        block = None
        for y4 in range(4):
            rows = raw[pl.ds(y4, 16, stride=4), :]
            shift = ((y4 - zb) * 32) % 128
            rows = rows if shift == 0 else pltpu.roll(rows, shift, 1)
            block = rows if block is None else jnp.where(group == y4, rows, block)
        for r in range(16):
            brick[r // 2, r % 2, zb, :, :] = block[r : r + 1, :]

    for c in loads[2:]:
        c.wait()
    lane = lane_iota((64, 640))
    first = jnp.where(lane < 576, k_fine[:, 0:640].astype(F32), 0.0)
    second = pltpu.roll(k_fine[:, 512:1152].astype(F32), 576, 1)
    kf[0:64, :] = first.astype(BF16)
    kf[64:128, :] = jnp.where(lane < 576, second, 0.0).astype(BF16)
    for n in (128, 192):
        kf[n : n + 64, 0:576] = k_fine[:, 1152:1728]
    for t in range(27):
        for q in range(2):
            row = t * 64 + q * 32
            wblk[row : row + 32, q * 128 : q * 128 + 128] = kb[
                (t // 9) * 32 : (t // 9) * 32 + 32, (t % 9) * 128 : (t % 9) * 128 + 128
            ]
    my = gy * 8 - 3 + lax.broadcasted_iota(jnp.int32, (13, 24, 128), 0)
    mz = gz * 16 - 3 + lax.broadcasted_iota(jnp.int32, (13, 24, 128), 1)
    inside = (my >= 0) & (my < ny * 8) & (mz >= 0) & (mz < nz * 16)
    fmask[...] = jnp.where(inside, 1.0, 0.0)

    pl.semaphore_wait(barrier, len(partners))

    x_src = {1: (6, 2, 0), 0: (0, 8, 2), -1: (0, 1, 10)}
    y_src = {1: (1, 1, 0), 0: (0, 2, 1), -1: (0, 1, 3)}
    z_src = {1: (3, 1, 0), 0: (0, 4, 1), -1: (0, 1, 5)}
    halo = []
    for number, (dx, dy, dz) in enumerate(near):
        (xs, xn, xd), (ys, yn, yd), (zs, zn, zd) = x_src[dx], y_src[dy], z_src[dz]
        halo.append(
            pltpu.make_async_remote_copy(
                src_ref=brick.at[xs : xs + xn, ys : ys + yn, zs : zs + zn],
                dst_ref=ext.at[xd : xd + xn, yd : yd + yn, zd : zd + zn],
                send_sem=s1.at[number],
                recv_sem=r1.at[number],
                device_id=device(dx, dy, dz),
                device_id_type=MESH,
            )
        )
    for c in halo:
        c.start()
    own = pltpu.make_async_copy(brick, ext.at[2:10, 1:3, 1:5], sem_l.at[0])
    own.start()

    row8 = lax.broadcasted_iota(jnp.int32, (128, 7), 0) % 8
    pick = jnp.where(row8 == lax.broadcasted_iota(jnp.int32, (128, 7), 1), 1.0, 0.0).astype(BF16)
    emb_lane = lane_iota((128, 128)) // 8
    twice = jnp.where(
        lax.broadcasted_iota(jnp.int32, (64, 128), 1) % 64
        == lax.broadcasted_iota(jnp.int32, (64, 128), 0),
        1.0,
        0.0,
    ).astype(BF16)
    w_rows = dot(pick, dot(w_in[...], twice).astype(BF16))
    table2 = jnp.concatenate([table[...]] * 2, axis=0)
    w_cols = jnp.transpose(w_rows)

    own.wait()
    for c, n in zip(halo, near):
        if n[0] == 0:
            c.wait()

    by = lax.broadcasted_iota(jnp.int32, (4, 8, 128), 0)
    bz = lax.broadcasted_iota(jnp.int32, (4, 8, 128), 1)
    outside = ((by == 0) & (gy == 0)) | ((by == 3) & (gy == ny - 1))
    outside = outside | ((bz == 0) & (gz == 0)) | ((bz == 5) & (gz == nz - 1))
    fill = jnp.where(lane_iota((4, 8, 128)) % 8 == 7, -1.0, 0.0)

    def embed(planes_x):
        rows = len(planes_x) * 32
        blocks = []
        for x in planes_x:
            block = jnp.where(outside, fill, ext[x].reshape(4, 8, 128))
            if x < 2:
                block = jnp.where(gx == 0, fill, block)
            if x == 10:
                block = jnp.where(gx == nx - 1, fill, block)
            blocks.append(block)
        blocks = jnp.concatenate(blocks, axis=0).reshape(rows, 128)
        components = blocks.astype(BF16)
        lanes = lane_iota((rows, 128)).astype(F32)
        for p in range(16):
            y4, z4 = p // 4, p % 4
            w_p = jnp.where(emb_lane == p, w_cols, 0.0).astype(BF16)
            grain = jnp.broadcast_to(blocks[:, p * 8 + 7 : p * 8 + 8], (rows, 128))
            onehot = jnp.where(grain == lanes, 1.0, 0.0).astype(BF16)
            both = jnp.concatenate([onehot, components], axis=1)
            value = silu(dot_nt(both, jnp.concatenate([table2, w_p], axis=1)))
            value = value.reshape(len(planes_x), 4, 8, 128)
            for i, x in enumerate(planes_x):
                for yb in range(4):
                    es[x, yb * 4 + y4, pl.ds(z4, 8, stride=4), :] = value[i, yb]

    half = lane_iota((13, 24, 128)) < 64

    def spread_plane(e):
        for t in range(5):
            ay, az = (2 * t) // 3, (2 * t) % 3
            by_, bz_ = min(2 * t + 1, 8) // 3, min(2 * t + 1, 8) % 3
            low = es[e, ay : ay + 13, az : az + 24, :]
            high = es[e, by_ : by_ + 13, bz_ : bz_ + 24, :]
            block = jnp.where(half, low, high)
            af[:, t * 128 : t * 128 + 128] = block.reshape(312, 128).astype(BF16)
        yf[e] = dot_nt(af[...], kf[...])

    half_rows = lane_iota((312, 128)) < 64

    def next_plane(x, carry):
        spread_plane(x + 2)
        fine_plane(x)
        return carry

    def fine_plane(x):
        two = jnp.where(half_rows, yf[x, :, 0:128], yf[x + 1, :, 0:128])
        value = two + pltpu.roll(two, 64, 1) + yf[x + 2, :, 128:256]
        value = silu(value).reshape(13, 24, 128)
        keep = jnp.where((x > 0) | (gx > 0), 1.0, 0.0)
        value = value * fmask[...] * keep
        fs[x, :, 0:24, :] = value.astype(BF16).astype(F32)

    def coarse_copy(x, k):
        return pltpu.make_async_remote_copy(
            src_ref=cs.at[x],
            dst_ref=sb.at[gx, x],
            send_sem=s2.at[x, k],
            recv_sem=r2.at[x, k],
            device_id=device(k, 0, 0),
            device_id_type=MESH,
        )

    half16 = lane_iota((16, 128)) < 64
    cy = gy * 4 - 1 + lax.broadcasted_iota(jnp.int32, (6, 16, 128), 0)
    cz = gz * 8 - 1 + lax.broadcasted_iota(jnp.int32, (6, 16, 128), 1)
    inside = (cy >= 0) & (cy < ny * 4) & (cz >= 0) & (cz < nz * 8)

    def coarse_plane(x, carry):
        lax.fori_loop(2 * x + 1, 2 * x + 3, next_plane, 0)
        for y in range(6):
            row = y * 16
            for t in range(14):
                (ax, ay, az), (bx_, by_, bz_) = tap_of(2 * t), tap_of(2 * t + 1)
                low = fs[2 * x + ax, 2 * y + ay, pl.ds(az, 16, stride=2), :]
                high = fs[2 * x + bx_, 2 * y + by_, pl.ds(bz_, 16, stride=2), :]
                ac[row : row + 16, t * 128 : t * 128 + 128] = jnp.where(half16, low, high).astype(BF16)
        before = dot(ac[...], kd[...]).reshape(6, 16, 128)
        pd[x] = before
        coarse = jnp.where(inside, silu(before), 0.0)
        for y in range(6):
            cb[x, y * 10 : y * 10 + 10, :] = coarse[y, 0:10, :]
        cs[x] = cb[x].astype(BF16)
        sb[gx, x] = cb[x].astype(BF16)
        for k in range(1, nx):
            coarse_copy(x, k).start()
        return carry

    embed(range(2, 10))
    spread_plane(2)
    for c, n in zip(halo, near):
        if n[0] != 0:
            c.wait()
    embed((0, 1, 10))

    def first_planes(e, carry):
        spread_plane(e)
        return carry

    lax.fori_loop(0, 2, first_planes, 0)
    fine_plane(0)
    lax.fori_loop(0, 4, coarse_plane, 0)

    half8 = lane_iota((8, 128)) < 64
    for x in range(4):
        for t in range(14):
            (ax, ay, az), (bx_, by_, bz_) = tap_of(2 * t), tap_of(2 * t + 1)
            parts = []
            for y in range(4):
                low = fs[2 * x + ax, 2 * y + 2 + ay, pl.ds(2 + az, 8, stride=2), :]
                high = fs[2 * x + bx_, 2 * y + 2 + by_, pl.ds(2 + bz_, 8, stride=2), :]
                parts.append(jnp.where(half8, low, high))
            ad[x * 32 : x * 32 + 32, t * 128 : t * 128 + 128] = jnp.concatenate(parts, axis=0).astype(BF16)


    cotf[:, 0:32] = cot[...].astype(F32).reshape(1024, 32)
    group = lane_iota((32, 128)) // 8
    spread = lax.broadcasted_iota(jnp.int32, (8, 128), 0)
    spread = jnp.where(lane_iota((8, 128)) % 8 == spread, 1.0, 0.0).astype(BF16)
    for y in range(4):
        for z in range(8):
            rows = cotf[pl.ds(y * 8 + z, 32, stride=32), :]
            rows = jnp.concatenate([jnp.where(group == q, rows, 0.0) for q in range(4)], axis=0)
            cotp[pl.ds(y * 8 + z, 8, stride=32), :] = dot_nt(spread, rows.astype(BF16))

    def bottle_plane(x, carry):
        for k in range(1, nx):
            coarse_copy(x, k).wait()
        slab[...] = sb[:, x].astype(F32)
        for pair in range(2):
            for t in range(9):
                start = (2 * pair + t // 3) * 10 + t % 3
                window = [slab[:, start : start + 8, :], slab[:, start + 10 : start + 18, :]]
                window = jnp.concatenate(window, axis=1).astype(BF16)
                for n in range(nx):
                    a3[1 + 4 * n + x, pair * 16 : pair * 16 + 16, t * 128 : t * 128 + 128] = window[n]
        part = jnp.concatenate([a3[1 + 4 * n + x] for n in range(nx)], axis=0)
        part = dot_nt(part, kb[...]).reshape(nx, 32, 128)
        for n in range(nx):
            ysum[1 + 4 * n + x] = part[n]
        return carry

    lax.fori_loop(0, 4, bottle_plane, 0)
    group = lane_iota((256, 128)) // 32
    z = None
    for ax in range(3):
        term = None
        for q in range(4):
            rows = ysum[8 * q + ax : 8 * q + ax + 8].reshape(256, 128)
            shift = ((q - ax) * 32) % 128
            rows = rows if shift == 0 else pltpu.roll(rows, shift, 1)
            term = rows if term is None else jnp.where(group == q, rows, term)
        z = term if z is None else z + term
    pre[...] = z
    grad = cotp[...] * silu_grad(z)
    grad = grad.astype(BF16).astype(F32)
    gp[...] = grad

    for side in range(2):
        row = 3 - 3 * side
        ysend[side] = grad.reshape(8, 32, 128)[:, row * 8 : row * 8 + 8].reshape(64, 128).astype(BF16)
        zsend[side] = gp[pl.ds(7 - 7 * side, 32, stride=8), :].astype(BF16)
        for other in range(2):
            corner = gp[pl.ds(row * 8 + 7 - 7 * other, 8, stride=32), :]
            csend[side * 2 + other] = jnp.concatenate([corner, corner], axis=0).astype(BF16)
    rim = []

    def rim_copy(src, dst, number, dy, dz):
        c = pltpu.make_async_remote_copy(
            src_ref=src,
            dst_ref=dst,
            send_sem=s3.at[number],
            recv_sem=r3.at[number],
            device_id=device(0, dy, dz),
            device_id_type=MESH,
        )
        c.start()
        rim.append(c)

    for side in range(2):
        rim_copy(ysend.at[side], yrecv.at[side], side, 1 - 2 * side, 0)
    for side in range(2):
        rim_copy(zsend.at[side], zrecv.at[side], 2 + side, 0, 1 - 2 * side)
    for corner in range(4):
        rim_copy(
            csend.at[corner],
            crecv.at[corner],
            4 + corner,
            1 - 2 * (corner // 2),
            1 - 2 * (corner % 2),
        )

    turned = jnp.transpose(grad)
    turned = [turned[32 * q : 32 * q + 32] for q in range(4)] + [jnp.zeros((32, 128), F32)]
    turned = jnp.concatenate(turned, axis=1)
    turned = [turned, pltpu.roll(turned, 32, 1), pltpu.roll(turned, 64, 1)]
    gt[...] = jnp.concatenate(turned, axis=0).astype(BF16)
    for n in range(3):
        columns_n = a3[:, :, n * 384 : n * 384 + 384].reshape(1152, 384)
        gball[:, n * 384 : n * 384 + 384] = dot(gt[...], columns_n) * scale

    def gball_tile(tile):
        row, lane = (tile // 9) * 32, (tile % 9) * 128
        return gball[row : row + 32, lane : lane + 128]

    for k in range(ny * nz):
        cut = piece(gball_tile, 108 * k, 108)
        gbs[k % nz, k // nz] = cut.astype(BF16)
    me = gy * nz + gz
    gb_copies = []
    for k in range(1, nz):
        target = lax.rem(gz + k, nz)
        gb_copies.append(
            pltpu.make_async_remote_copy(
                src_ref=gbs.at[target],
                dst_ref=gbr.at[gz],
                send_sem=s6.at[k],
                recv_sem=r6.at[k],
                device_id=(gx, gy, target),
                device_id_type=MESH,
            )
        )

    gpad[1:9, 1:5, 1:9, :] = gp[...].reshape(8, 4, 8, 128)
    for c in rim:
        c.wait()
    for c in gb_copies:
        c.start()

    def kept(flag, value):
        return jnp.where(flag, value.astype(F32), 0.0)

    y_ok = (gy > 0, gy < ny - 1)
    z_ok = (gz > 0, gz < nz - 1)
    for side in range(2):
        gpad[1:9, 5 * side, 1:9, :] = kept(y_ok[side], yrecv[side]).reshape(8, 8, 128)
        value = kept(z_ok[side], zrecv[side])
        gpad[1:9, 1:5, 9 * side : 9 * side + 1, :] = value.reshape(8, 4, 1, 128)
        for other in range(2):
            value = kept(y_ok[side] & z_ok[other], crecv[side * 2 + other])
            gpad[1:9, 5 * side, 9 * other : 9 * other + 1, :] = value[0:8].reshape(8, 1, 128)
    edge = lane_iota((96, 128))
    low = pltpu.roll(gpad[8].reshape(96, 128), 32, 1)
    gpad[0] = jnp.where(edge < 32, 0.0, low).reshape(6, 16, 128)
    high = pltpu.roll(gpad[1].reshape(96, 128), 96, 1)
    gpad[9] = jnp.where(edge >= 96, 0.0, high).reshape(6, 16, 128)
    gpadr[...] = pltpu.roll(gpad[...].reshape(960, 128), 64, 1).reshape(10, 6, 16, 128)

    def grad_window(ref, t):
        ax, ay, az = tap_of(t)
        window = ref[2 - ax : 10 - ax, 2 - ay : 6 - ay, 2 - az : 10 - az, :]
        return window.reshape(256, 128)

    half_rows = lane_iota((256, 128)) < 64
    for t in range(14):
        for pair, (one, two) in enumerate([(gpad, gpadr), (gpadr, gpad)]):
            window = jnp.where(half_rows, grad_window(one, 2 * t), grad_window(two, 2 * t + 1))
            ag[pair, :, t * 128 : t * 128 + 128] = window.astype(BF16)
    def act_copy(slot, target, source):
        return pltpu.make_async_remote_copy(
            src_ref=acts.at[target],
            dst_ref=actr.at[slot],
            send_sem=s4.at[target],
            recv_sem=r4.at[source],
            device_id=(target, gy, gz),
            device_id_type=MESH,
        )

    for pair in range(2):
        act = dot(ag[pair], wblk[...]).astype(BF16)
        for part in range(4):
            target = 4 * pair + part
            row, lane = (part % 2) * 128, (part // 2) * 128
            acts[target] = act[row : row + 128, lane : lane + 128]

            @pl.when(gx != target)
            def _(target=target):
                act_copy(gx, target, gx).start()

    out = silu(pre[...]).astype(BF16).astype(F32).reshape(8, 4, 8, 128)
    for y in range(4):
        turned = jnp.transpose(jnp.concatenate([out[:, y].reshape(64, 128), jnp.zeros((64, 128), F32)], axis=0))
        for q in range(4):
            tt[y * 32 : y * 32 + 32, q * 128 : q * 128 + 128] = turned[q * 32 : q * 32 + 32].astype(BF16)
    row = lax.broadcasted_iota(jnp.int32, (512, 128), 0)
    x_of = (row // 128) * 8 + (row % 128) // 8
    x_of = jnp.where(row % 128 < 64, x_of, -1)
    for k in range(8):
        select = jnp.where((x_of == lane_iota((512, 128))) & (row % 8 == k), 1.0, 0.0).astype(BF16)
        turned = dot(tt[...], select)
        for y in range(4):
            bo[pl.ds(y * 8 + k, 32, stride=32), :] = turned[y * 32 : y * 32 + 32]
    bottle_o[...] = bo[...].reshape(32, 4, 8, 128)[:, :, :, 0:32].astype(BF16)

    slope = [silu_grad(pd[x, y + 1, 1:9, :]) for x in range(4) for y in range(4)]
    slope = jnp.concatenate(slope, axis=0)
    total = acts[gx].astype(F32)
    for k in range(1, nx):
        source = lax.rem(gx - k + nx, nx)
        act_copy(source, lax.rem(gx + k, nx), source).wait()
        total = total + actr[source].astype(F32)
    grad_down = (total * slope).astype(BF16).astype(F32)
    grad_down_t = jnp.transpose(grad_down).astype(BF16)

    part = dot(grad_down_t, ad[...]) * scale
    part = part.reshape(nx, 16, 1792)
    downs[...] = part[:, 0:8].astype(BF16)
    dpart[...] = part[:, 8:16].reshape(8 * nx, 1792)
    down_copies = []
    for k in range(1, nx):
        target = lax.rem(gx + k, nx)
        down_copies.append(
            pltpu.make_async_remote_copy(
                src_ref=downs.at[target],
                dst_ref=downr.at[gx],
                send_sem=s5.at[k],
                recv_sem=r5.at[k],
                device_id=(target, gy, gz),
                device_id_type=MESH,
            )
        )
    for c in down_copies:
        c.start()

    low_half = lane_iota((8 * nx, 128)) < 64
    for k in range(ny * nz // 2):
        tz, pair = k % nz, k // nz
        low = piece(lambda tile: dpart[:, tile * 128 : tile * 128 + 128], 54 * (2 * pair * nz + tz), 54)
        high = 54 * ((2 * pair + 1) * nz + tz) - 64
        high = piece(lambda tile: dpart[:, tile * 128 : tile * 128 + 128], high, 118)
        bds[tz, pair] = jnp.where(low_half, low, high).reshape(nx, 8, 128).astype(BF16)
    bd_copies = []
    for k in range(1, nz):
        target = lax.rem(gz + k, nz)
        c = pltpu.make_async_remote_copy(
            src_ref=bds.at[target],
            dst_ref=bdr.at[gz],
            send_sem=s9.at[k],
            recv_sem=r9.at[k],
            device_id=(gx, gy, target),
            device_id_type=MESH,
        )
        c.start()
        bd_copies.append(c)

    total = gbs[gz].astype(F32)
    for k, c in enumerate(gb_copies, 1):
        c.wait()
        total = total + gbr[lax.rem(gz - k + nz, nz)].astype(F32)
    gb2s[...] = total.astype(BF16)
    gb2_copies = []
    for k in range(1, ny):
        target = lax.rem(gy + k, ny)
        c = pltpu.make_async_remote_copy(
            src_ref=gb2s.at[target],
            dst_ref=gb2r.at[gy],
            send_sem=s8.at[k],
            recv_sem=r8.at[k],
            device_id=(gx, target, gz),
            device_id_type=MESH,
        )
        c.start()
        gb2_copies.append(c)

    dsum[...] = downs[gx].astype(F32)
    for k, c in enumerate(down_copies, 1):
        c.wait()
        dsum[...] += downr[lax.rem(gx - k + nx, nx)].astype(F32)
    for k in range(ny * nz):
        gds[k] = piece(lambda tile: dsum[:, tile * 128 : tile * 128 + 128], 54 * k, 54).astype(BF16)
    gd_copies = []
    planes.sort(key=lambda p: -2 * min(p[1], ny - p[1]) - min(p[2], nz - p[2]))
    for k, (_, dy, dz) in enumerate(planes):
        ty, tz = lax.rem(gy + dy, ny), lax.rem(gz + dz, nz)
        c = pltpu.make_async_remote_copy(
            src_ref=gds.at[ty * nz + tz],
            dst_ref=gdr.at[me],
            send_sem=s7.at[k],
            recv_sem=r7.at[k],
            device_id=(gx, ty, tz),
            device_id_type=MESH,
        )
        c.start()
        gd_copies.append(c)
    total = bds[gz].astype(F32)
    for k, c in enumerate(bd_copies, 1):
        c.wait()
        total = total + bdr[lax.rem(gz - k + nz, nz)].astype(F32)
    b2s[...] = total.astype(BF16)
    sheets.sort(key=lambda p: -2 * min(p[1], ny - p[1]) - min(p[0], nx - p[0]))
    b2_copies = []
    for k, (dx, dy, _) in enumerate(sheets):
        tx, ty = lax.rem(gx + dx, nx), lax.rem(gy + dy, ny)
        c = pltpu.make_async_remote_copy(
            src_ref=b2s.at[ty // 2, tx],
            dst_ref=b2r.at[gx * ny + gy],
            send_sem=s10.at[k],
            recv_sem=r10.at[k],
            device_id=(tx, ty, gz),
            device_id_type=MESH,
        )
        c.start()
        b2_copies.append(c)
    total = gb2s[gy].astype(F32)
    for k, c in enumerate(gb2_copies, 1):
        c.wait()
        total = total + gb2r[lax.rem(gy - k + ny, ny)].astype(F32)
    gbot_o[...] = total[:, 0:108]
    total = gds[me].astype(F32)
    for c in gd_copies:
        c.wait()
    for k, (_, dy, dz) in enumerate(planes):
        source = lax.rem(gy - dy + ny, ny) * nz + lax.rem(gz - dz + nz, nz)
        total = total + gdr[source].astype(F32)
    gdown_o[0:8, :] = total[:, 0:54]
    total = b2s[gy // 2, gx].astype(F32)
    for c in b2_copies:
        c.wait()
    for k, (dx, dy, _) in enumerate(sheets):
        source = lax.rem(gx - dx + nx, nx) * ny + lax.rem(gy - dy + ny, ny)
        total = total + b2r[source].astype(F32)
    total = jnp.where(lax.rem(gy, 2) == 1, pltpu.roll(total, 64, 1), total)
    gdown_o[8:16, :] = total[:, 0:54]


def put_out(a, b, c, a_out, b_out, c_out, sems):
    copies = [
        pltpu.make_async_copy(source, out, sems.at[i])
        for i, (source, out) in enumerate([(a, a_out), (b, b_out), (c, c_out)])
    ]
    for copy in copies:
        copy.start()
    for copy in copies:
        copy.wait()


def per_device(sizes, fields, grain_ids, table, w_in, k_fine, k_down, k_bot, cotangent):
    nx, ny, nz = sizes
    n = ny * nz
    cot = cotangent.transpose(0, 2, 3, 1)
    vmem = pl.BlockSpec(memory_space=pltpu.VMEM)
    V = pltpu.VMEM
    D = pltpu.SemaphoreType.DMA
    scratch = [
        V((7, 8, 8, 16), BF16),
        V((8, 8, 16), jnp.int32),
        V((64, 128), BF16),
        V((7, 64), BF16),
        V((64, 1728), BF16),
        V((32, 4, 8, 32), BF16),
        V((1024, 128), F32),
        V((256, 128), F32),
        V((128, 512), BF16),
        V((1024, 128), F32),
        V((64, 128), F32),
        V((8, 2, 4, 1, 128), F32),
        V((11, 4, 8, 1, 128), F32),
        V((11, 16, 32, 128), F32),
        V((312, 640), BF16),
        V((11, 312, 256), F32),
        V((9, 13, 40, 128), F32),
        V((13, 24, 128), F32),
        V((256, 640), BF16),
        V((1792, 128), BF16),
        V((128, 1152), BF16),
        V((1792, 256), BF16),
        V((96, 1792), BF16),
        V((128, 1792), BF16),
        V((4, 6, 16, 128), F32),
        V((4, 64, 128), F32),
        V((4, 64, 128), BF16),
        V((nx, 4, 64, 128), BF16),
        V((nx, 64, 128), F32),
        V((36, 32, 1152), BF16),
        V((36, 32, 128), F32),
        V((256, 128), F32),
        V((256, 128), F32),
        V((96, 1152), BF16),
        V((2, 64, 128), BF16),
        V((2, 32, 128), BF16),
        V((4, 16, 128), BF16),
        V((2, 64, 128), BF16),
        V((2, 32, 128), BF16),
        V((4, 16, 128), BF16),
        V((10, 6, 16, 128), F32),
        V((10, 6, 16, 128), F32),
        V((2, 256, 1792), BF16),
        V((nx, 128, 128), BF16),
        V((nx, 128, 128), BF16),
        V((nx, 8, 1792), BF16),
        V((nx, 8, 1792), BF16),
        V((8, 1792), F32),
        V((8 * nx, 1792), F32),
        V((nz, ny // 2, nx, 8, 128), BF16),
        V((nz, ny // 2, nx, 8, 128), BF16),
        V((ny // 2, nx, 8, 128), BF16),
        V((nx * ny, 8, 128), BF16),
        V((96, 1152), F32),
        V((nz, ny, 32, 128), BF16),
        V((nz, ny, 32, 128), BF16),
        V((ny, 32, 128), BF16),
        V((ny, 32, 128), BF16),
        V((n, 8, 128), BF16),
        V((n, 8, 128), BF16),
        D((12,)),
        D((26,)),
        D((26,)),
        D((4, nx)),
        D((4, nx)),
        D((8,)),
        D((8,)),
        D((nx,)),
        D((nx,)),
        D((nx,)),
        D((nx,)),
        D((nz,)),
        D((nz,)),
        D((n,)),
        D((n,)),
        D((ny,)),
        D((ny,)),
        D((nz,)),
        D((nz,)),
        D((nx * ny,)),
        D((nx * ny,)),
    ]
    bottle, grad_down, grad_bottle = pl.pallas_call(
        functools.partial(body, sizes),
        out_shape=(
            V((32, 4, 8, 32), BF16),
            V((16, 54), F32),
            V((32, 108), F32),
        ),
        in_specs=[pl.BlockSpec(memory_space=pl.ANY)] * 8,
        out_specs=(vmem, vmem, vmem),
        scratch_shapes=scratch,
        compiler_params=pltpu.CompilerParams(
            collective_id=0, has_side_effects=True, vmem_limit_bytes=60 * 1024 * 1024
        ),
    )(fields, grain_ids, table.T, w_in.T, k_fine, k_down.T, k_bot, cot)
    bottle, grad_down, grad_bottle = pl.pallas_call(
        put_out,
        out_shape=(
            jax.ShapeDtypeStruct((32, 4, 8, 32), BF16),
            jax.ShapeDtypeStruct((16, 54), F32),
            jax.ShapeDtypeStruct((32, 108), F32),
        ),
        in_specs=[vmem] * 3,
        out_specs=[pl.BlockSpec(memory_space=pl.ANY)] * 3,
        scratch_shapes=[D((3,))],
        compiler_params=pltpu.CompilerParams(vmem_limit_bytes=1024 * 1024),
    )(bottle, grad_down, grad_bottle)
    return bottle.transpose(0, 3, 1, 2), grad_down, grad_bottle


def solution(mesh):
    sizes = (mesh.shape["gx"], mesh.shape["gy"], mesh.shape["gz"])
    placed = (
        P(None, "gx", "gy", "gz"),
        P("gx", "gy", "gz"),
        P(),
        P(),
        P(),
        P(),
        P("gx", None),
        P("gx", None, "gy", "gz"),
    )
    return jax.shard_map(
        functools.partial(per_device, sizes),
        mesh=mesh,
        in_specs=placed,
        out_specs=(P("gx", None, "gy", "gz"), P("gx", ("gy", "gz")), P("gx", ("gy", "gz"))),
        check_vma=False,
    )
```

```python
import functools
import math

import jax
import jax.numpy as jnp
from jax import lax
from jax.experimental import pallas as pl
from jax.experimental.pallas import tpu as pltpu
from jax.sharding import PartitionSpec as P

MESH = pl.DeviceIdType.MESH
F32 = jnp.float32
BF16 = jnp.bfloat16
NT = (((1,), (1,)), ((), ()))


def silu(v):
    return v * jax.nn.sigmoid(v)


def silu_grad(v):
    s = jax.nn.sigmoid(v)
    return s * (1.0 + v * (1.0 - s))


def dot(a, b):
    return jnp.dot(a, b, preferred_element_type=F32)


def dot_nt(a, b):
    return lax.dot_general(a, b, NT, preferred_element_type=F32)


def tap_of(t):
    t = min(t, 26)
    return t // 9, (t // 3) % 3, t % 3


def lane_iota(shape):
    return lax.broadcasted_iota(jnp.int32, shape, len(shape) - 1)


def piece(ref_tiles, start, width):
    tile, shift = start // 128, start % 128
    low = ref_tiles(tile)
    if shift == 0:
        return low
    low = pltpu.roll(low, 128 - shift, 1)
    if shift + width <= 128:
        return low
    high = pltpu.roll(ref_tiles(tile + 1), 128 - shift, 1)
    return jnp.where(lane_iota(low.shape) < 128 - shift, low, high)


def body(
    sizes,
    fields_h,
    ids_h,
    table_h,
    w_in_h,
    k_fine_h,
    k_down_h,
    k_bot_h,
    cot_h,
    bottle_o,
    gdown_o,
    gbot_o,
    fields,
    ids,
    table,
    w_in,
    k_fine,
    cot,
    cotf,
    cotp,
    tt,
    bo,
    raw,
    brick,
    ext,
    es,
    af,
    yf,
    fs,
    fmask,
    kf,
    kd,
    kb,
    wblk,
    ac,
    ad,
    pd,
    cb,
    cs,
    sb,
    slab,
    a3,
    ysum,
    pre,
    gp,
    gt,
    ysend,
    zsend,
    csend,
    yrecv,
    zrecv,
    crecv,
    gpad,
    gpadr,
    ag,
    acts,
    actr,
    downs,
    downr,
    dsum,
    dpart,
    bds,
    bdr,
    b2s,
    b2r,
    gball,
    gbs,
    gbr,
    gb2s,
    gb2r,
    gds,
    gdr,
    sem_l,
    s1,
    r1,
    s2,
    r2,
    s3,
    r3,
    s4,
    r4,
    s5,
    r5,
    s6,
    r6,
    s7,
    r7,
    s8,
    r8,
    s9,
    r9,
    s10,
    r10,
):
    nx, ny, nz = sizes
    gx, gy, gz = lax.axis_index("gx"), lax.axis_index("gy"), lax.axis_index("gz")
    scale = 1.0 / math.sqrt(nx * 4 * ny * 4 * nz * 8)

    def device(dx, dy, dz):
        return (lax.rem(gx + dx + nx, nx), lax.rem(gy + dy + ny, ny), lax.rem(gz + dz + nz, nz))

    near = [(dx, dy, dz) for dx in (-1, 0, 1) for dy in (-1, 0, 1) for dz in (-1, 0, 1)]
    near = sorted([n for n in near if n != (0, 0, 0)], key=lambda n: abs(n[0]))
    columns = [(dx, 0, 0) for dx in range(1, nx)]
    planes = [(0, dy, dz) for dy in range(ny) for dz in range(nz) if (dy, dz) != (0, 0)]
    sheets = [(dx, dy, 0) for dx in range(nx) for dy in range(ny) if (dx, dy) != (0, 0)]
    partners = sorted({(a % nx, b % ny, c % nz) for a, b, c in near + columns + [(0, 0, nz // 2)]})
    partners.sort(key=lambda p: -2 * min(p[1], ny - p[1]) - min(p[2], nz - p[2]) - min(p[0], nx - p[0]))
    barrier = pltpu.get_barrier_semaphore()
    for p in partners:
        pl.semaphore_signal(barrier, inc=1, device_id=device(*p), device_id_type=MESH)

    loads = [
        pltpu.make_async_copy(src, dst, sem_l.at[1 + i])
        for i, (src, dst) in enumerate(
            [(fields_h, fields), (ids_h, ids), (table_h, table), (w_in_h, w_in), (k_fine_h, k_fine)]
            + [(k_down_h, kd.at[0:1728]), (cot_h, cot)]
            + [
                (k_bot_h.at[:, x * 1152 : x * 1152 + 1152], kb.at[32 * x : 32 * x + 32])
                for x in range(3)
            ]
        )
    ]
    for c in loads:
        c.start()
    kd[1728:1792, :] = jnp.zeros((64, 128), BF16)
    kb[96:128, :] = jnp.zeros((32, 1152), BF16)
    kf[...] = jnp.zeros(kf.shape, BF16)
    wblk[...] = jnp.zeros(wblk.shape, BF16)
    fs[...] = jnp.zeros(fs.shape, F32)
    gpad[...] = jnp.zeros(gpad.shape, F32)
    a3[0] = jnp.zeros((32, 1152), BF16)
    a3[4 * nx + 1 : 4 * nx + 4] = jnp.zeros((3, 32, 1152), BF16)
    ysum[0] = jnp.zeros((32, 128), F32)
    ysum[4 * nx + 1] = jnp.zeros((32, 128), F32)
    cb[...] = jnp.zeros(cb.shape, F32)
    cotf[...] = jnp.zeros(cotf.shape, F32)
    ext[:, :, 6:8] = jnp.zeros((11, 4, 2, 1, 128), F32)
    for c in loads[0:2]:
        c.wait()

    sel_row = lax.broadcasted_iota(jnp.int32, (16, 128), 0)
    sel_lane = lax.broadcasted_iota(jnp.int32, (16, 128), 1)
    packed = jnp.zeros((64, 128), F32)
    for ch in range(8):
        plane = (fields[ch] if ch < 7 else ids[...]).astype(F32).reshape(64, 16).astype(BF16)
        select = jnp.where(sel_lane == sel_row * 8 + ch, 1.0, 0.0).astype(BF16)
        packed = packed + dot(plane, select)
    raw[...] = packed
    group = lane_iota((16, 128)) // 32
    for zb in range(4):
        block = None
        for y4 in range(4):
            rows = raw[pl.ds(y4, 16, stride=4), :]
            shift = ((y4 - zb) * 32) % 128
            rows = rows if shift == 0 else pltpu.roll(rows, shift, 1)
            block = rows if block is None else jnp.where(group == y4, rows, block)
        for r in range(16):
            brick[r // 2, r % 2, zb, :, :] = block[r : r + 1, :]

    for c in loads[2:]:
        c.wait()
    lane = lane_iota((64, 640))
    first = jnp.where(lane < 576, k_fine[:, 0:640].astype(F32), 0.0)
    second = pltpu.roll(k_fine[:, 512:1152].astype(F32), 576, 1)
    kf[0:64, :] = first.astype(BF16)
    kf[64:128, :] = jnp.where(lane < 576, second, 0.0).astype(BF16)
    for n in (128, 192):
        kf[n : n + 64, 0:576] = k_fine[:, 1152:1728]
    for t in range(27):
        for q in range(2):
            row = t * 64 + q * 32
            wblk[row : row + 32, q * 128 : q * 128 + 128] = kb[
                (t // 9) * 32 : (t // 9) * 32 + 32, (t % 9) * 128 : (t % 9) * 128 + 128
            ]
    my = gy * 8 - 3 + lax.broadcasted_iota(jnp.int32, (13, 24, 128), 0)
    mz = gz * 16 - 3 + lax.broadcasted_iota(jnp.int32, (13, 24, 128), 1)
    inside = (my >= 0) & (my < ny * 8) & (mz >= 0) & (mz < nz * 16)
    fmask[...] = jnp.where(inside, 1.0, 0.0)

    pl.semaphore_wait(barrier, len(partners))

    x_src = {1: (6, 2, 0), 0: (0, 8, 2), -1: (0, 1, 10)}
    y_src = {1: (1, 1, 0), 0: (0, 2, 1), -1: (0, 1, 3)}
    z_src = {1: (3, 1, 0), 0: (0, 4, 1), -1: (0, 1, 5)}
    halo = []
    for number, (dx, dy, dz) in enumerate(near):
        (xs, xn, xd), (ys, yn, yd), (zs, zn, zd) = x_src[dx], y_src[dy], z_src[dz]
        halo.append(
            pltpu.make_async_remote_copy(
                src_ref=brick.at[xs : xs + xn, ys : ys + yn, zs : zs + zn],
                dst_ref=ext.at[xd : xd + xn, yd : yd + yn, zd : zd + zn],
                send_sem=s1.at[number],
                recv_sem=r1.at[number],
                device_id=device(dx, dy, dz),
                device_id_type=MESH,
            )
        )
    for c in halo:
        c.start()
    own = pltpu.make_async_copy(brick, ext.at[2:10, 1:3, 1:5], sem_l.at[0])
    own.start()

    row8 = lax.broadcasted_iota(jnp.int32, (128, 7), 0) % 8
    pick = jnp.where(row8 == lax.broadcasted_iota(jnp.int32, (128, 7), 1), 1.0, 0.0).astype(BF16)
    emb_lane = lane_iota((128, 128)) // 8
    twice = jnp.where(
        lax.broadcasted_iota(jnp.int32, (64, 128), 1) % 64
        == lax.broadcasted_iota(jnp.int32, (64, 128), 0),
        1.0,
        0.0,
    ).astype(BF16)
    w_rows = dot(pick, dot(w_in[...], twice).astype(BF16))
    table2 = jnp.concatenate([table[...]] * 2, axis=0)
    w_cols = jnp.transpose(w_rows)

    own.wait()
    for c, n in zip(halo, near):
        if n[0] == 0:
            c.wait()

    by = lax.broadcasted_iota(jnp.int32, (4, 8, 128), 0)
    bz = lax.broadcasted_iota(jnp.int32, (4, 8, 128), 1)
    outside = ((by == 0) & (gy == 0)) | ((by == 3) & (gy == ny - 1))
    outside = outside | ((bz == 0) & (gz == 0)) | ((bz == 5) & (gz == nz - 1))
    fill = jnp.where(lane_iota((4, 8, 128)) % 8 == 7, -1.0, 0.0)

    def embed(planes_x):
        rows = len(planes_x) * 32
        blocks = []
        for x in planes_x:
            block = jnp.where(outside, fill, ext[x].reshape(4, 8, 128))
            if x < 2:
                block = jnp.where(gx == 0, fill, block)
            if x == 10:
                block = jnp.where(gx == nx - 1, fill, block)
            blocks.append(block)
        blocks = jnp.concatenate(blocks, axis=0).reshape(rows, 128)
        components = blocks.astype(BF16)
        lanes = lane_iota((rows, 128)).astype(F32)
        for p in range(16):
            y4, z4 = p // 4, p % 4
            w_p = jnp.where(emb_lane == p, w_cols, 0.0).astype(BF16)
            grain = jnp.broadcast_to(blocks[:, p * 8 + 7 : p * 8 + 8], (rows, 128))
            onehot = jnp.where(grain == lanes, 1.0, 0.0).astype(BF16)
            both = jnp.concatenate([onehot, components], axis=1)
            value = silu(dot_nt(both, jnp.concatenate([table2, w_p], axis=1)))
            value = value.reshape(len(planes_x), 4, 8, 128)
            for i, x in enumerate(planes_x):
                for yb in range(4):
                    es[x, yb * 4 + y4, pl.ds(z4, 8, stride=4), :] = value[i, yb]

    half = lane_iota((13, 24, 128)) < 64

    def spread_plane(e):
        for t in range(5):
            ay, az = (2 * t) // 3, (2 * t) % 3
            by_, bz_ = min(2 * t + 1, 8) // 3, min(2 * t + 1, 8) % 3
            low = es[e, ay : ay + 13, az : az + 24, :]
            high = es[e, by_ : by_ + 13, bz_ : bz_ + 24, :]
            block = jnp.where(half, low, high)
            af[:, t * 128 : t * 128 + 128] = block.reshape(312, 128).astype(BF16)
        yf[e] = dot_nt(af[...], kf[...])

    half_rows = lane_iota((312, 128)) < 64

    def spread_planes(e, carry):
        spread_plane(e)
        return carry

    def next_plane(x, carry):
        fine_plane(x)
        return carry

    def fine_plane(x):
        two = jnp.where(half_rows, yf[x, :, 0:128], yf[x + 1, :, 0:128])
        value = two + pltpu.roll(two, 64, 1) + yf[x + 2, :, 128:256]
        value = silu(value).reshape(13, 24, 128)
        keep = jnp.where((x > 0) | (gx > 0), 1.0, 0.0)
        value = value * fmask[...] * keep
        fs[x, :, 0:24, :] = value.astype(BF16).astype(F32)

    def coarse_copy(x, k):
        return pltpu.make_async_remote_copy(
            src_ref=cs.at[x],
            dst_ref=sb.at[gx, x],
            send_sem=s2.at[x, k],
            recv_sem=r2.at[x, k],
            device_id=device(k, 0, 0),
            device_id_type=MESH,
        )

    half16 = lane_iota((16, 128)) < 64
    cy = gy * 4 - 1 + lax.broadcasted_iota(jnp.int32, (6, 16, 128), 0)
    cz = gz * 8 - 1 + lax.broadcasted_iota(jnp.int32, (6, 16, 128), 1)
    inside = (cy >= 0) & (cy < ny * 4) & (cz >= 0) & (cz < nz * 8)

    def coarse_plane(x, carry):
        lax.fori_loop(2 * x + 1, 2 * x + 3, next_plane, 0)
        for y in range(6):
            row = y * 16
            for t in range(14):
                (ax, ay, az), (bx_, by_, bz_) = tap_of(2 * t), tap_of(2 * t + 1)
                low = fs[2 * x + ax, 2 * y + ay, pl.ds(az, 16, stride=2), :]
                high = fs[2 * x + bx_, 2 * y + by_, pl.ds(bz_, 16, stride=2), :]
                ac[row : row + 16, t * 128 : t * 128 + 128] = jnp.where(half16, low, high).astype(BF16)
        before = dot(ac[...], kd[...]).reshape(6, 16, 128)
        pd[x] = before
        coarse = jnp.where(inside, silu(before), 0.0)
        for y in range(6):
            cb[x, y * 10 : y * 10 + 10, :] = coarse[y, 0:10, :]
        cs[x] = cb[x].astype(BF16)
        sb[gx, x] = cb[x].astype(BF16)
        for k in range(1, nx):
            coarse_copy(x, k).start()

        @pl.when(x < 3)
        def _():
            lax.fori_loop(2 * x + 5, 2 * x + 7, spread_planes, 0)

        return carry

    embed(range(2, 10))
    lax.fori_loop(2, 5, spread_planes, 0)
    for c, n in zip(halo, near):
        if n[0] != 0:
            c.wait()
    embed((0, 1, 10))

    lax.fori_loop(0, 2, spread_planes, 0)
    fine_plane(0)
    lax.fori_loop(0, 4, coarse_plane, 0)

    half8 = lane_iota((8, 128)) < 64
    for x in range(4):
        for t in range(14):
            (ax, ay, az), (bx_, by_, bz_) = tap_of(2 * t), tap_of(2 * t + 1)
            parts = []
            for y in range(4):
                low = fs[2 * x + ax, 2 * y + 2 + ay, pl.ds(2 + az, 8, stride=2), :]
                high = fs[2 * x + bx_, 2 * y + 2 + by_, pl.ds(2 + bz_, 8, stride=2), :]
                parts.append(jnp.where(half8, low, high))
            ad[x * 32 : x * 32 + 32, t * 128 : t * 128 + 128] = jnp.concatenate(parts, axis=0).astype(BF16)


    cotf[:, 0:32] = cot[...].astype(F32).reshape(1024, 32)
    group = lane_iota((32, 128)) // 8
    spread = lax.broadcasted_iota(jnp.int32, (8, 128), 0)
    spread = jnp.where(lane_iota((8, 128)) % 8 == spread, 1.0, 0.0).astype(BF16)
    for y in range(4):
        for z in range(8):
            rows = cotf[pl.ds(y * 8 + z, 32, stride=32), :]
            rows = jnp.concatenate([jnp.where(group == q, rows, 0.0) for q in range(4)], axis=0)
            cotp[pl.ds(y * 8 + z, 8, stride=32), :] = dot_nt(spread, rows.astype(BF16))

    def bottle_plane(x, carry):
        for k in range(1, nx):
            coarse_copy(x, k).wait()
        slab[...] = sb[:, x].astype(F32)
        for pair in range(2):
            for t in range(9):
                start = (2 * pair + t // 3) * 10 + t % 3
                window = [slab[:, start : start + 8, :], slab[:, start + 10 : start + 18, :]]
                window = jnp.concatenate(window, axis=1).astype(BF16)
                for n in range(nx):
                    a3[1 + 4 * n + x, pair * 16 : pair * 16 + 16, t * 128 : t * 128 + 128] = window[n]
        part = jnp.concatenate([a3[1 + 4 * n + x] for n in range(nx)], axis=0)
        part = dot_nt(part, kb[...]).reshape(nx, 32, 128)
        for n in range(nx):
            ysum[1 + 4 * n + x] = part[n]
        return carry

    lax.fori_loop(0, 4, bottle_plane, 0)
    group = lane_iota((256, 128)) // 32
    z = None
    for ax in range(3):
        term = None
        for q in range(4):
            rows = ysum[8 * q + ax : 8 * q + ax + 8].reshape(256, 128)
            shift = ((q - ax) * 32) % 128
            rows = rows if shift == 0 else pltpu.roll(rows, shift, 1)
            term = rows if term is None else jnp.where(group == q, rows, term)
        z = term if z is None else z + term
    pre[...] = z
    grad = cotp[...] * silu_grad(z)
    grad = grad.astype(BF16).astype(F32)
    gp[...] = grad

    for side in range(2):
        row = 3 - 3 * side
        ysend[side] = grad.reshape(8, 32, 128)[:, row * 8 : row * 8 + 8].reshape(64, 128).astype(BF16)
        zsend[side] = gp[pl.ds(7 - 7 * side, 32, stride=8), :].astype(BF16)
        for other in range(2):
            corner = gp[pl.ds(row * 8 + 7 - 7 * other, 8, stride=32), :]
            csend[side * 2 + other] = jnp.concatenate([corner, corner], axis=0).astype(BF16)
    rim = []

    def rim_copy(src, dst, number, dy, dz):
        c = pltpu.make_async_remote_copy(
            src_ref=src,
            dst_ref=dst,
            send_sem=s3.at[number],
            recv_sem=r3.at[number],
            device_id=device(0, dy, dz),
            device_id_type=MESH,
        )
        c.start()
        rim.append(c)

    for side in range(2):
        rim_copy(ysend.at[side], yrecv.at[side], side, 1 - 2 * side, 0)
    for side in range(2):
        rim_copy(zsend.at[side], zrecv.at[side], 2 + side, 0, 1 - 2 * side)
    for corner in range(4):
        rim_copy(
            csend.at[corner],
            crecv.at[corner],
            4 + corner,
            1 - 2 * (corner // 2),
            1 - 2 * (corner % 2),
        )

    turned = jnp.transpose(grad)
    turned = [turned[32 * q : 32 * q + 32] for q in range(4)] + [jnp.zeros((32, 128), F32)]
    turned = jnp.concatenate(turned, axis=1)
    turned = [turned, pltpu.roll(turned, 32, 1), pltpu.roll(turned, 64, 1)]
    gt[...] = jnp.concatenate(turned, axis=0).astype(BF16)
    for n in range(3):
        columns_n = a3[:, :, n * 384 : n * 384 + 384].reshape(1152, 384)
        gball[:, n * 384 : n * 384 + 384] = dot(gt[...], columns_n) * scale

    def gball_tile(tile):
        row, lane = (tile // 9) * 32, (tile % 9) * 128
        return gball[row : row + 32, lane : lane + 128]

    for k in range(ny * nz):
        cut = piece(gball_tile, 108 * k, 108)
        gbs[k % nz, k // nz] = cut.astype(BF16)
    me = gy * nz + gz
    gb_copies = []
    for k in range(1, nz):
        target = lax.rem(gz + k, nz)
        gb_copies.append(
            pltpu.make_async_remote_copy(
                src_ref=gbs.at[target],
                dst_ref=gbr.at[gz],
                send_sem=s6.at[k],
                recv_sem=r6.at[k],
                device_id=(gx, gy, target),
                device_id_type=MESH,
            )
        )

    gpad[1:9, 1:5, 1:9, :] = gp[...].reshape(8, 4, 8, 128)
    for c in rim:
        c.wait()
    for c in gb_copies:
        c.start()

    def kept(flag, value):
        return jnp.where(flag, value.astype(F32), 0.0)

    y_ok = (gy > 0, gy < ny - 1)
    z_ok = (gz > 0, gz < nz - 1)
    for side in range(2):
        gpad[1:9, 5 * side, 1:9, :] = kept(y_ok[side], yrecv[side]).reshape(8, 8, 128)
        value = kept(z_ok[side], zrecv[side])
        gpad[1:9, 1:5, 9 * side : 9 * side + 1, :] = value.reshape(8, 4, 1, 128)
        for other in range(2):
            value = kept(y_ok[side] & z_ok[other], crecv[side * 2 + other])
            gpad[1:9, 5 * side, 9 * other : 9 * other + 1, :] = value[0:8].reshape(8, 1, 128)
    edge = lane_iota((96, 128))
    low = pltpu.roll(gpad[8].reshape(96, 128), 32, 1)
    gpad[0] = jnp.where(edge < 32, 0.0, low).reshape(6, 16, 128)
    high = pltpu.roll(gpad[1].reshape(96, 128), 96, 1)
    gpad[9] = jnp.where(edge >= 96, 0.0, high).reshape(6, 16, 128)
    gpadr[...] = pltpu.roll(gpad[...].reshape(960, 128), 64, 1).reshape(10, 6, 16, 128)

    def grad_window(ref, t):
        ax, ay, az = tap_of(t)
        window = ref[2 - ax : 10 - ax, 2 - ay : 6 - ay, 2 - az : 10 - az, :]
        return window.reshape(256, 128)

    half_rows = lane_iota((256, 128)) < 64
    for t in range(14):
        for pair, (one, two) in enumerate([(gpad, gpadr), (gpadr, gpad)]):
            window = jnp.where(half_rows, grad_window(one, 2 * t), grad_window(two, 2 * t + 1))
            ag[pair, :, t * 128 : t * 128 + 128] = window.astype(BF16)
    def act_copy(slot, target, source):
        return pltpu.make_async_remote_copy(
            src_ref=acts.at[target],
            dst_ref=actr.at[slot],
            send_sem=s4.at[target],
            recv_sem=r4.at[source],
            device_id=(target, gy, gz),
            device_id_type=MESH,
        )

    for pair in range(2):
        act = dot(ag[pair], wblk[...]).astype(BF16)
        for part in range(4):
            target = 4 * pair + part
            row, lane = (part % 2) * 128, (part // 2) * 128
            acts[target] = act[row : row + 128, lane : lane + 128]

            @pl.when(gx != target)
            def _(target=target):
                act_copy(gx, target, gx).start()

    out = silu(pre[...]).astype(BF16).astype(F32).reshape(8, 4, 8, 128)
    for y in range(4):
        turned = jnp.transpose(jnp.concatenate([out[:, y].reshape(64, 128), jnp.zeros((64, 128), F32)], axis=0))
        for q in range(4):
            tt[y * 32 : y * 32 + 32, q * 128 : q * 128 + 128] = turned[q * 32 : q * 32 + 32].astype(BF16)
    row = lax.broadcasted_iota(jnp.int32, (512, 128), 0)
    x_of = (row // 128) * 8 + (row % 128) // 8
    x_of = jnp.where(row % 128 < 64, x_of, -1)
    for k in range(8):
        select = jnp.where((x_of == lane_iota((512, 128))) & (row % 8 == k), 1.0, 0.0).astype(BF16)
        turned = dot(tt[...], select)
        for y in range(4):
            bo[pl.ds(y * 8 + k, 32, stride=32), :] = turned[y * 32 : y * 32 + 32]
    bottle_o[...] = bo[...].reshape(32, 4, 8, 128)[:, :, :, 0:32].astype(BF16)

    slope = [silu_grad(pd[x, y + 1, 1:9, :]) for x in range(4) for y in range(4)]
    slope = jnp.concatenate(slope, axis=0)
    total = acts[gx].astype(F32)
    for k in range(1, nx):
        source = lax.rem(gx - k + nx, nx)
        act_copy(source, lax.rem(gx + k, nx), source).wait()
        total = total + actr[source].astype(F32)
    grad_down = (total * slope).astype(BF16).astype(F32)
    grad_down_t = jnp.transpose(grad_down).astype(BF16)

    part = dot(grad_down_t, ad[...]) * scale
    part = part.reshape(nx, 16, 1792)
    downs[...] = part[:, 0:8].astype(BF16)
    dpart[...] = part[:, 8:16].reshape(8 * nx, 1792)
    down_copies = []
    for k in range(1, nx):
        target = lax.rem(gx + k, nx)
        down_copies.append(
            pltpu.make_async_remote_copy(
                src_ref=downs.at[target],
                dst_ref=downr.at[gx],
                send_sem=s5.at[k],
                recv_sem=r5.at[k],
                device_id=(target, gy, gz),
                device_id_type=MESH,
            )
        )
    for c in down_copies:
        c.start()

    low_half = lane_iota((8 * nx, 128)) < 64
    for k in range(ny * nz // 2):
        tz, pair = k % nz, k // nz
        low = piece(lambda tile: dpart[:, tile * 128 : tile * 128 + 128], 54 * (2 * pair * nz + tz), 54)
        high = 54 * ((2 * pair + 1) * nz + tz) - 64
        high = piece(lambda tile: dpart[:, tile * 128 : tile * 128 + 128], high, 118)
        bds[tz, pair] = jnp.where(low_half, low, high).reshape(nx, 8, 128).astype(BF16)
    bd_copies = []
    for k in range(1, nz):
        target = lax.rem(gz + k, nz)
        c = pltpu.make_async_remote_copy(
            src_ref=bds.at[target],
            dst_ref=bdr.at[gz],
            send_sem=s9.at[k],
            recv_sem=r9.at[k],
            device_id=(gx, gy, target),
            device_id_type=MESH,
        )
        c.start()
        bd_copies.append(c)

    total = gbs[gz].astype(F32)
    for k, c in enumerate(gb_copies, 1):
        c.wait()
        total = total + gbr[lax.rem(gz - k + nz, nz)].astype(F32)
    gb2s[...] = total.astype(BF16)
    gb2_copies = []
    for k in range(1, ny):
        target = lax.rem(gy + k, ny)
        c = pltpu.make_async_remote_copy(
            src_ref=gb2s.at[target],
            dst_ref=gb2r.at[gy],
            send_sem=s8.at[k],
            recv_sem=r8.at[k],
            device_id=(gx, target, gz),
            device_id_type=MESH,
        )
        c.start()
        gb2_copies.append(c)

    dsum[...] = downs[gx].astype(F32)
    for k, c in enumerate(down_copies, 1):
        c.wait()
        dsum[...] += downr[lax.rem(gx - k + nx, nx)].astype(F32)
    for k in range(ny * nz):
        gds[k] = piece(lambda tile: dsum[:, tile * 128 : tile * 128 + 128], 54 * k, 54).astype(BF16)
    gd_copies = []
    planes.sort(key=lambda p: -2 * min(p[1], ny - p[1]) - min(p[2], nz - p[2]))
    for k, (_, dy, dz) in enumerate(planes):
        ty, tz = lax.rem(gy + dy, ny), lax.rem(gz + dz, nz)
        c = pltpu.make_async_remote_copy(
            src_ref=gds.at[ty * nz + tz],
            dst_ref=gdr.at[me],
            send_sem=s7.at[k],
            recv_sem=r7.at[k],
            device_id=(gx, ty, tz),
            device_id_type=MESH,
        )
        c.start()
        gd_copies.append(c)
    total = bds[gz].astype(F32)
    for k, c in enumerate(bd_copies, 1):
        c.wait()
        total = total + bdr[lax.rem(gz - k + nz, nz)].astype(F32)
    b2s[...] = total.astype(BF16)
    sheets.sort(key=lambda p: -2 * min(p[1], ny - p[1]) - min(p[0], nx - p[0]))
    b2_copies = []
    for k, (dx, dy, _) in enumerate(sheets):
        tx, ty = lax.rem(gx + dx, nx), lax.rem(gy + dy, ny)
        c = pltpu.make_async_remote_copy(
            src_ref=b2s.at[ty // 2, tx],
            dst_ref=b2r.at[gx * ny + gy],
            send_sem=s10.at[k],
            recv_sem=r10.at[k],
            device_id=(tx, ty, gz),
            device_id_type=MESH,
        )
        c.start()
        b2_copies.append(c)
    total = gb2s[gy].astype(F32)
    for k, c in enumerate(gb2_copies, 1):
        c.wait()
        total = total + gb2r[lax.rem(gy - k + ny, ny)].astype(F32)
    gbot_o[...] = total[:, 0:108]
    total = gds[me].astype(F32)
    for c in gd_copies:
        c.wait()
    for k, (_, dy, dz) in enumerate(planes):
        source = lax.rem(gy - dy + ny, ny) * nz + lax.rem(gz - dz + nz, nz)
        total = total + gdr[source].astype(F32)
    gdown_o[0:8, :] = total[:, 0:54]
    total = b2s[gy // 2, gx].astype(F32)
    for c in b2_copies:
        c.wait()
    for k, (dx, dy, _) in enumerate(sheets):
        source = lax.rem(gx - dx + nx, nx) * ny + lax.rem(gy - dy + ny, ny)
        total = total + b2r[source].astype(F32)
    total = jnp.where(lax.rem(gy, 2) == 1, pltpu.roll(total, 64, 1), total)
    gdown_o[8:16, :] = total[:, 0:54]


def put_out(a, b, c, a_out, b_out, c_out, sems):
    copies = [
        pltpu.make_async_copy(source, out, sems.at[i])
        for i, (source, out) in enumerate([(a, a_out), (b, b_out), (c, c_out)])
    ]
    for copy in copies:
        copy.start()
    for copy in copies:
        copy.wait()


def per_device(sizes, fields, grain_ids, table, w_in, k_fine, k_down, k_bot, cotangent):
    nx, ny, nz = sizes
    n = ny * nz
    cot = cotangent.transpose(0, 2, 3, 1)
    vmem = pl.BlockSpec(memory_space=pltpu.VMEM)
    V = pltpu.VMEM
    D = pltpu.SemaphoreType.DMA
    scratch = [
        V((7, 8, 8, 16), BF16),
        V((8, 8, 16), jnp.int32),
        V((64, 128), BF16),
        V((7, 64), BF16),
        V((64, 1728), BF16),
        V((32, 4, 8, 32), BF16),
        V((1024, 128), F32),
        V((256, 128), F32),
        V((128, 512), BF16),
        V((1024, 128), F32),
        V((64, 128), F32),
        V((8, 2, 4, 1, 128), F32),
        V((11, 4, 8, 1, 128), F32),
        V((11, 16, 32, 128), F32),
        V((312, 640), BF16),
        V((11, 312, 256), F32),
        V((9, 13, 40, 128), F32),
        V((13, 24, 128), F32),
        V((256, 640), BF16),
        V((1792, 128), BF16),
        V((128, 1152), BF16),
        V((1792, 256), BF16),
        V((96, 1792), BF16),
        V((128, 1792), BF16),
        V((4, 6, 16, 128), F32),
        V((4, 64, 128), F32),
        V((4, 64, 128), BF16),
        V((nx, 4, 64, 128), BF16),
        V((nx, 64, 128), F32),
        V((36, 32, 1152), BF16),
        V((36, 32, 128), F32),
        V((256, 128), F32),
        V((256, 128), F32),
        V((96, 1152), BF16),
        V((2, 64, 128), BF16),
        V((2, 32, 128), BF16),
        V((4, 16, 128), BF16),
        V((2, 64, 128), BF16),
        V((2, 32, 128), BF16),
        V((4, 16, 128), BF16),
        V((10, 6, 16, 128), F32),
        V((10, 6, 16, 128), F32),
        V((2, 256, 1792), BF16),
        V((nx, 128, 128), BF16),
        V((nx, 128, 128), BF16),
        V((nx, 8, 1792), BF16),
        V((nx, 8, 1792), BF16),
        V((8, 1792), F32),
        V((8 * nx, 1792), F32),
        V((nz, ny // 2, nx, 8, 128), BF16),
        V((nz, ny // 2, nx, 8, 128), BF16),
        V((ny // 2, nx, 8, 128), BF16),
        V((nx * ny, 8, 128), BF16),
        V((96, 1152), F32),
        V((nz, ny, 32, 128), BF16),
        V((nz, ny, 32, 128), BF16),
        V((ny, 32, 128), BF16),
        V((ny, 32, 128), BF16),
        V((n, 8, 128), BF16),
        V((n, 8, 128), BF16),
        D((12,)),
        D((26,)),
        D((26,)),
        D((4, nx)),
        D((4, nx)),
        D((8,)),
        D((8,)),
        D((nx,)),
        D((nx,)),
        D((nx,)),
        D((nx,)),
        D((nz,)),
        D((nz,)),
        D((n,)),
        D((n,)),
        D((ny,)),
        D((ny,)),
        D((nz,)),
        D((nz,)),
        D((nx * ny,)),
        D((nx * ny,)),
    ]
    bottle, grad_down, grad_bottle = pl.pallas_call(
        functools.partial(body, sizes),
        out_shape=(
            V((32, 4, 8, 32), BF16),
            V((16, 54), F32),
            V((32, 108), F32),
        ),
        in_specs=[pl.BlockSpec(memory_space=pl.ANY)] * 8,
        out_specs=(vmem, vmem, vmem),
        scratch_shapes=scratch,
        compiler_params=pltpu.CompilerParams(
            collective_id=0, has_side_effects=True, vmem_limit_bytes=60 * 1024 * 1024
        ),
    )(fields, grain_ids, table.T, w_in.T, k_fine, k_down.T, k_bot, cot)
    bottle, grad_down, grad_bottle = pl.pallas_call(
        put_out,
        out_shape=(
            jax.ShapeDtypeStruct((32, 4, 8, 32), BF16),
            jax.ShapeDtypeStruct((16, 54), F32),
            jax.ShapeDtypeStruct((32, 108), F32),
        ),
        in_specs=[vmem] * 3,
        out_specs=[pl.BlockSpec(memory_space=pl.ANY)] * 3,
        scratch_shapes=[D((3,))],
        compiler_params=pltpu.CompilerParams(vmem_limit_bytes=1024 * 1024),
    )(bottle, grad_down, grad_bottle)
    return bottle.transpose(0, 3, 1, 2), grad_down, grad_bottle


def solution(mesh):
    sizes = (mesh.shape["gx"], mesh.shape["gy"], mesh.shape["gz"])
    placed = (
        P(None, "gx", "gy", "gz"),
        P("gx", "gy", "gz"),
        P(),
        P(),
        P(),
        P(),
        P("gx", None),
        P("gx", None, "gy", "gz"),
    )
    return jax.shard_map(
        functools.partial(per_device, sizes),
        mesh=mesh,
        in_specs=placed,
        out_specs=(P("gx", None, "gy", "gz"), P("gx", ("gy", "gz")), P("gx", ("gy", "gz"))),
        check_vma=False,
    )
```
